32 devices in a mesh: seq: 2 (over y), row: 4 (over x, core), rep: 4 (over z).
Axes of the slice: x: 2, y: 2, z: 4, core: 2. Of those that a mesh axis runs over, the one named last changes fastest.
Arguments:
- block_input: bfloat16 [4, 2048, 2048], P('row', 'seq', 'rep'), may hold values from -6 to 6
- cotangent: bfloat16 [4, 2048, 2048], P('row', 'seq', 'rep'), may hold values from -6 to 6
- segment_ids: int32 [4, 2048], P('row', 'seq'), may hold values from 0 to 3, never falling along the last dimension, each value on 1 to 1024 neighbouring positions
- pad_mask: int32 [4, 2048], P('row', 'seq'), may hold values 0 or 1
- state_init: float32 [4, 2816], P('row', 'rep'), may hold values from -6 to 6
- window_init: bfloat16 [4, 3, 2816], P('row', None, 'rep'), may hold values from -6 to 6
- recur_input: bfloat16 [2048, 2816], P(('seq', 'row'), 'rep'), may hold values from -0.125 to 0.125
- recur_gate: bfloat16 [2048, 2816], P(('seq', 'row'), 'rep'), may hold values from -0.125 to 0.125
- recur_output: bfloat16 [2048, 2816], P(('seq', 'row'), 'rep'), may hold values from -0.3125 to 0.3125
- feed_gate: bfloat16 [2048, 6144], P(('seq', 'row'), 'rep'), may hold values from -0.125 to 0.125
- feed_up: bfloat16 [2048, 6144], P(('seq', 'row'), 'rep'), may hold values from -0.125 to 0.125
- feed_down: bfloat16 [2048, 6144], P(('seq', 'row'), 'rep'), may hold values from -0.15625 to 0.15625
- conv_kernel: float32 [4, 2816], P(None, 'rep'), may hold values from -3 to 3
- conv_bias: float32 [2816], P('rep'), may hold values from -3 to 3
- decay_gate: bfloat16 [16, 176, 176], P('rep'), may hold values from -0.4375 to 0.4375
- input_gate: bfloat16 [16, 176, 176], P('rep'), may hold values from -0.4375 to 0.4375
- decay_bias: float32 [2816], P('rep'), may hold values from -4 to 4
- input_bias: float32 [2816], P('rep'), may hold values from -4 to 4
- decay_logit: float32 [2816], P('rep'), may hold values from -10.5 to -4.5
- mixer_gain: float32 [2048], replicated, may hold values from 0.25 to 1.75
- feed_gain: float32 [2048], replicated, may hold values from 0.25 to 1.75
Outputs:
- block_output: bfloat16 [4, 2048, 2048], P('row', 'seq', 'rep')
- block_states: float32 [4, 2, 2816], P('row', 'seq', 'rep')
- block_windows: bfloat16 [4, 2, 3, 2816], P('row', 'seq', None, 'rep')
- input_grad: bfloat16 [4, 2048, 2048], P('row', 'seq', 'rep')
- recur_input_grad: float32 [2048, 2816], P(('seq', 'row'), 'rep')
- recur_gate_grad: float32 [2048, 2816], P(('seq', 'row'), 'rep')
- recur_output_grad: float32 [2048, 2816], P(('seq', 'row'), 'rep')
- feed_gate_grad: float32 [2048, 6144], P(('seq', 'row'), 'rep')
- feed_up_grad: float32 [2048, 6144], P(('seq', 'row'), 'rep')
- feed_down_grad: float32 [2048, 6144], P(('seq', 'row'), 'rep')
- conv_kernel_grad: float32 [4, 2816], P(None, 'rep')
- conv_bias_grad: float32 [2816], P('rep')
- decay_gate_grad: float32 [16, 176, 176], P('rep')
- input_gate_grad: float32 [16, 176, 176], P('rep')
- decay_bias_grad: float32 [2816], P('rep')
- input_bias_grad: float32 [2816], P('rep')
- decay_logit_grad: float32 [2816], P('rep')
- mixer_gain_grad: float32 [2048], replicated
- feed_gain_grad: float32 [2048], replicated
The draws below stay inside these ranges and needn't reach their ends.
Inputs may be any that keep to these rules, and one draw needn't show every extreme that they name: `segment_ids`: document numbers never fall along a row; each row holds 4 documents of at most 1024 positions.
All inputs are finite; a program needn't handle non-finite values. No bound on the sum of `pad_mask` on one device may be relied on, other than what follows from the above.
Results may differ from the reference program's by a relative error of at most 0.01.
Values may be sent and summed in bfloat16 or wider, within the bound.
A program may use at most 384 MiB of HBM per device.

```python
import math
import jax
import jax.numpy as jnp
import numpy as np
from jax import lax

D = 2048
W = 2816
HEADS = 16
HW = 176
F = 6144
TAPS = 4
GROUP = 1024
DOCS = 4
LEN = 2048
ROWS = 4
BLOCKS = 2
DOC_MOST = 1024


def touch_ends(values, own_key, least, largest):
    dims = values.shape
    index_at = [jax.random.randint(jax.random.fold_in(own_key, axis), (), 0, dims[axis]) for axis in range(len(dims))]
    values = values.at[tuple(index_at)].set(least)
    longest = dims.index(max(dims))
    index_at[longest] = (index_at[longest] + 1) % dims[longest]
    return values.at[tuple(index_at)].set(largest)


def steps_of(stream_key, shape, cuts, smallest, top_value):
    loudness = 1.0
    for dim, shards_of in cuts:
        heights = jax.random.uniform(jax.random.fold_in(jax.random.fold_in(stream_key, 6), dim), (shards_of,), jnp.float32, smallest / len(cuts), top_value / len(cuts))
        loudness = loudness * jnp.repeat(jnp.exp(heights), shape[dim] // shards_of).reshape((-1,) + (1,) * (len(shape) - 1 - dim))
    return loudness


def length_profile(number_of, total, limit, slope):
    weights = [(1 << 20) // math.isqrt(standing ** slope) + 1 for standing in range(2, number_of + 1)]
    spare, counts = total - limit - (number_of - 1), [1] * (number_of - 1)
    while spare > 0:
        movable = [i for i in range(number_of - 1) if counts[i] < limit]
        whole, left = sum([weights[i] for i in movable]), spare
        for i in movable:
            addition = min(limit - counts[i], max(1, left * weights[i] // whole), spare)
            counts[i] = counts[i] + addition
            spare = spare - addition
    return np.array([limit] + counts)


def ragged(key, amount, total, most, slope):
    if amount == 2:
        one = jax.random.randint(key, (), max(1, total - most), min(most, total - 1) + 1)
        return jnp.stack([one, total - one])
    sizes = jnp.asarray(length_profile(amount, total, most, slope), jnp.int32)
    twos = (amount - 1) // 2
    giver, receiver = sizes[1:1 + 2 * twos:2], sizes[2:2 + 2 * twos:2]
    margin = jnp.minimum(giver - 1, most - receiver)
    moved = jax.random.randint(jax.random.fold_in(key, 1), (twos,), 0, 1 << 20) % (margin + 1)
    sizes = sizes.at[1:1 + 2 * twos:2].set(giver - moved).at[2:2 + 2 * twos:2].set(receiver + moved)
    return sizes[jax.random.permutation(jax.random.fold_in(key, 2), amount)]


def bell_draw(stream_key, extent, spread, most, shards=(), kind=jnp.bfloat16):
    level = steps_of(stream_key, extent, shards, -0.22, 0.18) if shards else 1.0
    array = jax.random.normal(stream_key, extent, jnp.float32) * spread * level
    return jnp.minimum(jnp.maximum(array, -most), most).astype(kind)


def setup_inputs(seed: int = 0) -> dict:
    seeds = jax.random.split(jax.random.key(seed), 22)
    block_input = bell_draw(seeds[0], (ROWS, LEN, D), 1.0, 6.0, ((0, 4), (1, 2), (2, 4)))
    cotangent = bell_draw(seeds[1], (ROWS, LEN, D), 1.0, 6.0, ((0, 4), (1, 2), (2, 4)))
    segment_ids = jax.vmap(lambda own: jnp.searchsorted(jnp.cumsum(ragged(own, DOCS, LEN, DOC_MOST, 0)), jnp.arange(LEN), side="right"))(jax.random.split(seeds[2], ROWS)).reshape((ROWS, LEN)).astype(jnp.int32)
    pad_mask = touch_ends((jax.random.randint(seeds[3], (ROWS, LEN), 0, 4) < 3).astype(jnp.int32), jax.random.fold_in(seeds[3], 1), 0, 1)
    state_init = bell_draw(seeds[4], (ROWS, W), 1.0, 6.0, ((0, 4), (1, 4)), jnp.float32)
    window_init = bell_draw(seeds[5], (ROWS, TAPS - 1, W), 1.0, 6.0, ((0, 4), (2, 4)))
    recur_input = bell_draw(seeds[6], (D, W), D ** -0.5, 0.125, ((0, 8), (1, 4)))
    recur_gate = bell_draw(seeds[7], (D, W), D ** -0.5, 0.125, ((0, 8), (1, 4)))
    recur_output = bell_draw(seeds[8], (D, W), (W // 8) ** -0.5, 0.3125, ((0, 8), (1, 4)))
    feed_gate = bell_draw(seeds[9], (D, F), D ** -0.5, 0.125, ((0, 8), (1, 4)))
    feed_up = bell_draw(seeds[10], (D, F), D ** -0.5, 0.125, ((0, 8), (1, 4)))
    feed_down = bell_draw(seeds[11], (D, F), (F // 4) ** -0.5, 0.15625, ((0, 8), (1, 4)))
    conv_kernel = bell_draw(seeds[12], (TAPS, W), TAPS ** -0.5, 3.0, ((1, 4),), jnp.float32)
    conv_bias = bell_draw(seeds[13], (W,), 0.5, 3.0, ((0, 4),), jnp.float32)
    decay_gate = bell_draw(seeds[14], (HEADS, HW, HW), HW ** -0.5, 0.4375, ((0, 4),))
    input_gate = bell_draw(seeds[15], (HEADS, HW, HW), HW ** -0.5, 0.4375, ((0, 4),))
    decay_bias = bell_draw(seeds[16], (W,), 1.0, 4.0, ((0, 4),), jnp.float32)
    input_bias = bell_draw(seeds[17], (W,), 1.0, 4.0, ((0, 4),), jnp.float32)
    decay_logit = jnp.clip(-10.5 + 6.0 * jax.random.uniform(seeds[18], (W,), jnp.float32) ** steps_of(seeds[18], (W,), ((0, 4),), -0.2, 0.2), -10.5, -4.5)
    mixer_gain = jnp.clip(1.0 + 0.15 * jax.random.normal(seeds[19], (D,), jnp.float32), 0.25, 1.75)
    feed_gain = jnp.clip(1.0 + 0.15 * jax.random.normal(seeds[20], (D,), jnp.float32), 0.25, 1.75)
    return dict(block_input=block_input, cotangent=cotangent, segment_ids=segment_ids, pad_mask=pad_mask, state_init=state_init, window_init=window_init, recur_input=recur_input, recur_gate=recur_gate, recur_output=recur_output, feed_gate=feed_gate, feed_up=feed_up, feed_down=feed_down, conv_kernel=conv_kernel, conv_bias=conv_bias, decay_gate=decay_gate, input_gate=input_gate, decay_bias=decay_bias, input_bias=input_bias, decay_logit=decay_logit, mixer_gain=mixer_gain, feed_gain=feed_gain)


@jax.custom_vjp
def low(v):
    return lax.optimization_barrier(v.astype(jnp.bfloat16)).astype(jnp.float32)

@jax.custom_vjp
def low_back(v):
    return v

def low_keep(v):
    return (low(v), None)

def low_pass(kept, grad):
    return (grad,)

def back_keep(v):
    return (v, None)

def back_low(kept, grad):
    return (low(grad),)
low.defvjp(low_keep, low_pass)
low_back.defvjp(back_keep, back_low)
highest = lax.Precision.HIGHEST
eps = 1e-06

def rms_norm(values, scales):
    return values * lax.rsqrt(lax.optimization_barrier(jnp.mean(values * values, axis=-1, keepdims=True)) + eps) * scales

def affine(former, latter):
    return (former[0] * latter[0], latter[0] * former[1] + latter[1])

def row_pass(params, row):
    recur_input, recur_gate, recur_output, feed_gate, feed_up, feed_down, conv_kernel, conv_bias, decay_gate, input_gate, decay_bias, input_bias, decay_logit, mixer_gain, feed_gain = params
    tokens, segments, state_start, window_start = row
    normed = low(rms_norm(tokens, mixer_gain))
    conv_input = low_back(low(jnp.dot(normed, recur_input, precision=highest)))
    gate_branch = low_back(jnp.dot(normed, recur_gate, precision=highest))
    edge_width = TAPS - 1
    ids_ext = jnp.concatenate([jnp.broadcast_to(segments[:1], (edge_width,)), segments])
    padded = jnp.concatenate([window_start, conv_input], axis=0)
    conv_out = conv_bias
    for offset in range(TAPS):
        start = edge_width - offset
        same_mask = (ids_ext[start:start + LEN] == segments).astype(jnp.float32)
        conv_out = conv_out + conv_kernel[offset] * padded[start:start + LEN] * same_mask[:, None]
    retain_mask = (ids_ext[edge_width - 1:edge_width - 1 + LEN] == segments).astype(jnp.float32)
    conv_low = low(conv_out).reshape(LEN, HEADS, HW)
    decay_pre = low_back(jnp.einsum('thi,hij->thj', conv_low, decay_gate, precision=highest).reshape(LEN, W) + decay_bias)
    input_pre = low_back(jnp.einsum('thi,hij->thj', conv_low, input_gate, precision=highest).reshape(LEN, W) + input_bias)
    rate_scale = 8.0 * jax.nn.softplus(decay_logit)
    exponent = rate_scale * jax.nn.sigmoid(decay_pre)
    retain = retain_mask[:, None] * jnp.exp(-exponent)
    inflow = jnp.sqrt(-jnp.expm1(-2.0 * exponent)) * jax.nn.sigmoid(input_pre) * conv_out
    products, partial_states = lax.associative_scan(affine, (retain, inflow), axis=0)
    hidden = partial_states + products * state_start
    gated = low(hidden * jax.nn.gelu(gate_branch, approximate=True))
    branch = low_back(jnp.dot(gated, recur_output.T, precision=highest))
    middle = tokens + branch
    normed_mid = low(rms_norm(middle, feed_gain))
    gate_pre = low_back(jnp.dot(normed_mid, feed_gate, precision=highest))
    up_pre = low_back(jnp.dot(normed_mid, feed_up, precision=highest))
    feed_low = low(jax.nn.gelu(gate_pre, approximate=True) * up_pre)
    result = middle + jnp.dot(feed_low, feed_down.T, precision=highest)
    block_states = hidden.reshape(BLOCKS, GROUP, W)[:, GROUP - 1]
    block_windows = conv_input.reshape(BLOCKS, GROUP, W)[:, GROUP - edge_width:]
    return (result, (block_states, block_windows))

def reference(block_input, cotangent, segment_ids, pad_mask, state_init, window_init, recur_input, recur_gate, recur_output, feed_gate, feed_up, feed_down, conv_kernel, conv_bias, decay_gate, input_gate, decay_bias, input_bias, decay_logit, mixer_gain, feed_gain):
    params = tuple((p.astype(jnp.float32) for p in (recur_input, recur_gate, recur_output, feed_gate, feed_up, feed_down, conv_kernel, conv_bias, decay_gate, input_gate, decay_bias, input_bias, decay_logit, mixer_gain, feed_gain)))
    window_start = window_init.astype(jnp.float32)

    def forward(weights, tokens):

        def one_row(row):
            return row_pass(weights, row)
        return lax.map(jax.checkpoint(one_row), (tokens, segment_ids, state_init, window_start))
    result, backward, extra = jax.vjp(forward, params, block_input.astype(jnp.float32), has_aux=True)
    block_states, block_windows = extra
    masked_cot = cotangent.astype(jnp.float32) * pad_mask[..., None].astype(jnp.float32)
    grads, input_grad = backward(masked_cot)
    return (result.astype(jnp.bfloat16), block_states, block_windows.astype(jnp.bfloat16), input_grad.astype(jnp.bfloat16), grads[0], grads[1], grads[2], grads[3], grads[4], grads[5], grads[6], grads[7], grads[8], grads[9], grads[10], grads[11], grads[12], grads[13], grads[14])
```

```python
import jax
import jax.numpy as jnp
from jax import lax
from jax.experimental import pallas as pl
from jax.experimental.pallas import tpu as pltpu
from jax.sharding import PartitionSpec as P

eps = 1e-06
SEGS = 8
BF = jnp.bfloat16
F32 = jnp.float32
LIMIT = 48 * 1024 * 1024


def gelu(v):
    return 0.5 * v * (1.0 + jnp.tanh(0.7978845608 * (v + 0.044715 * v * v * v)))


def gelu_both(v):
    square = v * v
    t = jnp.tanh(0.7978845608 * v * (1.0 + 0.044715 * square))
    value = 0.5 * v * (1.0 + t)
    slope = 0.5 * (1.0 + t) + 0.5 * v * (1.0 - t * t) * 0.7978845608 * (1.0 + 3 * 0.044715 * square)
    return value, slope


def one_minus_exp(y):
    series = y * (1 - y / 2 * (1 - y / 3 * (1 - y / 4 * (1 - y / 5 * (1 - y / 6 * (1 - y / 7))))))
    return jnp.where(y < 0.4, series, 1.0 - jnp.exp(-y))


def gather_line(own, axis):
    count, me = lax.axis_size(axis), lax.axis_index(axis)
    width = own.shape[1]
    total = jnp.zeros((own.shape[0], count * width), own.dtype)
    total = lax.dynamic_update_slice(total, own, (0, me * width))
    right, left = own, own
    held = {}
    for k in range(1, count):
        right = lax.ppermute(right, axis, [(i, i + 1) for i in range(k - 1, count - 1)])
        left = lax.ppermute(left, axis, [(i, i - 1) for i in range(1, count - k + 1)])
        held[-k], held[k] = right, left
    for k in range(1, count):
        there = me + k
        piece = jnp.where(there < count, held[k], held[k - count])
        total = lax.dynamic_update_slice(total, piece, (0, lax.rem(there, count) * width))
    return total


def reduce_line(whole, axis):
    count, me = lax.axis_size(axis), lax.axis_index(axis)
    width = whole.shape[1] // count

    def part(target):
        target = jnp.clip(target, 0, count - 1)
        return lax.dynamic_slice_in_dim(whole, target * width, width, 1).astype(F32)

    right = left = None
    for k in range(1, count):
        far = count - k
        to_right, to_left = part(me + far), part(me - far)
        if k > 1:
            to_right, to_left = to_right + right, to_left + left
        right = lax.ppermute(to_right.astype(BF), axis, [(i, i + 1) for i in range(k)]).astype(F32)
        left = lax.ppermute(to_left.astype(BF), axis, [(i, i - 1) for i in range(far, count)]).astype(F32)
    return part(me) + right + left


def small_sum(own, axis):
    count = lax.axis_size(axis)
    total = own
    for k in range(1, count):
        total = total + lax.ppermute(own, axis, [(i, (i + k) % count) for i in range(count)])
    return total


def row_sum(values, axis):
    sums = jnp.sum(values, axis=1)
    return small_sum(sums.reshape(8, -1), axis).reshape(-1, 1)


def by_step(values):
    length, width = values.shape
    return values.reshape(SEGS, length // SEGS, width).transpose(1, 0, 2).reshape(length, width)


def by_segment(values):
    length, width = values.shape
    return values.reshape(length // SEGS, SEGS, width).transpose(1, 0, 2).reshape(length, width)


def block_diagonal(blocks):
    heads, wide = blocks.shape[0], blocks.shape[1]
    rows = [jnp.pad(blocks[h], ((0, 0), (h * wide, (heads - 1 - h) * wide))) for h in range(heads)]
    return jnp.concatenate(rows, axis=0)


def diagonal_blocks(dense, heads):
    wide = dense.shape[0] // heads
    return jnp.stack([dense[h * wide : (h + 1) * wide, h * wide : (h + 1) * wide] for h in range(heads)])


def forward_kernel(
    conv_in, same, prefix, params, decay_w, input_w,
    out_conv, out_decay, out_gate, out_retain, out_prod, out_state, out_pre_a, out_pre_b, out_total,
    last_rows, prod_now, state_now, inflow_s,
):
    step = pl.program_id(0)
    rows = conv_in.shape[0]

    @pl.when(step == 0)
    def _():
        last_rows[...] = prefix[...].astype(F32)
        prod_now[...] = jnp.ones_like(prod_now)
        state_now[...] = jnp.zeros_like(state_now)

    now = conv_in[...].astype(F32)
    ext = jnp.concatenate([last_rows[...], now], axis=0)
    same_all = same[...]
    total = params[4:5, :] + params[0:1, :] * now
    for k in (1, 2, 3):
        start = 24 - 8 * k
        total = total + params[k : k + 1, :] * ext[start : start + rows] * same_all[:, k : k + 1]
    last_rows[...] = now[rows - 24 :]
    out_conv[...] = total
    low = total.astype(BF)
    decay_sig = jax.nn.sigmoid(jnp.dot(low, decay_w[...], preferred_element_type=F32) + params[5:6, :])
    gate_sig = jax.nn.sigmoid(jnp.dot(low, input_w[...], preferred_element_type=F32) + params[6:7, :])
    out_decay[...] = decay_sig
    out_gate[...] = gate_sig
    expo = params[7:8, :] * decay_sig
    out_retain[...] = same_all[:, 1:2] * jnp.exp(-expo)
    inflow_s[...] = jnp.sqrt(one_minus_exp(2.0 * expo)) * gate_sig * total
    prod, state = prod_now[...], state_now[...]
    for t in range(rows // SEGS):
        at = slice(t * SEGS, (t + 1) * SEGS)
        keep = out_retain[at, :]
        prod = prod * keep
        state = state * keep + inflow_s[at, :]
        out_prod[at, :] = prod
        out_state[at, :] = state
    prod_now[...] = prod
    state_now[...] = state

    @pl.when(step == pl.num_programs(0) - 1)
    def _():
        carry_a = jnp.ones_like(prod[0:1])
        carry_b = jnp.zeros_like(carry_a)
        for s in range(SEGS):
            out_pre_a[s : s + 1, :] = carry_a
            out_pre_b[s : s + 1, :] = carry_b
            carry_b = prod[s : s + 1] * carry_b + state[s : s + 1]
            carry_a = prod[s : s + 1] * carry_a
        out_total[0:1, :] = carry_a
        out_total[1:2, :] = carry_b
        out_total[2:8, :] = jnp.zeros((6, carry_a.shape[1]), F32)


def recur_forward(conv_in, same, prefix, params, decay_w, input_w, rows=128):
    length, width = conv_in.shape
    block = pl.BlockSpec((rows, width), lambda i: (i, 0))
    fixed = lambda shape: pl.BlockSpec(shape, lambda i: (0, 0))
    big = jax.ShapeDtypeStruct((length, width), F32)
    small = jax.ShapeDtypeStruct((SEGS, width), F32)
    return pl.pallas_call(
        forward_kernel,
        grid=(length // rows,),
        in_specs=[
            block,
            pl.BlockSpec((rows, 8), lambda i: (i, 0)),
            fixed((24, width)),
            fixed((8, width)),
            fixed((width, width)),
            fixed((width, width)),
        ],
        out_specs=[block] * 6 + [fixed((SEGS, width))] * 3,
        out_shape=[big] * 6 + [small] * 3,
        scratch_shapes=[
            pltpu.VMEM((24, width), F32),
            pltpu.VMEM((SEGS, width), F32),
            pltpu.VMEM((SEGS, width), F32),
            pltpu.VMEM((rows, width), F32),
        ],
        compiler_params=pltpu.CompilerParams(vmem_limit_bytes=LIMIT),
        cost_estimate=pl.CostEstimate(
            flops=4 * length * width * width, bytes_accessed=26 * length * width, transcendentals=5 * length * width
        ),
    )(conv_in, same, prefix, params, decay_w, input_w)


def adjoint_kernel(
    gated_grad, gate_branch, hidden, retain,
    out_local, out_after, out_branch, out_pre_a, out_pre_b, out_total, out_dot,
    local_now, after_now, next_retain, grad_s,
):
    step = pl.program_id(0)
    rows = gated_grad.shape[0]

    @pl.when(step == 0)
    def _():
        local_now[...] = jnp.zeros_like(local_now)
        after_now[...] = jnp.ones_like(after_now)
        next_retain[...] = jnp.ones_like(next_retain)

    value, slope = gelu_both(gate_branch[...])
    upstream = gated_grad[...]
    grad_s[...] = upstream * value
    branch = upstream * hidden[...] * slope
    out_branch[...] = branch.astype(BF)
    out_dot[...] = jnp.broadcast_to(jnp.sum(branch * gate_branch[...], axis=1, keepdims=True), out_dot.shape)
    local, after, keep = local_now[...], after_now[...], next_retain[...]
    for t in reversed(range(rows // SEGS)):
        at = slice(t * SEGS, (t + 1) * SEGS)
        local = grad_s[at, :] + keep * local
        after = keep * after
        out_local[at, :] = local
        out_after[at, :] = after
        keep = retain[at, :]
    local_now[...] = local
    after_now[...] = after
    next_retain[...] = keep

    @pl.when(step == pl.num_programs(0) - 1)
    def _():
        carry_a = jnp.ones_like(local[0:1])
        carry_b = jnp.zeros_like(carry_a)
        for s in reversed(range(SEGS)):
            out_pre_a[s : s + 1, :] = carry_a
            out_pre_b[s : s + 1, :] = carry_b
            carry_b = keep[s : s + 1] * (local[s : s + 1] + after[s : s + 1] * carry_b)
            carry_a = keep[s : s + 1] * after[s : s + 1] * carry_a
        out_total[0:1, :] = carry_a
        out_total[1:2, :] = carry_b
        out_total[2:8, :] = jnp.zeros((6, carry_a.shape[1]), F32)


def recur_adjoint(gated_grad, gate_branch, hidden, retain, rows=128):
    length, width = gated_grad.shape
    last = length // rows - 1
    block = pl.BlockSpec((rows, width), lambda i: (last - i, 0))
    fixed = lambda shape: pl.BlockSpec(shape, lambda i: (0, 0))
    big = jax.ShapeDtypeStruct((length, width), F32)
    small = jax.ShapeDtypeStruct((SEGS, width), F32)
    return pl.pallas_call(
        adjoint_kernel,
        grid=(length // rows,),
        in_specs=[block] * 4,
        out_specs=[block] * 3 + [fixed((SEGS, width))] * 3 + [pl.BlockSpec((rows, 128), lambda i: (last - i, 0))],
        out_shape=[big, big, jax.ShapeDtypeStruct((length, width), BF)]
        + [small] * 3
        + [jax.ShapeDtypeStruct((length, 128), F32)],
        scratch_shapes=[pltpu.VMEM((SEGS, width), F32)] * 3 + [pltpu.VMEM((rows, width), F32)],
        compiler_params=pltpu.CompilerParams(vmem_limit_bytes=LIMIT),
        cost_estimate=pl.CostEstimate(
            flops=20 * length * width, bytes_accessed=26 * length * width, transcendentals=length * width
        ),
    )(gated_grad, gate_branch, hidden, retain)


def backward_kernel(
    local, after, enter, hidden, hidden_before, carry, conv_out, decay_sig, gate_sig, retain, same, params, conv_in,
    decay_w, input_w,
    out_decay, out_input, out_low, out_first, out_sums,
    next_one, next_two, next_three,
):
    step = pl.program_id(0)
    blocks = pl.num_programs(0)
    rows = local.shape[0]
    width = local.shape[1]

    @pl.when(step == 0)
    def _():
        for held in (next_one, next_two, next_three):
            held[...] = jnp.zeros_like(held)
        out_sums[...] = jnp.zeros_like(out_sums)

    def per_step(small):
        return jnp.broadcast_to(small[None], (rows // SEGS, SEGS, width)).reshape(rows, width)

    def sums(values):
        return jnp.sum(values.reshape(rows // SEGS, SEGS, width), axis=0)

    adjoint = local[...] + after[...] * per_step(enter[...])
    ahead = jnp.where(step == blocks - 1, carry[...], hidden_before[...])
    hidden_prev = jnp.concatenate([ahead, hidden[...][: rows - SEGS]], axis=0)
    conv, decay, gate = conv_out[...], decay_sig[...], gate_sig[...]
    rate = params[7:8, :]
    expo = rate * decay
    inner = one_minus_exp(2.0 * expo)
    root = jnp.sqrt(inner)
    expo_grad = adjoint * (gate * conv * (1.0 - inner) / root - retain[...] * hidden_prev)
    decay_grad = (expo_grad * rate * decay * (1.0 - decay)).astype(BF)
    input_grad = (adjoint * root * conv * gate * (1.0 - gate)).astype(BF)
    out_decay[...] = decay_grad
    out_input[...] = input_grad
    dims = (((1,), (1,)), ((), ()))
    conv_grad = (
        adjoint * root * gate
        + lax.dot_general(decay_grad, decay_w[...], dims, preferred_element_type=F32)
        + lax.dot_general(input_grad, input_w[...], dims, preferred_element_type=F32)
    )
    same_all = same[...]
    now = conv_in[...].astype(F32)
    low = params[0:1, :] * conv_grad
    out_sums[0:8, :] += sums(conv_grad * now)
    for k, held in ((1, next_one), (2, next_two), (3, next_three)):
        masked = conv_grad * same_all[:, k : k + 1]
        moved = jnp.concatenate([masked[8 * k :], held[...]], axis=0)
        held[...] = masked[: 8 * k]
        low = low + params[k : k + 1, :] * moved
        out_sums[8 * k : 8 * k + 8, :] += sums(moved * now)
    out_low[...] = low
    out_sums[32:40, :] += sums(conv_grad)
    out_sums[40:48, :] += sums(decay_grad.astype(F32))
    out_sums[48:56, :] += sums(input_grad.astype(F32))
    out_sums[56:64, :] += sums(expo_grad * decay)

    @pl.when(step == blocks - 1)
    def _():
        out_first[0:8, :] = next_one[...]
        out_first[8:24, :] = next_two[...]
        out_first[24:48, :] = next_three[...]


def recur_backward(
    local, after, enter, hidden, carry, conv_out, decay_sig, gate_sig, retain, same, params, conv_in, decay_w, input_w,
    rows=128,
):
    length, width = local.shape
    last = length // rows - 1
    block = pl.BlockSpec((rows, width), lambda i: (last - i, 0))
    fixed = lambda shape: pl.BlockSpec(shape, lambda i: (0, 0))
    steps = rows // SEGS
    before = pl.BlockSpec((SEGS, width), lambda i: (jnp.maximum((last - i) * steps - 1, 0), 0))
    return pl.pallas_call(
        backward_kernel,
        grid=(length // rows,),
        in_specs=[
            block, block, fixed((SEGS, width)), block, before, fixed((SEGS, width)), block, block, block, block,
            pl.BlockSpec((rows, 8), lambda i: (last - i, 0)),
            fixed((8, width)), block, fixed((width, width)), fixed((width, width)),
        ],
        out_specs=[block, block, block, fixed((48, width)), fixed((64, width))],
        out_shape=[
            jax.ShapeDtypeStruct((length, width), BF),
            jax.ShapeDtypeStruct((length, width), BF),
            jax.ShapeDtypeStruct((length, width), F32),
            jax.ShapeDtypeStruct((48, width), F32),
            jax.ShapeDtypeStruct((64, width), F32),
        ],
        scratch_shapes=[
            pltpu.VMEM((8, width), F32),
            pltpu.VMEM((16, width), F32),
            pltpu.VMEM((24, width), F32),
        ],
        compiler_params=pltpu.CompilerParams(vmem_limit_bytes=LIMIT),
        cost_estimate=pl.CostEstimate(
            flops=4 * length * width * width, bytes_accessed=40 * length * width, transcendentals=5 * length * width
        ),
    )(
        local, after, enter, hidden, hidden, carry, conv_out, decay_sig, gate_sig, retain, same, params, conv_in,
        decay_w, input_w,
    )


def per_segment(small, length):
    return jnp.broadcast_to(small[None], (length // SEGS,) + small.shape).reshape(length, small.shape[1])


def rows_dot(left, right):
    return lax.dot_general(left, right, (((0,), (0,)), ((), ())), preferred_element_type=F32)


def back_dot(left, right):
    return lax.dot_general(left, right, (((1,), (1,)), ((), ())), preferred_element_type=F32)


def dot(left, right):
    return jnp.dot(left, right, preferred_element_type=F32)


def shards(
    block_input, cotangent, segment_ids, pad_mask, state_init, window_init,
    recur_input, recur_gate, recur_output, feed_gate, feed_up, feed_down,
    conv_kernel, conv_bias, decay_gate, input_gate, decay_bias, input_bias, decay_logit, mixer_gain, feed_gain,
):
    own_width = block_input.shape[2]
    features = mixer_gain.shape[0]
    length = segment_ids.shape[1]
    taps = conv_kernel.shape[0]
    edge = taps - 1
    heads = decay_gate.shape[0]
    rep = lax.axis_index("rep")
    seq, seqs = lax.axis_index("seq"), lax.axis_size("seq")
    at_start = seq == 0
    to_next = [(i, i + 1) for i in range(seqs - 1)]
    to_last = [(i + 1, i) for i in range(seqs - 1)]

    def weights(shard):
        return lax.all_gather(shard, ("seq", "row"), axis=0, tiled=True)

    def spread(partial_grad):
        low = partial_grad.astype(BF)
        return lax.psum_scatter(low, ("seq", "row"), scatter_dimension=0, tiled=True).astype(F32)

    def own_part(vector):
        return lax.dynamic_slice_in_dim(vector, rep * own_width, own_width, 0)[None]

    x_own = by_step(block_input[0]).astype(F32)
    cot_own = by_step(cotangent[0] * pad_mask[0][:, None].astype(BF))
    mixer_own, feed_own = own_part(mixer_gain), own_part(feed_gain)
    s1 = lax.rsqrt(row_sum(x_own * x_own, "rep") / features + eps)
    normed = gather_line((x_own * s1 * mixer_own).astype(BF), "rep")
    w_input, w_gate, w_output = weights(recur_input), weights(recur_gate), weights(recur_output)
    w_feed_gate, w_feed_up, w_down = weights(feed_gate), weights(feed_up), weights(feed_down)

    left_ids = lax.ppermute(segment_ids[:, -edge:].astype(F32), "seq", to_next).astype(jnp.int32)
    left_ids = jnp.where(at_start, jnp.broadcast_to(segment_ids[:, :1], left_ids.shape), left_ids)
    ids_ext = jnp.concatenate([left_ids, segment_ids], axis=1)[0]
    same = [(ids_ext[edge - k : edge - k + length] == segment_ids[0]).astype(F32) for k in range(taps)]
    same = by_step(jnp.stack(same + [same[0]] * (8 - taps), axis=1))

    rate = 8.0 * jax.nn.softplus(decay_logit)
    params = jnp.concatenate([conv_kernel, jnp.stack([conv_bias, decay_bias, input_bias, rate])], axis=0)
    decay_w, input_w = block_diagonal(decay_gate), block_diagonal(input_gate)

    conv_in = dot(normed, w_input).astype(BF)
    gate_branch = dot(normed, w_gate)
    ends = conv_in.reshape(length // SEGS, SEGS, -1)[-edge:]
    left = lax.ppermute(ends[:, -1], "seq", to_next)
    left = jnp.where(at_start, window_init[0], left)
    prefix = jnp.concatenate([left[:, None], ends[:, :-1]], axis=1).reshape(edge * SEGS, -1)
    block_windows = ends[:, -1]

    conv_out, decay_sig, gate_sig, retain, products, states, pre_a, pre_b, total = recur_forward(
        conv_in, same, prefix, params, decay_w, input_w
    )
    state_in = state_init
    for k in range(1, seqs):
        arriving = lax.ppermute(total[0:1] * state_in + total[1:2], "seq", to_next)
        state_in = jnp.where(seq == k, arriving, state_in)
    block_states = total[0:1] * state_in + total[1:2]
    carry = pre_a * state_in + pre_b
    hidden = states + products * per_segment(carry, length)
    gated = (hidden * gelu(gate_branch)).astype(BF)

    middle = x_own + reduce_line(back_dot(gated, w_output).astype(BF), "rep")
    s2 = lax.rsqrt(row_sum(middle * middle, "rep") / features + eps)
    normed_mid = gather_line((middle * s2 * feed_own).astype(BF), "rep")
    cot = gather_line(cot_own, "rep")
    gate_pre, up_pre = dot(normed_mid, w_feed_gate), dot(normed_mid, w_feed_up)
    grad_feed = dot(cot, w_down)
    value, slope = gelu_both(gate_pre)
    feed_low = (value * up_pre).astype(BF)
    gate_grad_f, up_grad_f = grad_feed * up_pre * slope, grad_feed * value
    gate_grad, up_grad = gate_grad_f.astype(BF), up_grad_f.astype(BF)
    mid_mean = row_sum(gate_grad_f * gate_pre + up_grad_f * up_pre, "rep") / features

    mid_grad = reduce_line((back_dot(gate_grad, w_feed_gate) + back_dot(up_grad, w_feed_up)).astype(BF), "rep")
    xh2 = middle * s2
    feed_gain_own = jnp.sum(mid_grad * xh2, axis=0)
    middle_grad = cot_own.astype(F32) + s2 * (mid_grad * feed_own - xh2 * mid_mean)
    middle_low = gather_line(middle_grad.astype(BF), "rep")
    feed_down_grad = spread(rows_dot(cot, feed_low))
    feed_gate_grad = spread(rows_dot(normed_mid, gate_grad))
    feed_up_grad = spread(rows_dot(normed_mid, up_grad))
    feed_out = reduce_line(back_dot(feed_low, w_down).astype(BF), "rep")
    block_output = by_segment((middle + feed_out).astype(BF))[None]

    gated_grad = dot(middle_low, w_output)
    recur_output_grad = spread(rows_dot(middle_low, gated))
    local, after, branch_grad, enter_a, enter_b, back_total, branch_dot = recur_adjoint(
        gated_grad, gate_branch, hidden, retain
    )
    entering = jnp.zeros_like(state_init)
    for k in range(1, seqs):
        arriving = lax.ppermute(back_total[0:1] * entering + back_total[1:2], "seq", to_last)
        entering = jnp.where(seq == seqs - 1 - k, arriving, entering)
    enter = enter_a * entering + enter_b
    decay_grad, input_grad_low, low_grad, first, sums = recur_backward(
        local, after, enter, hidden, carry, conv_out, decay_sig, gate_sig, retain, same, params, conv_in, decay_w, input_w
    )
    owed = [first[0:8], first[8:24], first[24:48]]
    owed = [o.reshape(k + 1, SEGS, -1) for k, o in enumerate(owed)]
    ahead = prefix.reshape(edge, SEGS, -1).astype(F32)
    back_share = jnp.zeros_like(ahead)
    tap_extra = [jnp.zeros_like(conv_bias)]
    for k in range(1, taps):
        term = jnp.pad(owed[k - 1], ((edge - k, 0), (0, 0), (0, 0)))
        tap_extra.append(jnp.sum(term * ahead, axis=(0, 1)))
        back_share = back_share + conv_kernel[k] * term
    from_right = lax.ppermute(back_share[:, 0], "seq", to_last)
    share = jnp.concatenate([back_share[:, 1:], from_right[:, None]], axis=1)
    low_grad = low_grad.reshape(length // SEGS, SEGS, -1)
    low_grad = jnp.concatenate([low_grad[:-edge], low_grad[-edge:] + share], axis=0).reshape(length, -1)
    input_low = low_grad.astype(BF)
    in_mean = jnp.sum(low_grad * conv_in.astype(F32), axis=1) + branch_dot[:, 0]
    in_mean = small_sum(in_mean.reshape(8, -1), "rep").reshape(-1, 1) / features

    normed_grad = reduce_line((back_dot(input_low, w_input) + back_dot(branch_grad, w_gate)).astype(BF), "rep")
    recur_gate_grad = spread(rows_dot(normed, branch_grad))
    recur_input_grad = spread(rows_dot(normed, input_low))
    xh1 = x_own * s1
    mixer_gain_own = jnp.sum(normed_grad * xh1, axis=0)
    input_grad = middle_grad + s1 * (normed_grad * mixer_own - xh1 * in_mean)
    input_grad = by_segment(input_grad.astype(BF))[None]

    conv_low = conv_out.astype(BF)
    decay_gate_grad = diagonal_blocks(rows_dot(conv_low, decay_grad), heads)
    input_gate_grad = diagonal_blocks(rows_dot(conv_low, input_grad_low), heads)
    sums = jnp.sum(sums.reshape(8, 8, -1), axis=1)
    conv_kernel_grad = sums[:taps] + jnp.stack(tap_extra)
    small = (
        conv_kernel_grad, sums[4], decay_gate_grad, input_gate_grad, sums[5], sums[6],
        sums[7] * 8.0 * jax.nn.sigmoid(decay_logit),
    )
    small = lax.psum(small, ("seq", "row"))
    gains = jnp.stack([mixer_gain_own, feed_gain_own])
    gains = lax.dynamic_update_slice(jnp.zeros((2, features), F32), gains, (0, rep * own_width))
    gains = lax.psum(gains, ("seq", "row", "rep"))
    return (
        block_output, block_states[:, None], block_windows[None, None], input_grad,
        recur_input_grad, recur_gate_grad, recur_output_grad, feed_gate_grad, feed_up_grad, feed_down_grad,
        *small, gains[0], gains[1],
    )


def solution(mesh):
    tokens = P("row", "seq", "rep")
    matrix = P(("seq", "row"), "rep")
    in_specs = (
        tokens, tokens, P("row", "seq"), P("row", "seq"), P("row", "rep"), P("row", None, "rep"),
        matrix, matrix, matrix, matrix, matrix, matrix,
        P(None, "rep"), P("rep"), P("rep", None, None), P("rep", None, None), P("rep"), P("rep"), P("rep"), P(), P(),
    )
    out_specs = (
        tokens, tokens, P("row", "seq", None, "rep"), tokens,
        matrix, matrix, matrix, matrix, matrix, matrix,
        P(None, "rep"), P("rep"), P("rep", None, None), P("rep", None, None), P("rep"), P("rep"), P("rep"), P(), P(),
    )
    return jax.shard_map(shards, mesh=mesh, in_specs=in_specs, out_specs=out_specs, check_vma=False)
```

```python
from functools import partial as partial_call

import jax
import jax.numpy as jnp
from jax import lax
from jax.experimental import pallas as pl
from jax.experimental.pallas import tpu as pltpu
from jax.sharding import PartitionSpec as P

eps = 1e-06
SEGS = 8
BF = jnp.bfloat16
F32 = jnp.float32
LIMIT = 48 * 1024 * 1024


def gelu(v):
    return 0.5 * v * (1.0 + jnp.tanh(0.7978845608 * (v + 0.044715 * v * v * v)))


def gelu_both(v):
    square = v * v
    t = jnp.tanh(0.7978845608 * v * (1.0 + 0.044715 * square))
    value = 0.5 * v * (1.0 + t)
    slope = 0.5 * (1.0 + t) + 0.5 * v * (1.0 - t * t) * 0.7978845608 * (1.0 + 3 * 0.044715 * square)
    return value, slope


def one_minus_exp(y):
    series = y * (1 - y / 2 * (1 - y / 3 * (1 - y / 4 * (1 - y / 5 * (1 - y / 6 * (1 - y / 7))))))
    return jnp.where(y < 0.4, series, 1.0 - jnp.exp(-y))


after = lax.optimization_barrier


def pass_on(held, k, axis):
    count = lax.axis_size(axis)
    right = lax.ppermute(held[0], axis, [(i, i + 1) for i in range(k - 1, count - 1)])
    left = lax.ppermute(held[1], axis, [(i, i - 1) for i in range(1, count - k + 1)])
    return right, left


def put_together(passed, axis):
    count, me = lax.axis_size(axis), lax.axis_index(axis)
    own = passed[0][0]
    width = own.shape[1]
    total = jnp.zeros((own.shape[0], count * width), own.dtype)
    total = lax.dynamic_update_slice(total, own, (0, me * width))
    for k in range(1, count):
        there = me + k
        piece = jnp.where(there < count, passed[k][1], passed[count - k][0])
        total = lax.dynamic_update_slice(total, piece, (0, lax.rem(there, count) * width))
    return total


def line_part(whole, target, axis):
    count = lax.axis_size(axis)
    width = whole.shape[1] // count
    return lax.dynamic_slice_in_dim(whole, jnp.clip(target, 0, count - 1) * width, width, 1).astype(F32)


def reduce_step(whole, held, k, axis):
    count, me = lax.axis_size(axis), lax.axis_index(axis)
    far = count - k
    right, left = line_part(whole, me + far, axis), line_part(whole, me - far, axis)
    if held is not None:
        right, left = right + held[0].astype(F32), left + held[1].astype(F32)
    right = lax.ppermute(right.astype(BF), axis, [(i, i + 1) for i in range(k)])
    left = lax.ppermute(left.astype(BF), axis, [(i, i - 1) for i in range(far, count)])
    return right, left


def reduce_end(whole, held, axis):
    return line_part(whole, lax.axis_index(axis), axis) + held[0].astype(F32) + held[1].astype(F32)


def small_sum(own, axis):
    count = lax.axis_size(axis)
    total = own
    for k in range(1, count):
        total = total + lax.ppermute(own, axis, [(i, (i + k) % count) for i in range(count)])
    return total


def small_gather(own, axis):
    count, me = lax.axis_size(axis), lax.axis_index(axis)
    width = own.shape[1]
    total = lax.dynamic_update_slice(jnp.zeros((own.shape[0], count * width), own.dtype), own, (0, me * width))
    for k in range(1, count):
        piece = lax.ppermute(own, axis, [(i, (i + k) % count) for i in range(count)])
        total = lax.dynamic_update_slice(total, piece, (0, lax.rem(me - k + count, count) * width))
    return total


def sum_small(parts, axes):
    width = 256
    padded = []
    for part in parts:
        columns = -part.shape[1] % width
        padded.append(jnp.pad(part, ((0, 0), (0, columns))).reshape(-1, width))
    counts = [p.shape[0] for p in padded]
    joined = jnp.concatenate(padded + [jnp.zeros((-sum(counts) % 16, width), F32)], axis=0).astype(BF)
    joined = jnp.sum(lax.all_gather(joined, axes).astype(F32), axis=0)
    out, start = [], 0
    for part, rows in zip(parts, counts):
        out.append(joined[start : start + rows].reshape(part.shape[0], -1)[:, : part.shape[1]])
        start += rows
    return out


def by_step(values):
    length, width = values.shape
    return values.reshape(SEGS, length // SEGS, width).transpose(1, 0, 2).reshape(length, width)


def by_segment(values):
    length, width = values.shape
    return values.reshape(length // SEGS, SEGS, width).transpose(1, 0, 2).reshape(length, width)


def block_diagonal(blocks, width):
    heads, wide = blocks.shape[0], blocks.shape[1]
    rows = [jnp.pad(blocks[h], ((0, 0), (h * wide, width - (h + 1) * wide))) for h in range(heads)]
    rows.append(jnp.zeros((width - heads * wide, width), blocks.dtype))
    return jnp.concatenate(rows, axis=0)


def diagonal_rows(dense, heads, wide):
    blocks = [dense[h * wide : (h + 1) * wide, h * wide : (h + 1) * wide] for h in range(heads)]
    return jnp.concatenate(blocks, axis=0)


def forward_kernel(
    conv_in, same, prefix, params, decay_w, input_w,
    out_conv, out_decay, out_gate, out_retain, out_prod, out_state, out_pre_a, out_pre_b, out_total,
    last_rows, prod_now, state_now, inflow_s,
):
    step = pl.program_id(0)
    rows = conv_in.shape[0]

    @pl.when(step == 0)
    def _():
        last_rows[...] = prefix[...].astype(F32)
        prod_now[...] = jnp.ones_like(prod_now)
        state_now[...] = jnp.zeros_like(state_now)

    now = conv_in[...].astype(BF).astype(F32)
    ext = jnp.concatenate([last_rows[...], now], axis=0)
    same_all = same[...]
    total = params[4:5, :] + params[0:1, :] * now
    for k in (1, 2, 3):
        start = 24 - 8 * k
        total = total + params[k : k + 1, :] * ext[start : start + rows] * same_all[:, k : k + 1]
    last_rows[...] = now[rows - 24 :]
    out_conv[...] = total
    low = total.astype(BF)
    decay_sig = jax.nn.sigmoid(jnp.dot(low, decay_w[...], preferred_element_type=F32) + params[5:6, :])
    gate_sig = jax.nn.sigmoid(jnp.dot(low, input_w[...], preferred_element_type=F32) + params[6:7, :])
    out_decay[...] = decay_sig
    out_gate[...] = gate_sig
    expo = params[7:8, :] * decay_sig
    out_retain[...] = same_all[:, 1:2] * jnp.exp(-expo)
    inflow_s[...] = jnp.sqrt(one_minus_exp(2.0 * expo)) * gate_sig * total
    prod, state = prod_now[...], state_now[...]
    for t in range(rows // SEGS):
        at = slice(t * SEGS, (t + 1) * SEGS)
        keep = out_retain[at, :]
        prod = prod * keep
        state = state * keep + inflow_s[at, :]
        out_prod[at, :] = prod
        out_state[at, :] = state
    prod_now[...] = prod
    state_now[...] = state

    @pl.when(step == pl.num_programs(0) - 1)
    def _():
        carry_a = jnp.ones_like(prod[0:1])
        carry_b = jnp.zeros_like(carry_a)
        for s in range(SEGS):
            out_pre_a[s : s + 1, :] = carry_a
            out_pre_b[s : s + 1, :] = carry_b
            carry_b = prod[s : s + 1] * carry_b + state[s : s + 1]
            carry_a = prod[s : s + 1] * carry_a
        out_total[0:1, :] = carry_a
        out_total[1:2, :] = carry_b
        out_total[2:8, :] = jnp.zeros((6, carry_a.shape[1]), F32)


def recur_forward(conv_in, same, prefix, params, decay_w, input_w, rows=128):
    length, width = conv_in.shape[0], params.shape[1]
    block = pl.BlockSpec((rows, width), lambda i: (i, 0))
    fixed = lambda shape: pl.BlockSpec(shape, lambda i: (0, 0))
    big = jax.ShapeDtypeStruct((length, width), F32)
    small = jax.ShapeDtypeStruct((SEGS, width), F32)
    return pl.pallas_call(
        forward_kernel,
        grid=(length // rows,),
        in_specs=[
            block,
            pl.BlockSpec((rows, 8), lambda i: (i, 0)),
            fixed((24, width)),
            fixed((8, width)),
            fixed((width, width)),
            fixed((width, width)),
        ],
        out_specs=[block] * 6 + [fixed((SEGS, width))] * 3,
        out_shape=[big] * 6 + [small] * 3,
        scratch_shapes=[
            pltpu.VMEM((24, width), F32),
            pltpu.VMEM((SEGS, width), F32),
            pltpu.VMEM((SEGS, width), F32),
            pltpu.VMEM((rows, width), F32),
        ],
        compiler_params=pltpu.CompilerParams(vmem_limit_bytes=LIMIT),
        cost_estimate=pl.CostEstimate(flops=length * width, bytes_accessed=4 * length * width, transcendentals=0),
    )(conv_in, same, prefix, params, decay_w, input_w)


def adjoint_kernel(
    gated_grad, gate_branch, hidden, retain,
    out_local, out_after, out_branch, out_pre_a, out_pre_b, out_total, out_dot,
    local_now, after_now, next_retain, grad_s,
):
    step = pl.program_id(0)
    rows = gated_grad.shape[0]

    @pl.when(step == 0)
    def _():
        local_now[...] = jnp.zeros_like(local_now)
        after_now[...] = jnp.ones_like(after_now)
        next_retain[...] = jnp.ones_like(next_retain)

    value, slope = gelu_both(gate_branch[...])
    upstream = gated_grad[...]
    grad_s[...] = upstream * value
    branch = upstream * hidden[...] * slope
    out_branch[...] = branch.astype(BF)
    out_dot[...] = jnp.broadcast_to(jnp.sum(branch * gate_branch[...], axis=1, keepdims=True), out_dot.shape)
    local, after, keep = local_now[...], after_now[...], next_retain[...]
    for t in reversed(range(rows // SEGS)):
        at = slice(t * SEGS, (t + 1) * SEGS)
        local = grad_s[at, :] + keep * local
        after = keep * after
        out_local[at, :] = local
        out_after[at, :] = after
        keep = retain[at, :]
    local_now[...] = local
    after_now[...] = after
    next_retain[...] = keep

    @pl.when(step == pl.num_programs(0) - 1)
    def _():
        carry_a = jnp.ones_like(local[0:1])
        carry_b = jnp.zeros_like(carry_a)
        for s in reversed(range(SEGS)):
            out_pre_a[s : s + 1, :] = carry_a
            out_pre_b[s : s + 1, :] = carry_b
            carry_b = keep[s : s + 1] * (local[s : s + 1] + after[s : s + 1] * carry_b)
            carry_a = keep[s : s + 1] * after[s : s + 1] * carry_a
        out_total[0:1, :] = carry_a
        out_total[1:2, :] = carry_b
        out_total[2:8, :] = jnp.zeros((6, carry_a.shape[1]), F32)


def recur_adjoint(gated_grad, gate_branch, hidden, retain, rows=128):
    length, width = gated_grad.shape
    last = length // rows - 1
    block = pl.BlockSpec((rows, width), lambda i: (last - i, 0))
    second = pl.BlockSpec((rows, width), lambda i: (last - i, 1))
    fixed = lambda shape: pl.BlockSpec(shape, lambda i: (0, 0))
    big = jax.ShapeDtypeStruct((length, width), F32)
    small = jax.ShapeDtypeStruct((SEGS, width), F32)
    return pl.pallas_call(
        adjoint_kernel,
        grid=(length // rows,),
        in_specs=[block, second, block, block],
        out_specs=[block] * 3 + [fixed((SEGS, width))] * 3 + [pl.BlockSpec((rows, 128), lambda i: (last - i, 0))],
        out_shape=[big, big, jax.ShapeDtypeStruct((length, width), BF)]
        + [small] * 3
        + [jax.ShapeDtypeStruct((length, 128), F32)],
        scratch_shapes=[pltpu.VMEM((SEGS, width), F32)] * 3 + [pltpu.VMEM((rows, width), F32)],
        compiler_params=pltpu.CompilerParams(vmem_limit_bytes=LIMIT),
        cost_estimate=pl.CostEstimate(flops=length * width, bytes_accessed=4 * length * width, transcendentals=0),
    )(gated_grad, gate_branch, hidden, retain)


def backward_kernel(
    local, after, enter, hidden, hidden_before, carry, conv_out, decay_sig, gate_sig, retain, same, params, conv_in,
    decay_w, input_w,
    out_decay, out_input, out_low, out_first, out_sums,
    next_one, next_two, next_three,
):
    step = pl.program_id(0)
    blocks = pl.num_programs(0)
    rows = local.shape[0]
    width = local.shape[1]

    @pl.when(step == 0)
    def _():
        for held in (next_one, next_two, next_three):
            held[...] = jnp.zeros_like(held)
        out_sums[...] = jnp.zeros_like(out_sums)

    def per_step(small):
        return jnp.broadcast_to(small[None], (rows // SEGS, SEGS, width)).reshape(rows, width)

    def sums(values):
        return jnp.sum(values.reshape(rows // SEGS, SEGS, width), axis=0)

    adjoint = local[...] + after[...] * per_step(enter[...])
    ahead = jnp.where(step == blocks - 1, carry[...], hidden_before[...])
    hidden_prev = jnp.concatenate([ahead, hidden[...][: rows - SEGS]], axis=0)
    conv, decay, gate = conv_out[...], decay_sig[...], gate_sig[...]
    rate = params[7:8, :]
    expo = rate * decay
    inner = one_minus_exp(2.0 * expo)
    root = jnp.sqrt(inner)
    expo_grad = adjoint * (gate * conv * (1.0 - inner) / root - retain[...] * hidden_prev)
    decay_grad = (expo_grad * rate * decay * (1.0 - decay)).astype(BF)
    input_grad = (adjoint * root * conv * gate * (1.0 - gate)).astype(BF)
    out_decay[...] = decay_grad
    out_input[...] = input_grad
    dims = (((1,), (1,)), ((), ()))
    conv_grad = (
        adjoint * root * gate
        + lax.dot_general(decay_grad, decay_w[...], dims, preferred_element_type=F32)
        + lax.dot_general(input_grad, input_w[...], dims, preferred_element_type=F32)
    )
    same_all = same[...]
    now = conv_in[...].astype(BF).astype(F32)
    low = params[0:1, :] * conv_grad
    out_sums[0:8, :] += sums(conv_grad * now)
    for k, held in ((1, next_one), (2, next_two), (3, next_three)):
        masked = conv_grad * same_all[:, k : k + 1]
        moved = jnp.concatenate([masked[8 * k :], held[...]], axis=0)
        held[...] = masked[: 8 * k]
        low = low + params[k : k + 1, :] * moved
        out_sums[8 * k : 8 * k + 8, :] += sums(moved * now)
    out_low[...] = low
    out_sums[32:40, :] += sums(conv_grad)
    out_sums[40:48, :] += sums(decay_grad.astype(F32))
    out_sums[48:56, :] += sums(input_grad.astype(F32))
    out_sums[56:64, :] += sums(expo_grad * decay)

    @pl.when(step == blocks - 1)
    def _():
        out_first[0:8, :] = next_one[...]
        out_first[8:24, :] = next_two[...]
        out_first[24:48, :] = next_three[...]


def recur_backward(
    local, after, enter, hidden, carry, conv_out, decay_sig, gate_sig, retain, same, params, conv_in, decay_w, input_w,
    rows=128,
):
    length, width = local.shape
    last = length // rows - 1
    block = pl.BlockSpec((rows, width), lambda i: (last - i, 0))
    fixed = lambda shape: pl.BlockSpec(shape, lambda i: (0, 0))
    steps = rows // SEGS
    before = pl.BlockSpec((SEGS, width), lambda i: (jnp.maximum((last - i) * steps - 1, 0), 0))
    return pl.pallas_call(
        backward_kernel,
        grid=(length // rows,),
        in_specs=[
            block, block, fixed((SEGS, width)), block, before, fixed((SEGS, width)), block, block, block, block,
            pl.BlockSpec((rows, 8), lambda i: (last - i, 0)),
            fixed((8, width)), block, fixed((width, width)), fixed((width, width)),
        ],
        out_specs=[block, block, block, fixed((48, width)), fixed((64, width))],
        out_shape=[
            jax.ShapeDtypeStruct((length, width), BF),
            jax.ShapeDtypeStruct((length, width), BF),
            jax.ShapeDtypeStruct((length, width), F32),
            jax.ShapeDtypeStruct((48, width), F32),
            jax.ShapeDtypeStruct((64, width), F32),
        ],
        scratch_shapes=[
            pltpu.VMEM((8, width), F32),
            pltpu.VMEM((16, width), F32),
            pltpu.VMEM((24, width), F32),
        ],
        compiler_params=pltpu.CompilerParams(vmem_limit_bytes=LIMIT),
        cost_estimate=pl.CostEstimate(flops=length * width, bytes_accessed=4 * length * width, transcendentals=0),
    )(
        local, after, enter, hidden, hidden, carry, conv_out, decay_sig, gate_sig, retain, same, params, conv_in,
        decay_w, input_w,
    )


def exchange_kernel(count, chunks, mode, *refs):
    backward, summing = mode == "back", mode != "first"
    if backward:
        (partial, residual, middle, scale, mean, gain, out, out_own, out_gain) = refs[:9]
        gathered = out
        rest = refs[9:]
    elif summing:
        (partial, residual, gain, out, out_scale, out_own, gathered) = refs[:7]
        rest = refs[7:]
    else:
        (residual, gain, out, out_scale, gathered) = refs[:5]
        rest = refs[5:]
    if summing:
        right, left, total, sum_send, sum_recv, all_send, all_recv = rest
    else:
        all_send, all_recv = rest
    me = lax.axis_index("rep")
    length, width = residual.shape
    rows = length // chunks
    last = count - 1

    barrier = pltpu.get_barrier_semaphore()

    @pl.when(me > 0)
    def _():
        pl.semaphore_signal(barrier, inc=1, device_id={"rep": me - 1}, device_id_type=pl.DeviceIdType.MESH)

    @pl.when(me < last)
    def _():
        pl.semaphore_signal(barrier, inc=1, device_id={"rep": me + 1}, device_id_type=pl.DeviceIdType.MESH)

    inner = jnp.logical_and(me > 0, me < last)

    @pl.when(inner)
    def _():
        pl.semaphore_wait(barrier, 2)

    @pl.when(jnp.logical_not(inner))
    def _():
        pl.semaphore_wait(barrier, 1)

    if backward:
        out_gain[...] = jnp.zeros_like(out_gain)

    def at(c):
        return pl.ds(pl.multiple_of(c * rows, rows), rows)

    def columns(device):
        return pl.ds(pl.multiple_of(device * width, width), width)

    def sum_copy(side, slot, c):
        buffer, to = ((right, me + 1), (left, me - 1))[side]
        return pltpu.make_async_remote_copy(
            src_ref=buffer.at[slot, at(c)],
            dst_ref=buffer.at[slot - 1, at(c)],
            send_sem=sum_send.at[side, slot, c],
            recv_sem=sum_recv.at[side, slot - 1, c],
            device_id={"rep": to},
            device_id_type=pl.DeviceIdType.MESH,
        )

    def sum_arrived(side, slot, c):
        buffer, sender = ((right, me - 1), (left, me + 1))[side]
        pltpu.make_async_remote_copy(
            src_ref=buffer.at[slot, at(c)],
            dst_ref=buffer.at[slot, at(c)],
            send_sem=sum_send.at[side, slot, c],
            recv_sem=sum_recv.at[side, slot, c],
            device_id={"rep": sender},
            device_id_type=pl.DeviceIdType.MESH,
        ).wait_recv()

    def all_copy(side, far, c):
        source, to = ((me - far, me + 1), (me + far, me - 1))[side]
        piece = gathered.at[at(c), columns(source)]
        return pltpu.make_async_remote_copy(
            src_ref=piece,
            dst_ref=piece,
            send_sem=all_send.at[side, far, c],
            recv_sem=all_recv.at[side, far + 1, c],
            device_id={"rep": to},
            device_id_type=pl.DeviceIdType.MESH,
        )

    def all_arrived(side, far, c):
        source, sender = ((me - far, me - 1), (me + far, me + 1))[side]
        piece = gathered.at[at(c), columns(source)]
        pltpu.make_async_remote_copy(
            src_ref=piece,
            dst_ref=piece,
            send_sem=all_send.at[side, far, c],
            recv_sem=all_recv.at[side, far, c],
            device_id={"rep": sender},
            device_id_type=pl.DeviceIdType.MESH,
        ).wait_recv()

    def inside(c):
        return jnp.logical_and(c >= 0, c < chunks)

    def tick(now, _):
        for side in (0, 1) if summing else ():
            place = (me, last - me)[side]
            c = now - place
            for slot in range(last, 0, -1):

                @pl.when(jnp.logical_and(inside(c), place + slot <= last))
                def _(side=side, place=place, c=c, slot=slot):
                    buffer = (right, left)[side]
                    target = (me + slot, me - slot)[side]

                    @pl.when(place > 0)
                    def _():
                        sum_arrived(side, slot, c)
                        added = buffer[slot, at(c), :].astype(F32) + partial[at(c), columns(target)].astype(F32)
                        buffer[slot, at(c), :] = added.astype(BF)

                    @pl.when(place == 0)
                    def _():
                        buffer[slot, at(c), :] = partial[at(c), columns(target)]

                    sum_copy(side, slot, c).start()

        def finish(done):
            total[...] = partial[at(done), columns(me)].astype(F32)

            @pl.when(me > 0)
            def _():
                sum_arrived(0, 0, done)
                total[...] += right[0, at(done), :].astype(F32)

            @pl.when(me < last)
            def _():
                sum_arrived(1, 0, done)
                total[...] += left[0, at(done), :].astype(F32)

            if backward:
                size = scale[at(done), 0:1]
                normal = middle[at(done), :] * size
                summed = total[...]
                own = residual[at(done), :].astype(F32) + size * (
                    summed * gain[...] - normal * mean[at(done), 0:1]
                )
                out_gain[...] += jnp.sum((summed * normal).reshape(rows // 8, 8, width), axis=0)
            else:
                own = residual[at(done), :].astype(F32) + total[...]
            out_own[at(done), :] = own
            gathered[at(done), columns(me)] = own.astype(BF)

        done = now - last if summing else now

        @pl.when(inside(done))
        def _():
            if summing:
                finish(done)
            else:
                gathered[at(done), columns(me)] = residual[at(done), :]

            @pl.when(me < last)
            def _():
                all_copy(0, 0, done).start()

            @pl.when(me > 0)
            def _():
                all_copy(1, 0, done).start()

        for far in range(1, count):
            c = done - far
            for side in (0, 1):
                place = (me, last - me)[side]

                @pl.when(jnp.logical_and(inside(c), place >= far))
                def _(side=side, place=place, c=c, far=far):
                    all_arrived(side, far, c)

                    @pl.when(place < last)
                    def _():
                        all_copy(side, far, c).start()

        if not backward:
            full = done - last

            @pl.when(inside(full))
            def _():
                values = gathered[at(full), :].astype(F32)
                size = lax.rsqrt(jnp.mean(values * values, axis=1, keepdims=True) + eps)
                out[at(full), :] = (values * size * gain[...]).astype(BF)
                out_scale[at(full), :] = jnp.broadcast_to(size, (rows, 128))

        return 0

    lax.fori_loop(0, chunks + (2 * last if summing else last), tick, 0)

    def settle(c, _):
        for side in (0, 1):
            place = (me, last - me)[side]
            for slot in range(1, count) if summing else ():

                @pl.when(place + slot <= last)
                def _(side=side, slot=slot):
                    sum_copy(side, slot, c).wait_send()

            for far in range(0, last):

                @pl.when(jnp.logical_and(place < last, place >= far))
                def _(side=side, far=far):
                    all_copy(side, far, c).wait_send()

        return 0

    lax.fori_loop(0, chunks, settle, 0)


def exchange(mode, operands, width, chunks=16):
    count = lax.axis_size("rep")
    length = operands[0].shape[0]
    features = count * width
    backward, summing = mode == "back", mode != "first"
    vmem = pl.BlockSpec(memory_space=pltpu.VMEM)
    scratch = [pltpu.SemaphoreType.DMA((2, count, chunks)), pltpu.SemaphoreType.DMA((2, count, chunks))]
    out_shape = [jax.ShapeDtypeStruct((length, features), BF)]
    if summing:
        scratch = [
            pltpu.VMEM((count, length, width), BF),
            pltpu.VMEM((count, length, width), BF),
            pltpu.VMEM((length // chunks, width), F32),
        ] + scratch * 2
    if not backward:
        out_shape.append(jax.ShapeDtypeStruct((length, 128), F32))
        scratch = [pltpu.VMEM((length, features), BF)] + scratch
    if summing:
        out_shape.append(jax.ShapeDtypeStruct((length, width), F32))
    if backward:
        out_shape.append(jax.ShapeDtypeStruct((8, width), F32))
    return pl.pallas_call(
        partial_call(exchange_kernel, count, chunks, mode),
        in_specs=[vmem] * len(operands),
        out_specs=[vmem] * len(out_shape),
        out_shape=out_shape,
        scratch_shapes=scratch,
        compiler_params=pltpu.CompilerParams(
            collective_id=("first", "norm", "back").index(mode), has_side_effects=True, vmem_limit_bytes=LIMIT
        ),
        cost_estimate=pl.CostEstimate(
            flops=10 * length * features, bytes_accessed=160 * length * features, transcendentals=0
        ),
    )(*operands)


def feed_kernel(cot, pre_gate, pre_up, down, out_low, out_grads, out_dot):
    half = out_low.shape[1]
    upstream = jnp.dot(cot[...], down[...], preferred_element_type=F32)
    gate_pre, up_pre = pre_gate[...], pre_up[...]
    value, slope = gelu_both(gate_pre)
    out_low[...] = (value * up_pre).astype(BF)
    gate_grad, up_grad = upstream * up_pre * slope, upstream * value
    out_grads[:, :half] = gate_grad.astype(BF)
    out_grads[:, half:] = up_grad.astype(BF)
    dots = jnp.sum(gate_grad * gate_pre + up_grad * up_pre, axis=1, keepdims=True)
    out_dot[...] = jnp.broadcast_to(dots, out_dot.shape)


def feed_backward(cot, pre, down, rows=256):
    length, features = cot.shape
    half = down.shape[1]
    block = lambda width, column=0: pl.BlockSpec((rows, width), lambda i: (i, column))
    return pl.pallas_call(
        feed_kernel,
        grid=(length // rows,),
        in_specs=[
            block(features), block(half), block(half, 1),
            pl.BlockSpec((features, half), lambda i: (0, 0), pipeline_mode=pl.Buffered(1)),
        ],
        out_specs=[block(half), block(2 * half), block(128)],
        out_shape=[
            jax.ShapeDtypeStruct((length, half), BF),
            jax.ShapeDtypeStruct((length, 2 * half), BF),
            jax.ShapeDtypeStruct((length, 128), F32),
        ],
        compiler_params=pltpu.CompilerParams(vmem_limit_bytes=LIMIT),
        cost_estimate=pl.CostEstimate(
            flops=2 * length * features * half, bytes_accessed=40 * length * half, transcendentals=length * half
        ),
    )(cot, pre, pre, down)


def per_segment(small, length):
    return jnp.broadcast_to(small[None], (length // SEGS,) + small.shape).reshape(length, small.shape[1])


def rows_dot(left, right):
    return lax.dot_general(left, right, (((0,), (0,)), ((), ())), preferred_element_type=F32)


def back_dot(left, right):
    return lax.dot_general(left, right, (((1,), (1,)), ((), ())), preferred_element_type=F32)


def dot(left, right):
    return jnp.dot(left, right, preferred_element_type=F32)


def shards(
    block_input, cotangent, segment_ids, pad_mask, state_init, window_init,
    recur_input, recur_gate, recur_output, feed_gate, feed_up, feed_down,
    conv_kernel, conv_bias, decay_gate, input_gate, decay_bias, input_bias, decay_logit, mixer_gain, feed_gain,
):
    own_width = block_input.shape[2]
    features = mixer_gain.shape[0]
    length = segment_ids.shape[1]
    taps = conv_kernel.shape[0]
    edge = taps - 1
    heads, head_width = decay_gate.shape[0], decay_gate.shape[2]
    rep = lax.axis_index("rep")
    seq, seqs = lax.axis_index("seq"), lax.axis_size("seq")
    at_start = seq == 0
    to_next = [(i, i + 1) for i in range(seqs - 1)]
    to_last = [(i + 1, i) for i in range(seqs - 1)]

    def weights(shard):
        return lax.all_gather(shard, ("seq", "row"), axis=0, tiled=True)

    def spread(partial_grad):
        return lax.psum_scatter(partial_grad, ("seq", "row"), scatter_dimension=0, tiled=True)

    def own_part(vector):
        return lax.dynamic_slice_in_dim(vector, rep * own_width, own_width, 0)[None]

    channels = conv_bias.shape[0]
    spare = -channels % 128

    def wide(values, fill=0):
        return jnp.pad(values, ((0, 0),) * (values.ndim - 1) + ((0, spare),), constant_values=fill)

    width = channels + spare

    x_low = by_step(block_input[0])
    x_own = x_low.astype(F32)
    cot_own = by_step(cotangent[0] * pad_mask[0][:, None].astype(BF))
    mixer_own, feed_own = own_part(mixer_gain), own_part(feed_gain)
    normed, s1 = exchange("first", (x_low, mixer_gain[None]), own_width)
    s1 = s1[:, :1]
    w_recur = weights(jnp.concatenate([wide(recur_input), wide(recur_gate), wide(recur_output)], axis=1))
    w_feed = weights(jnp.concatenate([feed_gate, feed_up], axis=1))
    w_down = weights(feed_down)
    w_input, w_output = w_recur[:, : 2 * width], w_recur[:, 2 * width :]

    left_ids = lax.ppermute(segment_ids[:, -edge:].astype(F32), "seq", to_next).astype(jnp.int32)
    left_ids = jnp.where(at_start, jnp.broadcast_to(segment_ids[:, :1], left_ids.shape), left_ids)
    ids_ext = jnp.concatenate([left_ids, segment_ids], axis=1)[0]
    same = [(ids_ext[edge - k : edge - k + length] == segment_ids[0]).astype(F32) for k in range(taps)]
    same = by_step(jnp.stack(same + [same[0]] * (8 - taps), axis=1))

    rate = 8.0 * jax.nn.softplus(decay_logit)
    params = wide(jnp.concatenate([conv_kernel, jnp.stack([conv_bias, decay_bias, input_bias])], axis=0))
    params = jnp.concatenate([params, wide(rate[None], 1)], axis=0)
    decay_w, input_w = block_diagonal(decay_gate, width), block_diagonal(input_gate, width)
    state_init = wide(state_init)

    projected = dot(normed, w_input)
    gate_branch = projected[:, width:]
    ends = projected[-edge * SEGS :, :width].astype(BF).reshape(edge, SEGS, width)
    left = lax.ppermute(ends[:, -1], "seq", to_next)
    left = jnp.where(at_start, wide(window_init[0]), left)
    prefix = jnp.concatenate([left[:, None], ends[:, :-1]], axis=1).reshape(edge * SEGS, -1)
    block_windows = ends[:, -1, :channels]

    conv_out, decay_sig, gate_sig, retain, products, states, pre_a, pre_b, total = recur_forward(
        projected, same, prefix, params, decay_w, input_w
    )
    state_in = state_init
    for k in range(1, seqs):
        arriving = lax.ppermute(total[0:1] * state_in + total[1:2], "seq", to_next)
        state_in = jnp.where(seq == k, arriving, state_in)
    block_states = total[0:1] * state_in + total[1:2]
    carry = pre_a * state_in + pre_b

    cot_own, normed = after((cot_own, normed))
    cot_pass = [(cot_own, cot_own)]
    cot_pass.append(pass_on(cot_pass[-1], 1, "rep"))
    states, cot_pass[-1] = after((states, cot_pass[-1]))
    cot_pass.append(pass_on(cot_pass[-1], 2, "rep"))

    hidden = states + products * per_segment(carry, length)
    gated = (hidden * gelu(gate_branch)).astype(BF)
    branch = back_dot(gated, w_output).astype(BF)
    branch, cot_pass[-1] = after((branch, cot_pass[-1]))
    normed_mid, s2, middle = exchange("norm", (branch, x_low, feed_gain[None]), own_width)
    normed_mid, cot_pass[-1] = after((normed_mid, cot_pass[-1]))
    cot_pass.append(pass_on(cot_pass[-1], 3, "rep"))
    pre = dot(normed_mid, w_feed)
    pre, cot_pass[-1] = after((pre, cot_pass[-1]))
    cot = put_together(cot_pass, "rep")
    feed_low, feed_grads, mid_mean = feed_backward(cot, pre, w_down)
    mid_mean = small_sum(mid_mean[:, 0].reshape(8, -1), "rep").reshape(-1, 1) / features

    half = w_down.shape[1]
    down_grad = rows_dot(cot, feed_low).astype(BF)
    feed_grads, down_grad = after((feed_grads, down_grad))
    feed_all = rows_dot(normed_mid, feed_grads).astype(BF)
    feed_part = back_dot(feed_low, w_down).astype(BF)
    feed_grads, feed_all, feed_part = after((feed_grads, feed_all, feed_part))
    mid_grad = back_dot(feed_grads, w_feed).astype(BF)
    down_grad, feed_all = spread(down_grad), spread(feed_all)
    middle_low, middle_grad, feed_gain_own = exchange(
        "back",
        (mid_grad, cot_own, middle, s2, jnp.broadcast_to(mid_mean, (length, 128)), feed_own),
        own_width,
    )
    middle_low, down_grad, feed_all = after((middle_low, down_grad, feed_all))
    feed_down_grad = down_grad.astype(F32)
    feed_gate_grad, feed_up_grad = feed_all[:, :half].astype(F32), feed_all[:, half:].astype(F32)
    feed_gain_own = jnp.sum(feed_gain_own, axis=0)

    feed_part, middle_low = after((feed_part, middle_low))
    feed_pass = reduce_step(feed_part, None, 1, "rep")
    gated_grad = dot(middle_low, w_output)
    local, after_prod, branch_grad, enter_a, enter_b, back_total, branch_dot = recur_adjoint(
        gated_grad, projected, hidden, retain
    )
    output_all = rows_dot(middle_low, gated).astype(BF)
    local, feed_pass, output_all = after((local, feed_pass, output_all))
    feed_pass = reduce_step(feed_part, feed_pass, 2, "rep")
    output_all = spread(output_all)
    entering = jnp.zeros_like(state_init)
    for k in range(1, seqs):
        arriving = lax.ppermute(back_total[0:1] * entering + back_total[1:2], "seq", to_last)
        entering = jnp.where(seq == seqs - 1 - k, arriving, entering)
    enter = enter_a * entering + enter_b
    decay_grad, input_grad_low, low_grad, first, sums = recur_backward(
        local, after_prod, enter, hidden, carry, conv_out, decay_sig, gate_sig, retain, same, params, projected,
        decay_w, input_w,
    )
    low_grad, feed_pass = after((low_grad, feed_pass))
    for k in range(3, lax.axis_size("rep")):
        feed_pass = reduce_step(feed_part, feed_pass, k, "rep")
    owed = [first[0:8], first[8:24], first[24:48]]
    owed = [o.reshape(k + 1, SEGS, -1) for k, o in enumerate(owed)]
    ahead = prefix.reshape(edge, SEGS, -1).astype(F32)
    back_share = jnp.zeros_like(ahead)
    tap_extra = [jnp.zeros((width,), F32)]
    for k in range(1, taps):
        term = jnp.pad(owed[k - 1], ((edge - k, 0), (0, 0), (0, 0)))
        tap_extra.append(jnp.sum(term * ahead, axis=(0, 1)))
        back_share = back_share + params[k] * term
    from_right = lax.ppermute(back_share[:, 0], "seq", to_last)
    share = jnp.concatenate([back_share[:, 1:], from_right[:, None]], axis=1)
    low_grad = low_grad.reshape(length // SEGS, SEGS, -1)
    low_grad = jnp.concatenate([low_grad[:-edge], low_grad[-edge:] + share], axis=0).reshape(length, -1)
    in_mean = jnp.sum(low_grad * projected[:, :width].astype(BF).astype(F32), axis=1) + branch_dot[:, 0]
    in_mean = small_sum(in_mean.reshape(8, -1), "rep").reshape(-1, 1) / features

    both_grads = jnp.concatenate([low_grad.astype(BF), branch_grad], axis=1)
    normed_part = back_dot(both_grads, w_input).astype(BF)
    normed_part, output_all, feed_pass = after((normed_part, output_all, feed_pass))
    feed_out = reduce_end(feed_part, feed_pass, "rep")
    block_output = by_segment((middle + feed_out).astype(BF))[None]
    normed_part, both_grads, conv_out, decay_grad, input_grad_low = after(
        (normed_part, both_grads, conv_out, decay_grad, input_grad_low)
    )
    conv_low = conv_out.astype(BF)
    decay_gate_grad = diagonal_rows(rows_dot(conv_low, decay_grad), heads, head_width)
    input_gate_grad = diagonal_rows(rows_dot(conv_low, input_grad_low), heads, head_width)
    sums = jnp.sum(sums.reshape(8, 8, -1), axis=1)
    conv_kernel_grad = sums[:taps] + jnp.stack(tap_extra)
    logit_grad = sums[7:, :channels] * 8.0 * jax.nn.sigmoid(decay_logit)
    vectors = jnp.concatenate([conv_kernel_grad, sums[4:7]], axis=0)[:, :channels]
    vectors = jnp.concatenate([vectors, logit_grad], axis=0)
    parts = (decay_gate_grad, input_gate_grad, vectors)
    both_grads, parts = after((both_grads, parts))
    summed = sum_small(parts, ("seq", "row"))
    recur_all = spread(rows_dot(normed, both_grads).astype(BF))
    recur_output_grad = output_all[:, :channels].astype(F32)
    recur_input_grad = recur_all[:, :channels].astype(F32)
    recur_gate_grad = recur_all[:, width : width + channels].astype(F32)
    decay_gate_grad, input_gate_grad = (g[:, :head_width].reshape(decay_gate.shape) for g in summed[:2])
    vectors = summed[2]

    normed_pass = None
    for k in range(1, lax.axis_size("rep")):
        normed_pass = reduce_step(normed_part, normed_pass, k, "rep")
    normed_grad = reduce_end(normed_part, normed_pass, "rep")
    xh1 = x_own * s1
    mixer_gain_own = jnp.sum(normed_grad * xh1, axis=0)
    input_grad = middle_grad + s1 * (normed_grad * mixer_own - xh1 * in_mean)
    input_grad = by_segment(input_grad.astype(BF))[None]
    gains = jnp.stack([mixer_gain_own, feed_gain_own]).reshape(8, -1)
    gains = small_sum(small_sum(gains, "row"), "seq").reshape(2, own_width)
    gains = small_gather(gains, "rep")
    return (
        block_output, block_states[:, None, :channels], block_windows[None, None], input_grad,
        recur_input_grad, recur_gate_grad, recur_output_grad, feed_gate_grad, feed_up_grad, feed_down_grad,
        vectors[:taps], vectors[4], decay_gate_grad, input_gate_grad, vectors[5], vectors[6], vectors[7],
        gains[0], gains[1],
    )


def solution(mesh):
    tokens = P("row", "seq", "rep")
    matrix = P(("seq", "row"), "rep")
    in_specs = (
        tokens, tokens, P("row", "seq"), P("row", "seq"), P("row", "rep"), P("row", None, "rep"),
        matrix, matrix, matrix, matrix, matrix, matrix,
        P(None, "rep"), P("rep"), P("rep", None, None), P("rep", None, None), P("rep"), P("rep"), P("rep"), P(), P(),
    )
    out_specs = (
        tokens, tokens, P("row", "seq", None, "rep"), tokens,
        matrix, matrix, matrix, matrix, matrix, matrix,
        P(None, "rep"), P("rep"), P("rep", None, None), P("rep", None, None), P("rep"), P("rep"), P("rep"), P(), P(),
    )
    return jax.shard_map(shards, mesh=mesh, in_specs=in_specs, out_specs=out_specs, check_vma=False)
```

```python
from functools import partial as partial_call

import jax
import jax.numpy as jnp
from jax import lax
from jax.experimental import pallas as pl
from jax.experimental.pallas import tpu as pltpu
from jax.sharding import PartitionSpec as P

eps = 1e-06
SEGS = 8
BF = jnp.bfloat16
F32 = jnp.float32
LIMIT = 48 * 1024 * 1024


def gelu(v):
    return 0.5 * v * (1.0 + jnp.tanh(0.7978845608 * (v + 0.044715 * v * v * v)))


def gelu_both(v):
    square = v * v
    t = jnp.tanh(0.7978845608 * v * (1.0 + 0.044715 * square))
    value = 0.5 * v * (1.0 + t)
    slope = 0.5 * (1.0 + t) + 0.5 * v * (1.0 - t * t) * 0.7978845608 * (1.0 + 3 * 0.044715 * square)
    return value, slope


def one_minus_exp(y):
    series = y * (1 - y / 2 * (1 - y / 3 * (1 - y / 4 * (1 - y / 5 * (1 - y / 6 * (1 - y / 7))))))
    return jnp.where(y < 0.4, series, 1.0 - jnp.exp(-y))


after = lax.optimization_barrier


def small_sum(own, axis):
    count = lax.axis_size(axis)
    total = own
    for k in range(1, count):
        total = total + lax.ppermute(own, axis, [(i, (i + k) % count) for i in range(count)])
    return total


def small_gather(own, axis):
    count, me = lax.axis_size(axis), lax.axis_index(axis)
    width = own.shape[1]
    total = lax.dynamic_update_slice(jnp.zeros((own.shape[0], count * width), own.dtype), own, (0, me * width))
    for k in range(1, count):
        piece = lax.ppermute(own, axis, [(i, (i + k) % count) for i in range(count)])
        total = lax.dynamic_update_slice(total, piece, (0, lax.rem(me - k + count, count) * width))
    return total


def join_small(parts):
    width = 256
    padded = []
    for part in parts:
        columns = -part.shape[1] % width
        padded.append(jnp.pad(part, ((0, 0), (0, columns))).reshape(-1, width))
    counts = [p.shape[0] for p in padded]
    spare = jnp.zeros((-sum(counts) % 16, width), F32)
    return jnp.concatenate(padded + [spare], axis=0).astype(BF), counts


def split_small(joined, counts, parts):
    out, start = [], 0
    for part, rows in zip(parts, counts):
        out.append(joined[start : start + rows].reshape(part.shape[0], -1)[:, : part.shape[1]])
        start += rows
    return out


def by_step(values):
    length, width = values.shape
    return values.reshape(SEGS, length // SEGS, width).transpose(1, 0, 2).reshape(length, width)


def by_segment(values):
    length, width = values.shape
    return values.reshape(length // SEGS, SEGS, width).transpose(1, 0, 2).reshape(length, width)


def block_diagonal(blocks, width):
    heads, wide = blocks.shape[0], blocks.shape[1]
    rows = [jnp.pad(blocks[h], ((0, 0), (h * wide, width - (h + 1) * wide))) for h in range(heads)]
    rows.append(jnp.zeros((width - heads * wide, width), blocks.dtype))
    return jnp.concatenate(rows, axis=0)


def diagonal_rows(dense, heads, wide):
    blocks = [dense[h * wide : (h + 1) * wide, h * wide : (h + 1) * wide] for h in range(heads)]
    return jnp.concatenate(blocks, axis=0)


def forward_kernel(
    conv_in, gate_branch, same, prefix, params, decay_w, input_w,
    out_gelu, out_conv, out_decay, out_gate, out_retain, out_prod, out_state, out_pre_a, out_pre_b, out_total,
    last_rows, prod_now, state_now, inflow_s,
):
    step = pl.program_id(0)
    rows = conv_in.shape[0]

    @pl.when(step == 0)
    def _():
        last_rows[...] = prefix[...].astype(F32)
        prod_now[...] = jnp.ones_like(prod_now)
        state_now[...] = jnp.zeros_like(state_now)

    out_gelu[...] = gelu(gate_branch[...])
    now = conv_in[...].astype(BF).astype(F32)
    ext = jnp.concatenate([last_rows[...], now], axis=0)
    same_all = same[...]
    total = params[4:5, :] + params[0:1, :] * now
    for k in (1, 2, 3):
        start = 24 - 8 * k
        total = total + params[k : k + 1, :] * ext[start : start + rows] * same_all[:, k : k + 1]
    last_rows[...] = now[rows - 24 :]
    out_conv[...] = total
    low = total.astype(BF)
    decay_sig = jax.nn.sigmoid(jnp.dot(low, decay_w[...], preferred_element_type=F32) + params[5:6, :])
    gate_sig = jax.nn.sigmoid(jnp.dot(low, input_w[...], preferred_element_type=F32) + params[6:7, :])
    out_decay[...] = decay_sig
    out_gate[...] = gate_sig
    expo = params[7:8, :] * decay_sig
    out_retain[...] = same_all[:, 1:2] * jnp.exp(-expo)
    inflow_s[...] = jnp.sqrt(one_minus_exp(2.0 * expo)) * gate_sig * total
    prod, state = prod_now[...], state_now[...]
    for t in range(rows // SEGS):
        at = slice(t * SEGS, (t + 1) * SEGS)
        keep = out_retain[at, :]
        prod = prod * keep
        state = state * keep + inflow_s[at, :]
        out_prod[at, :] = prod
        out_state[at, :] = state
    prod_now[...] = prod
    state_now[...] = state

    @pl.when(step == pl.num_programs(0) - 1)
    def _():
        carry_a = jnp.ones_like(prod[0:1])
        carry_b = jnp.zeros_like(carry_a)
        for s in range(SEGS):
            out_pre_a[s : s + 1, :] = carry_a
            out_pre_b[s : s + 1, :] = carry_b
            carry_b = prod[s : s + 1] * carry_b + state[s : s + 1]
            carry_a = prod[s : s + 1] * carry_a
        out_total[0:1, :] = carry_a
        out_total[1:2, :] = carry_b
        out_total[2:8, :] = jnp.zeros((6, carry_a.shape[1]), F32)


def recur_forward(conv_in, same, prefix, params, decay_w, input_w, rows=128):
    length, width = conv_in.shape[0], params.shape[1]
    block = pl.BlockSpec((rows, width), lambda i: (i, 0))
    fixed = lambda shape: pl.BlockSpec(shape, lambda i: (0, 0))
    big = jax.ShapeDtypeStruct((length, width), F32)
    small = jax.ShapeDtypeStruct((SEGS, width), F32)
    return pl.pallas_call(
        forward_kernel,
        grid=(length // rows,),
        in_specs=[
            block,
            pl.BlockSpec((rows, width), lambda i: (i, 1)),
            pl.BlockSpec((rows, 8), lambda i: (i, 0)),
            fixed((24, width)),
            fixed((8, width)),
            fixed((width, width)),
            fixed((width, width)),
        ],
        out_specs=[block] * 7 + [fixed((SEGS, width))] * 3,
        out_shape=[big] * 7 + [small] * 3,
        scratch_shapes=[
            pltpu.VMEM((24, width), F32),
            pltpu.VMEM((SEGS, width), F32),
            pltpu.VMEM((SEGS, width), F32),
            pltpu.VMEM((rows, width), F32),
        ],
        compiler_params=pltpu.CompilerParams(vmem_limit_bytes=LIMIT),
        cost_estimate=pl.CostEstimate(flops=length * width, bytes_accessed=4 * length * width, transcendentals=0),
    )(conv_in, conv_in, same, prefix, params, decay_w, input_w)


def adjoint_kernel(
    gated_grad, gate_branch, hidden, retain,
    out_local, out_after, out_branch, out_pre_a, out_pre_b, out_total, out_dot,
    local_now, after_now, next_retain, grad_s,
):
    step = pl.program_id(0)
    rows = gated_grad.shape[0]

    @pl.when(step == 0)
    def _():
        local_now[...] = jnp.zeros_like(local_now)
        after_now[...] = jnp.ones_like(after_now)
        next_retain[...] = jnp.ones_like(next_retain)

    value, slope = gelu_both(gate_branch[...])
    upstream = gated_grad[...]
    grad_s[...] = upstream * value
    branch = upstream * hidden[...] * slope
    out_branch[...] = branch.astype(BF)
    out_dot[...] = jnp.broadcast_to(jnp.sum(branch * gate_branch[...], axis=1, keepdims=True), out_dot.shape)
    local, after, keep = local_now[...], after_now[...], next_retain[...]
    for t in reversed(range(rows // SEGS)):
        at = slice(t * SEGS, (t + 1) * SEGS)
        local = grad_s[at, :] + keep * local
        after = keep * after
        out_local[at, :] = local
        out_after[at, :] = after
        keep = retain[at, :]
    local_now[...] = local
    after_now[...] = after
    next_retain[...] = keep

    @pl.when(step == pl.num_programs(0) - 1)
    def _():
        carry_a = jnp.ones_like(local[0:1])
        carry_b = jnp.zeros_like(carry_a)
        for s in reversed(range(SEGS)):
            out_pre_a[s : s + 1, :] = carry_a
            out_pre_b[s : s + 1, :] = carry_b
            carry_b = keep[s : s + 1] * (local[s : s + 1] + after[s : s + 1] * carry_b)
            carry_a = keep[s : s + 1] * after[s : s + 1] * carry_a
        out_total[0:1, :] = carry_a
        out_total[1:2, :] = carry_b
        out_total[2:8, :] = jnp.zeros((6, carry_a.shape[1]), F32)


def recur_adjoint(gated_grad, gate_branch, hidden, retain, rows=128):
    length, width = gated_grad.shape
    last = length // rows - 1
    block = pl.BlockSpec((rows, width), lambda i: (last - i, 0))
    second = pl.BlockSpec((rows, width), lambda i: (last - i, 1))
    fixed = lambda shape: pl.BlockSpec(shape, lambda i: (0, 0))
    big = jax.ShapeDtypeStruct((length, width), F32)
    small = jax.ShapeDtypeStruct((SEGS, width), F32)
    return pl.pallas_call(
        adjoint_kernel,
        grid=(length // rows,),
        in_specs=[block, second, block, block],
        out_specs=[block] * 3 + [fixed((SEGS, width))] * 3 + [pl.BlockSpec((rows, 128), lambda i: (last - i, 0))],
        out_shape=[big, big, jax.ShapeDtypeStruct((length, width), BF)]
        + [small] * 3
        + [jax.ShapeDtypeStruct((length, 128), F32)],
        scratch_shapes=[pltpu.VMEM((SEGS, width), F32)] * 3 + [pltpu.VMEM((rows, width), F32)],
        compiler_params=pltpu.CompilerParams(vmem_limit_bytes=LIMIT),
        cost_estimate=pl.CostEstimate(flops=length * width, bytes_accessed=4 * length * width, transcendentals=0),
    )(gated_grad, gate_branch, hidden, retain)


def backward_kernel(
    local, after, enter, hidden, hidden_before, carry, conv_out, decay_sig, gate_sig, retain, same, params, conv_in,
    decay_w, input_w,
    out_decay, out_input, out_low, out_first, out_sums,
    next_one, next_two, next_three,
):
    step = pl.program_id(0)
    blocks = pl.num_programs(0)
    rows = local.shape[0]
    width = local.shape[1]

    @pl.when(step == 0)
    def _():
        for held in (next_one, next_two, next_three):
            held[...] = jnp.zeros_like(held)
        out_sums[...] = jnp.zeros_like(out_sums)

    def per_step(small):
        return jnp.broadcast_to(small[None], (rows // SEGS, SEGS, width)).reshape(rows, width)

    def sums(values):
        return jnp.sum(values.reshape(rows // SEGS, SEGS, width), axis=0)

    adjoint = local[...] + after[...] * per_step(enter[...])
    ahead = jnp.where(step == blocks - 1, carry[...], hidden_before[...])
    hidden_prev = jnp.concatenate([ahead, hidden[...][: rows - SEGS]], axis=0)
    conv, decay, gate = conv_out[...], decay_sig[...], gate_sig[...]
    rate = params[7:8, :]
    expo = rate * decay
    inner = one_minus_exp(2.0 * expo)
    root = jnp.sqrt(inner)
    expo_grad = adjoint * (gate * conv * (1.0 - inner) / root - retain[...] * hidden_prev)
    decay_grad = (expo_grad * rate * decay * (1.0 - decay)).astype(BF)
    input_grad = (adjoint * root * conv * gate * (1.0 - gate)).astype(BF)
    out_decay[...] = decay_grad
    out_input[...] = input_grad
    dims = (((1,), (1,)), ((), ()))
    conv_grad = (
        adjoint * root * gate
        + lax.dot_general(decay_grad, decay_w[...], dims, preferred_element_type=F32)
        + lax.dot_general(input_grad, input_w[...], dims, preferred_element_type=F32)
    )
    same_all = same[...]
    now = conv_in[...].astype(BF).astype(F32)
    low = params[0:1, :] * conv_grad
    out_sums[0:8, :] += sums(conv_grad * now)
    for k, held in ((1, next_one), (2, next_two), (3, next_three)):
        masked = conv_grad * same_all[:, k : k + 1]
        moved = jnp.concatenate([masked[8 * k :], held[...]], axis=0)
        held[...] = masked[: 8 * k]
        low = low + params[k : k + 1, :] * moved
        out_sums[8 * k : 8 * k + 8, :] += sums(moved * now)
    out_low[...] = low
    out_sums[32:40, :] += sums(conv_grad)
    out_sums[40:48, :] += sums(decay_grad.astype(F32))
    out_sums[48:56, :] += sums(input_grad.astype(F32))
    out_sums[56:64, :] += sums(expo_grad * decay)

    @pl.when(step == blocks - 1)
    def _():
        out_first[0:8, :] = next_one[...]
        out_first[8:24, :] = next_two[...]
        out_first[24:48, :] = next_three[...]


def recur_backward(
    local, after, enter, hidden, carry, conv_out, decay_sig, gate_sig, retain, same, params, conv_in, decay_w, input_w,
    rows=128,
):
    length, width = local.shape
    last = length // rows - 1
    block = pl.BlockSpec((rows, width), lambda i: (last - i, 0))
    fixed = lambda shape: pl.BlockSpec(shape, lambda i: (0, 0))
    steps = rows // SEGS
    before = pl.BlockSpec((SEGS, width), lambda i: (jnp.maximum((last - i) * steps - 1, 0), 0))
    return pl.pallas_call(
        backward_kernel,
        grid=(length // rows,),
        in_specs=[
            block, block, fixed((SEGS, width)), block, before, fixed((SEGS, width)), block, block, block, block,
            pl.BlockSpec((rows, 8), lambda i: (last - i, 0)),
            fixed((8, width)), block, fixed((width, width)), fixed((width, width)),
        ],
        out_specs=[block, block, block, fixed((48, width)), fixed((64, width))],
        out_shape=[
            jax.ShapeDtypeStruct((length, width), BF),
            jax.ShapeDtypeStruct((length, width), BF),
            jax.ShapeDtypeStruct((length, width), F32),
            jax.ShapeDtypeStruct((48, width), F32),
            jax.ShapeDtypeStruct((64, width), F32),
        ],
        scratch_shapes=[
            pltpu.VMEM((8, width), F32),
            pltpu.VMEM((16, width), F32),
            pltpu.VMEM((24, width), F32),
        ],
        compiler_params=pltpu.CompilerParams(vmem_limit_bytes=LIMIT),
        cost_estimate=pl.CostEstimate(flops=length * width, bytes_accessed=4 * length * width, transcendentals=0),
    )(
        local, after, enter, hidden, hidden, carry, conv_out, decay_sig, gate_sig, retain, same, params, conv_in,
        decay_w, input_w,
    )


def exchange_kernel(count, chunks, mode, *refs):
    backward, summing, gathering = mode in ("back", "last"), mode != "first", mode != "last"
    refs = list(refs)
    take = lambda number: [refs.pop(0) for _ in range(number)]
    if mode == "first":
        residual, gain, out, out_scale, gathered = take(5)
    elif mode == "norm":
        states, products, gates, carry, weight, residual, gain, out, out_scale, out_own, out_hidden, out_gated = take(12)
        (gathered,) = take(1)
    elif mode == "back":
        grads, weight, residual, middle, scale, mean, gain, out, out_own, out_gain = take(10)
        gathered = out
    else:
        grads, weight, residual, middle, scale, mean, gain, small, feed_sums, out_own, out_small, out_gains = take(12)
        out_gain, gain_own, gain_row, gain_seq, small_own, small_row, small_seq = take(7)
        gain_sems, small_sems = take(2)
    if summing:
        partial, held_weight, right, left, total, weight_sem, sum_send, sum_recv = take(8)
    if gathering:
        all_send, all_recv = take(2)
    me = lax.axis_index("rep")
    length, width = residual.shape
    rows = length // chunks
    last = count - 1

    if summing:
        start = weight.shape[1] - held_weight.shape[1] if mode == "norm" else 0
        load = pltpu.make_async_copy(weight.at[:, pl.ds(start, held_weight.shape[1])], held_weight, weight_sem)
        load.start()
    barrier = pltpu.get_barrier_semaphore()
    if gathering:

        @pl.when(me > 0)
        def _():
            pl.semaphore_signal(barrier, inc=1, device_id={"rep": me - 1}, device_id_type=pl.DeviceIdType.MESH)

        @pl.when(me < last)
        def _():
            pl.semaphore_signal(barrier, inc=1, device_id={"rep": me + 1}, device_id_type=pl.DeviceIdType.MESH)

        inner = jnp.logical_and(me > 0, me < last)

        @pl.when(inner)
        def _():
            pl.semaphore_wait(barrier, 2)

        @pl.when(jnp.logical_not(inner))
        def _():
            pl.semaphore_wait(barrier, 1)

    else:
        for axis in ("row", "seq", "rep"):
            for d in range(1, lax.axis_size(axis)):
                peer = lax.rem(lax.axis_index(axis) + d, lax.axis_size(axis))
                pl.semaphore_signal(barrier, inc=1, device_id={axis: peer}, device_id_type=pl.DeviceIdType.MESH)
        pl.semaphore_wait(barrier, sum(lax.axis_size(axis) - 1 for axis in ("row", "seq", "rep")))

    def to_peers(axis, source, target, sems):
        copies = []
        for d in range(1, lax.axis_size(axis)):
            peer = lax.rem(lax.axis_index(axis) + d, lax.axis_size(axis))
            copies.append(
                pltpu.make_async_remote_copy(
                    src_ref=source,
                    dst_ref=target(d),
                    send_sem=sems.at[0, d],
                    recv_sem=sems.at[1, d],
                    device_id={axis: peer},
                    device_id_type=pl.DeviceIdType.MESH,
                )
            )
        return copies

    if mode == "last":
        small_rows = to_peers("row", small_own, lambda d: small_row.at[d], small_sems.at[0])
        small_seqs = to_peers("seq", small_row.at[0], lambda d: small_seq.at[d], small_sems.at[1])
        gain_rows = to_peers("row", gain_own, lambda d: gain_row.at[d], gain_sems.at[0])
        gain_seqs = to_peers("seq", gain_row.at[0], lambda d: gain_seq.at[d], gain_sems.at[1])
        own_gains = out_gains.at[:, pl.ds(pl.multiple_of(me * width, width), width)]
        gain_reps = to_peers("rep", gain_seq.at[0], lambda d: own_gains, gain_sems.at[2])
        small_own[...] = small[...]
        for copy in small_rows:
            copy.start()

    if backward:
        out_gain[...] = jnp.zeros_like(out_gain)
    if summing:
        load.wait()

    def at(c):
        return pl.ds(pl.multiple_of(c * rows, rows), rows)

    def columns(device):
        return pl.ds(pl.multiple_of(device * width, width), width)

    def sum_copy(side, slot, c):
        buffer, to = ((right, me + 1), (left, me - 1))[side]
        return pltpu.make_async_remote_copy(
            src_ref=buffer.at[slot, at(c)],
            dst_ref=buffer.at[slot - 1, at(c)],
            send_sem=sum_send.at[side, slot, c],
            recv_sem=sum_recv.at[side, slot - 1, c],
            device_id={"rep": to},
            device_id_type=pl.DeviceIdType.MESH,
        )

    def sum_arrived(side, slot, c):
        buffer, sender = ((right, me - 1), (left, me + 1))[side]
        pltpu.make_async_remote_copy(
            src_ref=buffer.at[slot, at(c)],
            dst_ref=buffer.at[slot, at(c)],
            send_sem=sum_send.at[side, slot, c],
            recv_sem=sum_recv.at[side, slot, c],
            device_id={"rep": sender},
            device_id_type=pl.DeviceIdType.MESH,
        ).wait_recv()

    def all_copy(side, far, c):
        source, to = ((me - far, me + 1), (me + far, me - 1))[side]
        piece = gathered.at[at(c), columns(source)]
        return pltpu.make_async_remote_copy(
            src_ref=piece,
            dst_ref=piece,
            send_sem=all_send.at[side, far, c],
            recv_sem=all_recv.at[side, far + 1, c],
            device_id={"rep": to},
            device_id_type=pl.DeviceIdType.MESH,
        )

    def all_arrived(side, far, c):
        source, sender = ((me - far, me - 1), (me + far, me + 1))[side]
        piece = gathered.at[at(c), columns(source)]
        pltpu.make_async_remote_copy(
            src_ref=piece,
            dst_ref=piece,
            send_sem=all_send.at[side, far, c],
            recv_sem=all_recv.at[side, far, c],
            device_id={"rep": sender},
            device_id_type=pl.DeviceIdType.MESH,
        ).wait_recv()

    def inside(c):
        return jnp.logical_and(c >= 0, c < chunks)

    stride = 1

    def produce(c):
        some = pl.ds(pl.multiple_of(c * rows, stride * rows), stride * rows)
        if mode == "norm":
            wide = (stride * rows // SEGS, SEGS, carry.shape[1])
            enter = jnp.broadcast_to(carry[...][None], wide).reshape(stride * rows, carry.shape[1])
            hidden = states[some, :] + products[some, :] * enter
            low = (hidden * gates[some, :]).astype(BF)
            out_hidden[some, :] = hidden
            out_gated[some, :] = low
        else:
            low = grads[some, :]
        partial[some, :] = back_dot(low, held_weight[...]).astype(BF)

    def tick(now, _):
        if mode == "last":

            @pl.when(now == chunks - 2)
            def _():
                for copy in small_rows:
                    copy.wait_recv()
                added = small_own[...].astype(F32)
                for d in range(1, lax.axis_size("row")):
                    added = added + small_row[d].astype(F32)
                small_row[0] = added.astype(BF)
                for copy in small_seqs:
                    copy.start()

        if summing:

            @pl.when(jnp.logical_and(now < chunks, lax.rem(now, stride) == 0))
            def _():
                produce(now)

        for side in (0, 1) if summing else ():
            place = (me, last - me)[side]
            c = now - place
            for slot in range(last, 0, -1):

                @pl.when(jnp.logical_and(inside(c), place + slot <= last))
                def _(side=side, place=place, c=c, slot=slot):
                    buffer = (right, left)[side]
                    target = (me + slot, me - slot)[side]

                    @pl.when(place > 0)
                    def _():
                        sum_arrived(side, slot, c)
                        added = buffer[slot, at(c), :].astype(F32) + partial[at(c), columns(target)].astype(F32)
                        buffer[slot, at(c), :] = added.astype(BF)

                    @pl.when(place == 0)
                    def _():
                        buffer[slot, at(c), :] = partial[at(c), columns(target)]

                    sum_copy(side, slot, c).start()

        def finish(done):
            total[...] = partial[at(done), columns(me)].astype(F32)

            @pl.when(me > 0)
            def _():
                sum_arrived(0, 0, done)
                total[...] += right[0, at(done), :].astype(F32)

            @pl.when(me < last)
            def _():
                sum_arrived(1, 0, done)
                total[...] += left[0, at(done), :].astype(F32)

            if backward:
                size = scale[at(done), 0:1]
                normal = middle[at(done), :].astype(F32) * size
                summed = total[...]
                own = residual[at(done), :].astype(F32) + size * (
                    summed * gain[...] - normal * mean[at(done), 0:1]
                )
                out_gain[...] += jnp.sum((summed * normal).reshape(rows // 8, 8, width), axis=0)
            else:
                own = residual[at(done), :].astype(F32) + total[...]
            out_own[at(done), :] = own.astype(out_own.dtype)
            if gathering:
                gathered[at(done), columns(me)] = own.astype(BF)

        done = now - last if summing else now

        @pl.when(inside(done))
        def _():
            if summing:
                finish(done)
            else:
                gathered[at(done), columns(me)] = residual[at(done), :]
            if gathering:

                @pl.when(me < last)
                def _():
                    all_copy(0, 0, done).start()

                @pl.when(me > 0)
                def _():
                    all_copy(1, 0, done).start()

        for far in range(1, count) if gathering else ():
            c = done - far
            for side in (0, 1):
                place = (me, last - me)[side]

                @pl.when(jnp.logical_and(inside(c), place >= far))
                def _(side=side, place=place, c=c, far=far):
                    all_arrived(side, far, c)

                    @pl.when(place < last)
                    def _():
                        all_copy(side, far, c).start()

        if not backward:
            full = done - last

            @pl.when(inside(full))
            def _():
                values = gathered[at(full), :].astype(F32)
                size = lax.rsqrt(jnp.mean(values * values, axis=1, keepdims=True) + eps)
                out[at(full), :] = (values * size * gain[...]).astype(BF)
                out_scale[at(full), :] = jnp.broadcast_to(size, (rows, 128))

        return 0

    lax.fori_loop(0, chunks + last * (summing + gathering), tick, 0)

    def settle(c, _):
        for side in (0, 1):
            place = (me, last - me)[side]
            for slot in range(1, count) if summing else ():

                @pl.when(place + slot <= last)
                def _(side=side, slot=slot):
                    sum_copy(side, slot, c).wait_send()

            for far in range(0, last) if gathering else ():

                @pl.when(jnp.logical_and(place < last, place >= far))
                def _(side=side, far=far):
                    all_copy(side, far, c).wait_send()

        return 0

    if mode == "last":
        mixer_sum = jnp.sum(out_gain[...], axis=0, keepdims=True)
        feed_sum = jnp.sum(feed_sums[...], axis=0, keepdims=True)
        gain_own[...] = jnp.concatenate([mixer_sum, feed_sum, jnp.zeros((6, width), F32)], axis=0)
        for copy in gain_rows:
            copy.start()
        for copy in small_seqs:
            copy.wait_recv()
        added = small_row[0].astype(F32)
        for d in range(1, lax.axis_size("seq")):
            added = added + small_seq[d].astype(F32)
        out_small[...] = added
        for copy in gain_rows:
            copy.wait_recv()
        added = gain_own[...]
        for d in range(1, lax.axis_size("row")):
            added = added + gain_row[d]
        gain_row[0] = added
        for copy in gain_seqs:
            copy.start()
        for copy in gain_seqs:
            copy.wait_recv()
        added = gain_row[0]
        for d in range(1, lax.axis_size("seq")):
            added = added + gain_seq[d]
        gain_seq[0] = added
        for copy in gain_reps:
            copy.start()
        own_gains[...] = added
        for copy in gain_reps:
            copy.wait_recv()
        for copy in small_rows + small_seqs + gain_rows + gain_seqs + gain_reps:
            copy.wait_send()

    lax.fori_loop(0, chunks, settle, 0)


def exchange(mode, operands, width, chunks=16):
    count = lax.axis_size("rep")
    length = operands[0].shape[0]
    features = count * width
    backward, summing, gathering = mode in ("back", "last"), mode != "first", mode != "last"
    vmem = pl.BlockSpec(memory_space=pltpu.VMEM)
    in_specs = [vmem] * len(operands)
    sems = [pltpu.SemaphoreType.DMA((2, count, chunks)), pltpu.SemaphoreType.DMA((2, count, chunks))]
    full, own = jax.ShapeDtypeStruct((length, features), BF), jax.ShapeDtypeStruct((length, width), F32)
    scale, gain = jax.ShapeDtypeStruct((length, 128), F32), jax.ShapeDtypeStruct((8, width), F32)
    if mode == "first":
        out_shape = [full, scale]
    elif mode == "norm":
        hidden = operands[0].shape
        out_shape = [full, scale, own, jax.ShapeDtypeStruct(hidden, F32), jax.ShapeDtypeStruct(hidden, BF)]
    elif mode == "back":
        out_shape = [full, own, gain]
    else:
        small = operands[7].shape
        out_shape = [
            jax.ShapeDtypeStruct((length, width), BF),
            jax.ShapeDtypeStruct(small, F32),
            jax.ShapeDtypeStruct((8, features), F32),
        ]
    scratch = [] if backward else [pltpu.VMEM((length, features), BF)]
    if mode == "last":
        row, seq = lax.axis_size("row"), lax.axis_size("seq")
        most = max(row, seq, count)
        scratch += [
            pltpu.VMEM((8, width), F32),
            pltpu.VMEM((8, width), F32),
            pltpu.VMEM((row, 8, width), F32),
            pltpu.VMEM((seq, 8, width), F32),
            pltpu.VMEM(small, BF),
            pltpu.VMEM((row,) + small, BF),
            pltpu.VMEM((seq,) + small, BF),
            pltpu.SemaphoreType.DMA((3, 2, most)),
            pltpu.SemaphoreType.DMA((2, 2, most)),
        ]
    if summing:
        in_specs[4 if mode == "norm" else 1] = pl.BlockSpec(memory_space=pl.ANY)
        scratch += [
            pltpu.VMEM((length, features), BF),
            pltpu.VMEM((features, operands[0].shape[1]), BF),
            pltpu.VMEM((count, length, width), BF),
            pltpu.VMEM((count, length, width), BF),
            pltpu.VMEM((length // chunks, width), F32),
            pltpu.SemaphoreType.DMA,
        ] + sems
    if gathering:
        scratch += sems
    return pl.pallas_call(
        partial_call(exchange_kernel, count, chunks, mode),
        in_specs=in_specs,
        out_specs=[vmem] * len(out_shape),
        out_shape=out_shape,
        scratch_shapes=scratch,
        compiler_params=pltpu.CompilerParams(
            collective_id=("first", "norm", "back", "last").index(mode), has_side_effects=True, vmem_limit_bytes=LIMIT
        ),
        cost_estimate=pl.CostEstimate(
            flops=10 * length * features, bytes_accessed=160 * length * features, transcendentals=0
        ),
    )(*operands)


def feed_kernel(cot, pre_gate, pre_up, down, out_low, out_grads, out_dot):
    half = out_low.shape[1]
    upstream = jnp.dot(cot[...], down[...], preferred_element_type=F32)
    gate_pre, up_pre = pre_gate[...], pre_up[...]
    value, slope = gelu_both(gate_pre)
    out_low[...] = (value * up_pre).astype(BF)
    gate_grad, up_grad = upstream * up_pre * slope, upstream * value
    out_grads[:, :half] = gate_grad.astype(BF)
    out_grads[:, half:] = up_grad.astype(BF)
    dots = jnp.sum(gate_grad * gate_pre + up_grad * up_pre, axis=1, keepdims=True)
    out_dot[...] = jnp.broadcast_to(dots, out_dot.shape)


def feed_backward(cot, pre, down, rows=256):
    length, features = cot.shape
    half = down.shape[1]
    block = lambda width, column=0: pl.BlockSpec((rows, width), lambda i: (i, column))
    return pl.pallas_call(
        feed_kernel,
        grid=(length // rows,),
        in_specs=[
            block(features), block(half), block(half, 1),
            pl.BlockSpec((features, half), lambda i: (0, 0), pipeline_mode=pl.Buffered(1)),
        ],
        out_specs=[block(half), block(2 * half), block(128)],
        out_shape=[
            jax.ShapeDtypeStruct((length, half), BF),
            jax.ShapeDtypeStruct((length, 2 * half), BF),
            jax.ShapeDtypeStruct((length, 128), F32),
        ],
        compiler_params=pltpu.CompilerParams(vmem_limit_bytes=LIMIT),
        cost_estimate=pl.CostEstimate(
            flops=2 * length * features * half, bytes_accessed=40 * length * half, transcendentals=length * half
        ),
    )(cot, pre, pre, down)


def per_segment(small, length):
    return jnp.broadcast_to(small[None], (length // SEGS,) + small.shape).reshape(length, small.shape[1])


def rows_dot(left, right):
    return lax.dot_general(left, right, (((0,), (0,)), ((), ())), preferred_element_type=F32)


def back_dot(left, right):
    return lax.dot_general(left, right, (((1,), (1,)), ((), ())), preferred_element_type=F32)


def dot(left, right):
    return jnp.dot(left, right, preferred_element_type=F32)


def shards(
    block_input, cotangent, segment_ids, pad_mask, state_init, window_init,
    recur_input, recur_gate, recur_output, feed_gate, feed_up, feed_down,
    conv_kernel, conv_bias, decay_gate, input_gate, decay_bias, input_bias, decay_logit, mixer_gain, feed_gain,
):
    own_width = block_input.shape[2]
    features = mixer_gain.shape[0]
    length = segment_ids.shape[1]
    taps = conv_kernel.shape[0]
    edge = taps - 1
    heads, head_width = decay_gate.shape[0], decay_gate.shape[2]
    rep = lax.axis_index("rep")
    seq, seqs = lax.axis_index("seq"), lax.axis_size("seq")
    at_start = seq == 0
    to_next = [(i, i + 1) for i in range(seqs - 1)]
    to_last = [(i + 1, i) for i in range(seqs - 1)]

    def weights(shard):
        return lax.all_gather(shard, ("seq", "row"), axis=0, tiled=True)

    def spread(partial_grad):
        return lax.psum_scatter(partial_grad, ("seq", "row"), scatter_dimension=0, tiled=True)

    def own_part(vector):
        return lax.dynamic_slice_in_dim(vector, rep * own_width, own_width, 0)[None]

    channels = conv_bias.shape[0]
    spare = -channels % 128

    def wide(values, fill=0):
        return jnp.pad(values, ((0, 0),) * (values.ndim - 1) + ((0, spare),), constant_values=fill)

    width = channels + spare

    x_low = by_step(block_input[0])
    cot_own = by_step(cotangent[0] * pad_mask[0][:, None].astype(BF))
    mixer_own, feed_own = own_part(mixer_gain), own_part(feed_gain)
    normed, s1 = exchange("first", (x_low, mixer_gain[None]), own_width)
    w_recur = weights(jnp.concatenate([wide(recur_input), wide(recur_gate), wide(recur_output)], axis=1))
    cot_own, normed, w_recur = after((cot_own, normed, w_recur))
    cot = lax.all_gather(cot_own, "rep", axis=1, tiled=True)
    w_input, w_output = w_recur[:, : 2 * width], w_recur[:, 2 * width :]

    left_ids = lax.ppermute(segment_ids[:, -edge:].astype(F32), "seq", to_next).astype(jnp.int32)
    left_ids = jnp.where(at_start, jnp.broadcast_to(segment_ids[:, :1], left_ids.shape), left_ids)
    ids_ext = jnp.concatenate([left_ids, segment_ids], axis=1)[0]
    same = [(ids_ext[edge - k : edge - k + length] == segment_ids[0]).astype(F32) for k in range(taps)]
    same = by_step(jnp.stack(same + [same[0]] * (8 - taps), axis=1))

    rate = 8.0 * jax.nn.softplus(decay_logit)
    params = wide(jnp.concatenate([conv_kernel, jnp.stack([conv_bias, decay_bias, input_bias])], axis=0))
    params = jnp.concatenate([params, wide(rate[None], 1)], axis=0)
    decay_w, input_w = block_diagonal(decay_gate, width), block_diagonal(input_gate, width)
    state_init = wide(state_init)

    projected = dot(normed, w_input)
    feed_shard, feed_down, projected = after(
        (jnp.concatenate([feed_gate, feed_up], axis=1), feed_down, projected)
    )
    w_feed = weights(feed_shard)
    w_down = weights(feed_down)
    ends = projected[-edge * SEGS :, :width].astype(BF).reshape(edge, SEGS, width)
    left = lax.ppermute(ends[:, -1], "seq", to_next)
    left = jnp.where(at_start, wide(window_init[0]), left)
    prefix = jnp.concatenate([left[:, None], ends[:, :-1]], axis=1).reshape(edge * SEGS, -1)
    block_windows = ends[:, -1, :channels]

    gates, conv_out, decay_sig, gate_sig, retain, products, states, pre_a, pre_b, total = recur_forward(
        projected, same, prefix, params, decay_w, input_w
    )
    state_in = state_init
    for k in range(1, seqs):
        arriving = lax.ppermute(total[0:1] * state_in + total[1:2], "seq", to_next)
        state_in = jnp.where(seq == k, arriving, state_in)
    block_states = total[0:1] * state_in + total[1:2]
    carry = pre_a * state_in + pre_b

    normed_mid, s2, middle, hidden, gated = exchange(
        "norm", (states, products, gates, carry, w_recur, x_low, feed_gain[None]), own_width
    )
    normed_mid, cot = after((normed_mid, cot))
    pre = dot(normed_mid, w_feed)
    feed_low, feed_grads, mid_mean = feed_backward(cot, pre, w_down)
    mid_mean = small_sum(mid_mean[:, 0].reshape(8, -1), "rep").reshape(-1, 1) / features

    half = w_down.shape[1]
    feed_part = back_dot(feed_low, w_down).astype(BF)
    feed_low, feed_part = after((feed_low, feed_part))
    down_grad = rows_dot(cot, feed_low).astype(BF)
    feed_grads, down_grad, mid_mean = after((feed_grads, down_grad, mid_mean))
    feed_all = rows_dot(normed_mid, feed_grads).astype(BF)
    feed_grads, feed_all = after((feed_grads, feed_all))
    down_grad, feed_all = spread(down_grad), spread(feed_all)
    middle_low, middle_grad, feed_gain_own = exchange(
        "back",
        (feed_grads, w_feed, cot_own, middle, s2, jnp.broadcast_to(mid_mean, (length, 128)), feed_own),
        own_width,
    )

    feed_part, middle_low = after((feed_part, middle_low))
    feed_out = lax.psum_scatter(feed_part, "rep", scatter_dimension=1, tiled=True)
    gated_grad = dot(middle_low, w_output)
    local, after_prod, branch_grad, enter_a, enter_b, back_total, branch_dot = recur_adjoint(
        gated_grad, projected, hidden, retain
    )
    output_all = rows_dot(middle_low, gated).astype(BF)
    entering = jnp.zeros_like(state_init)
    for k in range(1, seqs):
        arriving = lax.ppermute(back_total[0:1] * entering + back_total[1:2], "seq", to_last)
        entering = jnp.where(seq == seqs - 1 - k, arriving, entering)
    enter = enter_a * entering + enter_b
    decay_grad, input_grad_low, low_grad, first, sums = recur_backward(
        local, after_prod, enter, hidden, carry, conv_out, decay_sig, gate_sig, retain, same, params, projected,
        decay_w, input_w,
    )
    owed = [first[0:8], first[8:24], first[24:48]]
    owed = [o.reshape(k + 1, SEGS, -1) for k, o in enumerate(owed)]
    ahead = prefix.reshape(edge, SEGS, -1).astype(F32)
    back_share = jnp.zeros_like(ahead)
    tap_extra = [jnp.zeros((width,), F32)]
    for k in range(1, taps):
        term = jnp.pad(owed[k - 1], ((edge - k, 0), (0, 0), (0, 0)))
        tap_extra.append(jnp.sum(term * ahead, axis=(0, 1)))
        back_share = back_share + params[k] * term
    from_right = lax.ppermute(back_share[:, 0], "seq", to_last)
    share = jnp.concatenate([back_share[:, 1:], from_right[:, None]], axis=1)
    low_grad = low_grad.reshape(length // SEGS, SEGS, -1)
    low_grad = jnp.concatenate([low_grad[:-edge], low_grad[-edge:] + share], axis=0).reshape(length, -1)
    in_mean = jnp.sum(low_grad * projected[:, :width].astype(BF).astype(F32), axis=1) + branch_dot[:, 0]
    in_mean = small_sum(in_mean.reshape(8, -1), "rep").reshape(-1, 1) / features

    both_grads = jnp.concatenate([low_grad.astype(BF), branch_grad], axis=1)
    both_grads, in_mean, down_grad, feed_all = after((both_grads, in_mean, down_grad, feed_all))
    feed_down_grad = down_grad.astype(F32)
    feed_gate_grad, feed_up_grad = feed_all[:, :half].astype(F32), feed_all[:, half:].astype(F32)
    conv_low = conv_out.astype(BF)
    decay_gate_grad = diagonal_rows(rows_dot(conv_low, decay_grad), heads, head_width)
    input_gate_grad = diagonal_rows(rows_dot(conv_low, input_grad_low), heads, head_width)
    sums = jnp.sum(sums.reshape(8, 8, -1), axis=1)
    conv_kernel_grad = sums[:taps] + jnp.stack(tap_extra)
    logit_grad = sums[7:, :channels] * 8.0 * jax.nn.sigmoid(decay_logit)
    vectors = jnp.concatenate([conv_kernel_grad, sums[4:7]], axis=0)[:, :channels]
    vectors = jnp.concatenate([vectors, logit_grad], axis=0)
    parts = (decay_gate_grad, input_gate_grad, vectors)
    small, counts = join_small(parts)
    recur_raw = rows_dot(normed, both_grads).astype(BF)
    both_grads, recur_raw, output_all, feed_out = after((both_grads, recur_raw, output_all, feed_out))
    output_all, recur_all = spread(output_all), spread(recur_raw)
    input_grad, summed, gains = exchange(
        "last",
        (
            both_grads, w_recur, middle_grad, x_low, s1, jnp.broadcast_to(in_mean, (length, 128)), mixer_own,
            small, feed_gain_own,
        ),
        own_width,
    )
    input_grad, feed_out, recur_all, output_all = after((input_grad, feed_out, recur_all, output_all))
    recur_output_grad = output_all[:, :channels].astype(F32)
    recur_input_grad = recur_all[:, :channels].astype(F32)
    recur_gate_grad = recur_all[:, width : width + channels].astype(F32)
    input_grad = by_segment(input_grad)[None]
    block_output = by_segment((middle + feed_out.astype(F32)).astype(BF))[None]
    decay_gate_grad, input_gate_grad, vectors = split_small(summed, counts, parts)
    decay_gate_grad, input_gate_grad = (
        g[:, :head_width].reshape(decay_gate.shape) for g in (decay_gate_grad, input_gate_grad)
    )
    return (
        block_output, block_states[:, None, :channels], block_windows[None, None], input_grad,
        recur_input_grad, recur_gate_grad, recur_output_grad, feed_gate_grad, feed_up_grad, feed_down_grad,
        vectors[:taps], vectors[4], decay_gate_grad, input_gate_grad, vectors[5], vectors[6], vectors[7],
        gains[0], gains[1],
    )


def solution(mesh):
    tokens = P("row", "seq", "rep")
    matrix = P(("seq", "row"), "rep")
    in_specs = (
        tokens, tokens, P("row", "seq"), P("row", "seq"), P("row", "rep"), P("row", None, "rep"),
        matrix, matrix, matrix, matrix, matrix, matrix,
        P(None, "rep"), P("rep"), P("rep", None, None), P("rep", None, None), P("rep"), P("rep"), P("rep"), P(), P(),
    )
    out_specs = (
        tokens, tokens, P("row", "seq", None, "rep"), tokens,
        matrix, matrix, matrix, matrix, matrix, matrix,
        P(None, "rep"), P("rep"), P("rep", None, None), P("rep", None, None), P("rep"), P("rep"), P("rep"), P(), P(),
    )
    return jax.shard_map(shards, mesh=mesh, in_specs=in_specs, out_specs=out_specs, check_vma=False)
```

```python
from functools import partial as partial_call

import jax
import jax.numpy as jnp
from jax import lax
from jax.experimental import pallas as pl
from jax.experimental.pallas import tpu as pltpu
from jax.sharding import PartitionSpec as P

eps = 1e-06
SEGS = 8
BF = jnp.bfloat16
F32 = jnp.float32
LIMIT = 48 * 1024 * 1024


def gelu(v):
    return 0.5 * v * (1.0 + jnp.tanh(0.7978845608 * (v + 0.044715 * v * v * v)))


def gelu_both(v):
    square = v * v
    t = jnp.tanh(0.7978845608 * v * (1.0 + 0.044715 * square))
    value = 0.5 * v * (1.0 + t)
    slope = 0.5 * (1.0 + t) + 0.5 * v * (1.0 - t * t) * 0.7978845608 * (1.0 + 3 * 0.044715 * square)
    return value, slope


def one_minus_exp(y):
    series = y * (1 - y / 2 * (1 - y / 3 * (1 - y / 4 * (1 - y / 5 * (1 - y / 6 * (1 - y / 7))))))
    return jnp.where(y < 0.4, series, 1.0 - jnp.exp(-y))


after = lax.optimization_barrier


def small_sum(own, axis):
    count = lax.axis_size(axis)
    total = own
    for k in range(1, count):
        total = total + lax.ppermute(own, axis, [(i, (i + k) % count) for i in range(count)])
    return total


def small_gather(own, axis):
    count, me = lax.axis_size(axis), lax.axis_index(axis)
    width = own.shape[1]
    total = lax.dynamic_update_slice(jnp.zeros((own.shape[0], count * width), own.dtype), own, (0, me * width))
    for k in range(1, count):
        piece = lax.ppermute(own, axis, [(i, (i + k) % count) for i in range(count)])
        total = lax.dynamic_update_slice(total, piece, (0, lax.rem(me - k + count, count) * width))
    return total


def join_small(parts):
    width = 256
    padded = []
    for part in parts:
        columns = -part.shape[1] % width
        padded.append(jnp.pad(part, ((0, 0), (0, columns))).reshape(-1, width))
    counts = [p.shape[0] for p in padded]
    spare = jnp.zeros((-sum(counts) % 16, width), F32)
    return jnp.concatenate(padded + [spare], axis=0).astype(BF), counts


def split_small(joined, counts, parts):
    out, start = [], 0
    for part, rows in zip(parts, counts):
        out.append(joined[start : start + rows].reshape(part.shape[0], -1)[:, : part.shape[1]])
        start += rows
    return out


def by_step(values):
    length, width = values.shape
    return values.reshape(SEGS, length // SEGS, width).transpose(1, 0, 2).reshape(length, width)


def by_segment(values):
    length, width = values.shape
    return values.reshape(length // SEGS, SEGS, width).transpose(1, 0, 2).reshape(length, width)


def block_diagonal(blocks, width):
    heads, wide = blocks.shape[0], blocks.shape[1]
    rows = [jnp.pad(blocks[h], ((0, 0), (h * wide, width - (h + 1) * wide))) for h in range(heads)]
    rows.append(jnp.zeros((width - heads * wide, width), blocks.dtype))
    return jnp.concatenate(rows, axis=0)


def diagonal_rows(dense, heads, wide):
    blocks = [dense[h * wide : (h + 1) * wide, h * wide : (h + 1) * wide] for h in range(heads)]
    return jnp.concatenate(blocks, axis=0)


def forward_kernel(
    conv_in, gate_branch, same, prefix, params, decay_w, input_w,
    out_gelu, out_conv, out_decay, out_gate, out_retain, out_prod, out_state, out_pre_a, out_pre_b, out_total,
    last_rows, prod_now, state_now, inflow_s,
):
    step = pl.program_id(0)
    rows = conv_in.shape[0]

    @pl.when(step == 0)
    def _():
        last_rows[...] = prefix[...].astype(F32)
        prod_now[...] = jnp.ones_like(prod_now)
        state_now[...] = jnp.zeros_like(state_now)

    out_gelu[...] = gelu(gate_branch[...])
    now = conv_in[...].astype(BF).astype(F32)
    ext = jnp.concatenate([last_rows[...], now], axis=0)
    same_all = same[...]
    total = params[4:5, :] + params[0:1, :] * now
    for k in (1, 2, 3):
        start = 24 - 8 * k
        total = total + params[k : k + 1, :] * ext[start : start + rows] * same_all[:, k : k + 1]
    last_rows[...] = now[rows - 24 :]
    out_conv[...] = total
    low = total.astype(BF)
    decay_sig = jax.nn.sigmoid(jnp.dot(low, decay_w[...], preferred_element_type=F32) + params[5:6, :])
    gate_sig = jax.nn.sigmoid(jnp.dot(low, input_w[...], preferred_element_type=F32) + params[6:7, :])
    out_decay[...] = decay_sig
    out_gate[...] = gate_sig
    expo = params[7:8, :] * decay_sig
    out_retain[...] = same_all[:, 1:2] * jnp.exp(-expo)
    inflow_s[...] = jnp.sqrt(one_minus_exp(2.0 * expo)) * gate_sig * total
    prod, state = prod_now[...], state_now[...]
    for t in range(rows // SEGS):
        at = slice(t * SEGS, (t + 1) * SEGS)
        keep = out_retain[at, :]
        prod = prod * keep
        state = state * keep + inflow_s[at, :]
        out_prod[at, :] = prod
        out_state[at, :] = state
    prod_now[...] = prod
    state_now[...] = state

    @pl.when(step == pl.num_programs(0) - 1)
    def _():
        carry_a = jnp.ones_like(prod[0:1])
        carry_b = jnp.zeros_like(carry_a)
        for s in range(SEGS):
            out_pre_a[s : s + 1, :] = carry_a
            out_pre_b[s : s + 1, :] = carry_b
            carry_b = prod[s : s + 1] * carry_b + state[s : s + 1]
            carry_a = prod[s : s + 1] * carry_a
        out_total[0:1, :] = carry_a
        out_total[1:2, :] = carry_b
        out_total[2:8, :] = jnp.zeros((6, carry_a.shape[1]), F32)


def recur_forward(conv_in, same, prefix, params, decay_w, input_w, rows=256):
    length, width = conv_in.shape[0], params.shape[1]
    block = pl.BlockSpec((rows, width), lambda i: (i, 0))
    fixed = lambda shape: pl.BlockSpec(shape, lambda i: (0, 0))
    big = jax.ShapeDtypeStruct((length, width), F32)
    small = jax.ShapeDtypeStruct((SEGS, width), F32)
    return pl.pallas_call(
        forward_kernel,
        grid=(length // rows,),
        in_specs=[
            block,
            pl.BlockSpec((rows, width), lambda i: (i, 1)),
            pl.BlockSpec((rows, 8), lambda i: (i, 0)),
            fixed((24, width)),
            fixed((8, width)),
            fixed((width, width)),
            fixed((width, width)),
        ],
        out_specs=[block] * 7 + [fixed((SEGS, width))] * 3,
        out_shape=[big] * 7 + [small] * 3,
        scratch_shapes=[
            pltpu.VMEM((24, width), F32),
            pltpu.VMEM((SEGS, width), F32),
            pltpu.VMEM((SEGS, width), F32),
            pltpu.VMEM((rows, width), F32),
        ],
        compiler_params=pltpu.CompilerParams(vmem_limit_bytes=LIMIT),
        cost_estimate=pl.CostEstimate(flops=length * width, bytes_accessed=4 * length * width, transcendentals=0),
    )(conv_in, conv_in, same, prefix, params, decay_w, input_w)


def adjoint_kernel(
    middle_low, weight, gate_branch, hidden, retain,
    out_local, out_after, out_branch, out_pre_a, out_pre_b, out_total, out_dot,
    local_now, after_now, next_retain, grad_s,
):
    step = pl.program_id(0)
    rows = hidden.shape[0]

    @pl.when(step == 0)
    def _():
        local_now[...] = jnp.zeros_like(local_now)
        after_now[...] = jnp.ones_like(after_now)
        next_retain[...] = jnp.ones_like(next_retain)

    value, slope = gelu_both(gate_branch[...])
    upstream = jnp.dot(middle_low[...], weight[...], preferred_element_type=F32)
    grad_s[...] = upstream * value
    branch = upstream * hidden[...] * slope
    out_branch[...] = branch.astype(BF)
    out_dot[...] = jnp.broadcast_to(jnp.sum(branch * gate_branch[...], axis=1, keepdims=True), out_dot.shape)
    local, after, keep = local_now[...], after_now[...], next_retain[...]
    for t in reversed(range(rows // SEGS)):
        at = slice(t * SEGS, (t + 1) * SEGS)
        local = grad_s[at, :] + keep * local
        after = keep * after
        out_local[at, :] = local
        out_after[at, :] = after
        keep = retain[at, :]
    local_now[...] = local
    after_now[...] = after
    next_retain[...] = keep

    @pl.when(step == pl.num_programs(0) - 1)
    def _():
        carry_a = jnp.ones_like(local[0:1])
        carry_b = jnp.zeros_like(carry_a)
        for s in reversed(range(SEGS)):
            out_pre_a[s : s + 1, :] = carry_a
            out_pre_b[s : s + 1, :] = carry_b
            carry_b = keep[s : s + 1] * (local[s : s + 1] + after[s : s + 1] * carry_b)
            carry_a = keep[s : s + 1] * after[s : s + 1] * carry_a
        out_total[0:1, :] = carry_a
        out_total[1:2, :] = carry_b
        out_total[2:8, :] = jnp.zeros((6, carry_a.shape[1]), F32)


def recur_adjoint(middle_low, w_recur, gate_branch, hidden, retain, rows=256):
    length, width = hidden.shape
    features = middle_low.shape[1]
    last = length // rows - 1
    block = pl.BlockSpec((rows, width), lambda i: (last - i, 0))
    second = pl.BlockSpec((rows, width), lambda i: (last - i, 1))
    fixed = lambda shape: pl.BlockSpec(shape, lambda i: (0, 0))
    big = jax.ShapeDtypeStruct((length, width), F32)
    small = jax.ShapeDtypeStruct((SEGS, width), F32)
    return pl.pallas_call(
        adjoint_kernel,
        grid=(length // rows,),
        in_specs=[
            pl.BlockSpec((rows, features), lambda i: (last - i, 0)),
            pl.BlockSpec((features, width), lambda i: (0, 2), pipeline_mode=pl.Buffered(1)),
            second, block, block,
        ],
        out_specs=[block] * 3 + [fixed((SEGS, width))] * 3 + [pl.BlockSpec((rows, 128), lambda i: (last - i, 0))],
        out_shape=[big, big, jax.ShapeDtypeStruct((length, width), BF)]
        + [small] * 3
        + [jax.ShapeDtypeStruct((length, 128), F32)],
        scratch_shapes=[pltpu.VMEM((SEGS, width), F32)] * 3 + [pltpu.VMEM((rows, width), F32)],
        compiler_params=pltpu.CompilerParams(vmem_limit_bytes=LIMIT),
        cost_estimate=pl.CostEstimate(flops=length * width, bytes_accessed=4 * length * width, transcendentals=0),
    )(middle_low, w_recur, gate_branch, hidden, retain)


def backward_kernel(
    local, after, enter, hidden, hidden_before, carry, conv_out, decay_sig, gate_sig, retain, same, params, conv_in,
    decay_w, input_w,
    out_decay, out_input, out_low, out_dot, out_first, out_sums,
    next_one, next_two, next_three,
):
    step = pl.program_id(0)
    blocks = pl.num_programs(0)
    rows = local.shape[0]
    width = local.shape[1]

    @pl.when(step == 0)
    def _():
        for held in (next_one, next_two, next_three):
            held[...] = jnp.zeros_like(held)
        out_sums[...] = jnp.zeros_like(out_sums)

    def per_step(small):
        return jnp.broadcast_to(small[None], (rows // SEGS, SEGS, width)).reshape(rows, width)

    def sums(values):
        return jnp.sum(values.reshape(rows // SEGS, SEGS, width), axis=0)

    adjoint = local[...] + after[...] * per_step(enter[...])
    ahead = jnp.where(step == blocks - 1, carry[...], hidden_before[...])
    hidden_prev = jnp.concatenate([ahead, hidden[...][: rows - SEGS]], axis=0)
    conv, decay, gate = conv_out[...], decay_sig[...], gate_sig[...]
    rate = params[7:8, :]
    expo = rate * decay
    inner = one_minus_exp(2.0 * expo)
    root = jnp.sqrt(inner)
    expo_grad = adjoint * (gate * conv * (1.0 - inner) / root - retain[...] * hidden_prev)
    decay_grad = (expo_grad * rate * decay * (1.0 - decay)).astype(BF)
    input_grad = (adjoint * root * conv * gate * (1.0 - gate)).astype(BF)
    out_decay[...] = decay_grad
    out_input[...] = input_grad
    dims = (((1,), (1,)), ((), ()))
    conv_grad = (
        adjoint * root * gate
        + lax.dot_general(decay_grad, decay_w[...], dims, preferred_element_type=F32)
        + lax.dot_general(input_grad, input_w[...], dims, preferred_element_type=F32)
    )
    same_all = same[...]
    now = conv_in[...].astype(BF).astype(F32)
    low = params[0:1, :] * conv_grad
    out_sums[0:8, :] += sums(conv_grad * now)
    for k, held in ((1, next_one), (2, next_two), (3, next_three)):
        masked = conv_grad * same_all[:, k : k + 1]
        moved = jnp.concatenate([masked[8 * k :], held[...]], axis=0)
        held[...] = masked[: 8 * k]
        low = low + params[k : k + 1, :] * moved
        out_sums[8 * k : 8 * k + 8, :] += sums(moved * now)
    out_low[...] = low
    out_dot[...] = jnp.broadcast_to(jnp.sum(low * now, axis=1, keepdims=True), out_dot.shape)
    out_sums[32:40, :] += sums(conv_grad)
    out_sums[40:48, :] += sums(decay_grad.astype(F32))
    out_sums[48:56, :] += sums(input_grad.astype(F32))
    out_sums[56:64, :] += sums(expo_grad * decay)

    @pl.when(step == blocks - 1)
    def _():
        out_first[0:8, :] = next_one[...]
        out_first[8:24, :] = next_two[...]
        out_first[24:48, :] = next_three[...]


def recur_backward(
    local, after, enter, hidden, carry, conv_out, decay_sig, gate_sig, retain, same, params, conv_in, decay_w, input_w,
    rows=256,
):
    length, width = local.shape
    last = length // rows - 1
    block = pl.BlockSpec((rows, width), lambda i: (last - i, 0))
    fixed = lambda shape: pl.BlockSpec(shape, lambda i: (0, 0))
    steps = rows // SEGS
    before = pl.BlockSpec((SEGS, width), lambda i: (jnp.maximum((last - i) * steps - 1, 0), 0))
    return pl.pallas_call(
        backward_kernel,
        grid=(length // rows,),
        in_specs=[
            block, block, fixed((SEGS, width)), block, before, fixed((SEGS, width)), block, block, block, block,
            pl.BlockSpec((rows, 8), lambda i: (last - i, 0)),
            fixed((8, width)), block, fixed((width, width)), fixed((width, width)),
        ],
        out_specs=[
            block, block, block, pl.BlockSpec((rows, 128), lambda i: (last - i, 0)), fixed((48, width)),
            fixed((64, width)),
        ],
        out_shape=[
            jax.ShapeDtypeStruct((length, width), BF),
            jax.ShapeDtypeStruct((length, width), BF),
            jax.ShapeDtypeStruct((length, width), F32),
            jax.ShapeDtypeStruct((length, 128), F32),
            jax.ShapeDtypeStruct((48, width), F32),
            jax.ShapeDtypeStruct((64, width), F32),
        ],
        scratch_shapes=[
            pltpu.VMEM((8, width), F32),
            pltpu.VMEM((16, width), F32),
            pltpu.VMEM((24, width), F32),
        ],
        compiler_params=pltpu.CompilerParams(vmem_limit_bytes=LIMIT),
        cost_estimate=pl.CostEstimate(flops=length * width, bytes_accessed=4 * length * width, transcendentals=0),
    )(
        local, after, enter, hidden, hidden, carry, conv_out, decay_sig, gate_sig, retain, same, params, conv_in,
        decay_w, input_w,
    )


class Halving:
    def __init__(self, source, keep, arrivals, sends, receives, loads):
        self.source, self.keep, self.arrivals = source, keep, arrivals
        self.sends, self.receives, self.loads = sends, receives, loads
        rows, seqs = lax.axis_size("row"), lax.axis_size("seq")
        self.total = rows * seqs
        self.place = lax.axis_index("seq") * rows + lax.axis_index("row")
        self.stages = halving_stages()
        self.height = source.shape[0] // self.total

    def own_bit(self, p):
        axis, step = self.stages[p]
        return lax.rem(lax.axis_index(axis) // step, 2)

    def block(self, p, mine, j):
        bit = self.own_bit(p) if mine else 1 - self.own_bit(p)
        return lax.rem(self.place, 2**p) + bit * 2**p + j * 2 ** (p + 1)

    def many(self, p):
        return self.total // 2 ** (p + 1)

    def held(self, p, mine, j):
        return self.keep.at[self.block(p, mine, j) // 2]

    def rows_of(self, block):
        return self.source.at[pl.ds(pl.multiple_of(block * self.height, self.height), self.height)]

    def moves(self, p):
        axis, step = self.stages[p]
        partner = lax.axis_index(axis) + step - 2 * step * self.own_bit(p)
        start = self.total - self.total // 2**p
        copies = []
        for j in range(self.many(p)):
            copies.append(
                pltpu.make_async_remote_copy(
                    src_ref=self.held(p, False, j) if p else self.rows_of(self.block(0, False, j)),
                    dst_ref=self.arrivals.at[start + j],
                    send_sem=self.sends.at[start + j],
                    recv_sem=self.receives.at[start + j],
                    device_id={axis: partner},
                    device_id_type=pl.DeviceIdType.MESH,
                )
            )
        return copies

    def local(self):
        return [
            pltpu.make_async_copy(self.rows_of(self.block(0, True, j)), self.keep.at[j], self.loads.at[j])
            for j in range(self.many(0))
        ]

    def begin(self):
        for copy in self.moves(0) + self.local():
            copy.start()

    def stage(self, p, out=None):
        if p == 0:
            for copy in self.local():
                copy.wait()
        for copy in self.moves(p):
            copy.wait_recv()
        start = self.total - self.total // 2**p
        piece = 32
        for j in range(self.many(p)):
            slot = self.block(p, True, j) // 2

            def add(i, _, j=j, slot=slot):
                at = pl.ds(pl.multiple_of(i * piece, piece), piece)
                added = self.keep[slot, at, :].astype(F32) + self.arrivals[start + j, at, :].astype(F32)
                if out is None:
                    self.keep[slot, at, :] = added.astype(BF)
                else:
                    out[at, :] = added
                return 0

            lax.fori_loop(0, self.height // piece, add, 0)
        if out is None:
            for copy in self.moves(p + 1):
                copy.start()

    def settle(self):
        for p in range(len(self.stages)):
            for copy in self.moves(p):
                copy.wait_send()

    def partners(self):
        found = []
        for p, (axis, step) in enumerate(self.stages):
            found.append({axis: lax.axis_index(axis) + step - 2 * step * self.own_bit(p)})
        return found


def halving_stages():
    stages = []
    for axis in ("row", "seq"):
        step = 1
        while step < lax.axis_size(axis):
            stages.append((axis, step))
            step *= 2
    return stages


def halving_scratch(shape):
    total = lax.axis_size("row") * lax.axis_size("seq")
    height = shape[0] // total
    return [
        pltpu.VMEM((total // 2, height, shape[1]), BF),
        pltpu.VMEM((total - 1, height, shape[1]), BF),
        pltpu.SemaphoreType.DMA((total - 1,)),
        pltpu.SemaphoreType.DMA((total - 1,)),
        pltpu.SemaphoreType.DMA((total // 2,)),
    ]


def exchange_kernel(count, chunks, mode, *refs):
    backward, summing, gathering = mode in ("back", "last"), mode != "first", mode != "last"
    refs = list(refs)
    take = lambda number: [refs.pop(0) for _ in range(number)]
    if mode == "first":
        residual, gain, out, out_scale, gathered = take(5)
    elif mode == "norm":
        states, products, gates, carry, weight, residual, gain, out, out_scale, out_own, out_hidden, out_gated = take(12)
        (gathered,) = take(1)
    elif mode == "back":
        grads, weight, residual, middle, scale, mean, gain, spread_in, out, out_own, out_gain, out_spread = take(12)
        gathered = out
        halving = Halving(spread_in, *take(5))
    else:
        grads, weight, residual, middle, scale, mean, gain, small, feed_sums, spread_in = take(10)
        out_own, out_small, out_gains, out_spread = take(4)
        halving = Halving(spread_in, *take(5))
        out_gain, gain_own, gain_row, gain_seq, small_held, small_got, gain_sems, small_sems = take(8)
    if summing:
        partial, held_weight, right, left, total, weight_sem, sum_send, sum_recv = take(8)
    if gathering:
        all_send, all_recv = take(2)
    me = lax.axis_index("rep")
    length, width = residual.shape
    rows = length // chunks
    last = count - 1

    if summing:
        start = weight.shape[1] - held_weight.shape[1] if mode == "norm" else 0
        load = pltpu.make_async_copy(weight.at[:, pl.ds(start, held_weight.shape[1])], held_weight, weight_sem)
        load.start()
    barrier = pltpu.get_barrier_semaphore()
    if gathering:
        partners = halving.partners() if mode == "back" else []
        for partner in partners:
            pl.semaphore_signal(barrier, inc=1, device_id=partner, device_id_type=pl.DeviceIdType.MESH)

        @pl.when(me > 0)
        def _():
            pl.semaphore_signal(barrier, inc=1, device_id={"rep": me - 1}, device_id_type=pl.DeviceIdType.MESH)

        @pl.when(me < last)
        def _():
            pl.semaphore_signal(barrier, inc=1, device_id={"rep": me + 1}, device_id_type=pl.DeviceIdType.MESH)

        inner = jnp.logical_and(me > 0, me < last)

        @pl.when(inner)
        def _():
            pl.semaphore_wait(barrier, 2 + len(partners))

        @pl.when(jnp.logical_not(inner))
        def _():
            pl.semaphore_wait(barrier, 1 + len(partners))

        if mode == "back":
            halving.begin()

    else:
        for axis in ("row", "seq", "rep"):
            for d in range(1, lax.axis_size(axis)):
                peer = lax.rem(lax.axis_index(axis) + d, lax.axis_size(axis))
                pl.semaphore_signal(barrier, inc=1, device_id={axis: peer}, device_id_type=pl.DeviceIdType.MESH)
        pl.semaphore_wait(barrier, sum(lax.axis_size(axis) - 1 for axis in ("row", "seq", "rep")))

    def to_peers(axis, source, target, sems):
        copies = []
        for d in range(1, lax.axis_size(axis)):
            peer = lax.rem(lax.axis_index(axis) + d, lax.axis_size(axis))
            copies.append(
                pltpu.make_async_remote_copy(
                    src_ref=source,
                    dst_ref=target(d),
                    send_sem=sems.at[0, d],
                    recv_sem=sems.at[1, d],
                    device_id={axis: peer},
                    device_id_type=pl.DeviceIdType.MESH,
                )
            )
        return copies

    if mode == "last":
        small_moves = [
            pltpu.make_async_remote_copy(
                src_ref=small_held.at[p],
                dst_ref=small_got.at[p],
                send_sem=small_sems.at[0, p],
                recv_sem=small_sems.at[1, p],
                device_id=partner,
                device_id_type=pl.DeviceIdType.MESH,
            )
            for p, partner in enumerate(halving.partners())
        ]
        gain_rows = to_peers("row", gain_own, lambda d: gain_row.at[d], gain_sems.at[0])
        gain_seqs = to_peers("seq", gain_row.at[0], lambda d: gain_seq.at[d], gain_sems.at[1])
        own_gains = out_gains.at[:, pl.ds(pl.multiple_of(me * width, width), width)]
        gain_reps = to_peers("rep", gain_seq.at[0], lambda d: own_gains, gain_sems.at[2])
        small_held[0] = small[...]
        small_moves[0].start()
        halving.begin()

    def small_stage(p):
        small_moves[p].wait_recv()
        added = small_held[p].astype(F32) + small_got[p].astype(F32)
        if p + 1 < len(small_moves):
            small_held[p + 1] = added.astype(BF)
            small_moves[p + 1].start()
        else:
            out_small[...] = added

    if backward:
        out_gain[...] = jnp.zeros_like(out_gain)
    if summing:
        load.wait()

    def at(c):
        return pl.ds(pl.multiple_of(c * rows, rows), rows)

    def columns(device):
        return pl.ds(pl.multiple_of(device * width, width), width)

    def sum_copy(side, slot, c):
        buffer, to = ((right, me + 1), (left, me - 1))[side]
        return pltpu.make_async_remote_copy(
            src_ref=buffer.at[slot, at(c)],
            dst_ref=buffer.at[slot - 1, at(c)],
            send_sem=sum_send.at[side, slot, c],
            recv_sem=sum_recv.at[side, slot - 1, c],
            device_id={"rep": to},
            device_id_type=pl.DeviceIdType.MESH,
        )

    def sum_arrived(side, slot, c):
        buffer, sender = ((right, me - 1), (left, me + 1))[side]
        pltpu.make_async_remote_copy(
            src_ref=buffer.at[slot, at(c)],
            dst_ref=buffer.at[slot, at(c)],
            send_sem=sum_send.at[side, slot, c],
            recv_sem=sum_recv.at[side, slot, c],
            device_id={"rep": sender},
            device_id_type=pl.DeviceIdType.MESH,
        ).wait_recv()

    def all_copy(side, far, c):
        source, to = ((me - far, me + 1), (me + far, me - 1))[side]
        piece = gathered.at[at(c), columns(source)]
        return pltpu.make_async_remote_copy(
            src_ref=piece,
            dst_ref=piece,
            send_sem=all_send.at[side, far, c],
            recv_sem=all_recv.at[side, far + 1, c],
            device_id={"rep": to},
            device_id_type=pl.DeviceIdType.MESH,
        )

    def all_arrived(side, far, c):
        source, sender = ((me - far, me - 1), (me + far, me + 1))[side]
        piece = gathered.at[at(c), columns(source)]
        pltpu.make_async_remote_copy(
            src_ref=piece,
            dst_ref=piece,
            send_sem=all_send.at[side, far, c],
            recv_sem=all_recv.at[side, far, c],
            device_id={"rep": sender},
            device_id_type=pl.DeviceIdType.MESH,
        ).wait_recv()

    def inside(c):
        return jnp.logical_and(c >= 0, c < chunks)

    stride = 1

    def produce(c):
        some = pl.ds(pl.multiple_of(c * rows, stride * rows), stride * rows)
        if mode == "norm":
            wide = (stride * rows // SEGS, SEGS, carry.shape[1])
            enter = jnp.broadcast_to(carry[...][None], wide).reshape(stride * rows, carry.shape[1])
            hidden = states[some, :] + products[some, :] * enter
            low = (hidden * gates[some, :]).astype(BF)
            out_hidden[some, :] = hidden
            out_gated[some, :] = low
        else:
            low = grads[some, :]
        partial[some, :] = back_dot(low, held_weight[...]).astype(BF)

    def tick(now, _):
        if backward:
            for p, when in ((0, 2), (1, 15 if mode == "back" else 13)):
                if p < len(halving.stages) - 1:

                    @pl.when(now == when)
                    def _(p=p):
                        halving.stage(p)

        if mode == "last":
            for p, when in ((0, 1), (1, 8)):
                if p < len(small_moves) - 1:

                    @pl.when(now == when)
                    def _(p=p):
                        small_stage(p)

        if summing:

            @pl.when(jnp.logical_and(now < chunks, lax.rem(now, stride) == 0))
            def _():
                produce(now)

        for side in (0, 1) if summing else ():
            place = (me, last - me)[side]
            c = now - place
            for slot in range(last, 0, -1):

                @pl.when(jnp.logical_and(inside(c), place + slot <= last))
                def _(side=side, place=place, c=c, slot=slot):
                    buffer = (right, left)[side]
                    target = (me + slot, me - slot)[side]

                    @pl.when(place > 0)
                    def _():
                        sum_arrived(side, slot, c)
                        added = buffer[slot, at(c), :].astype(F32) + partial[at(c), columns(target)].astype(F32)
                        buffer[slot, at(c), :] = added.astype(BF)

                    @pl.when(place == 0)
                    def _():
                        buffer[slot, at(c), :] = partial[at(c), columns(target)]

                    sum_copy(side, slot, c).start()

        def finish(done):
            total[...] = partial[at(done), columns(me)].astype(F32)

            @pl.when(me > 0)
            def _():
                sum_arrived(0, 0, done)
                total[...] += right[0, at(done), :].astype(F32)

            @pl.when(me < last)
            def _():
                sum_arrived(1, 0, done)
                total[...] += left[0, at(done), :].astype(F32)

            if backward:
                size = scale[at(done), 0:1]
                normal = middle[at(done), :].astype(F32) * size
                summed = total[...]
                own = residual[at(done), :].astype(F32) + size * (
                    summed * gain[...] - normal * mean[at(done), 0:1]
                )
                out_gain[...] += jnp.sum((summed * normal).reshape(rows // 8, 8, width), axis=0)
            else:
                own = residual[at(done), :].astype(F32) + total[...]
            out_own[at(done), :] = own.astype(out_own.dtype)
            if gathering:
                gathered[at(done), columns(me)] = own.astype(BF)

        done = now - last if summing else now

        @pl.when(inside(done))
        def _():
            if summing:
                finish(done)
            else:
                gathered[at(done), columns(me)] = residual[at(done), :]
            if gathering:

                @pl.when(me < last)
                def _():
                    all_copy(0, 0, done).start()

                @pl.when(me > 0)
                def _():
                    all_copy(1, 0, done).start()

        for far in range(1, count) if gathering else ():
            c = done - far
            for side in (0, 1):
                place = (me, last - me)[side]

                @pl.when(jnp.logical_and(inside(c), place >= far))
                def _(side=side, place=place, c=c, far=far):
                    all_arrived(side, far, c)

                    @pl.when(place < last)
                    def _():
                        all_copy(side, far, c).start()

        if not backward:
            full = done - last

            @pl.when(inside(full))
            def _():
                values = gathered[at(full), :].astype(F32)
                size = lax.rsqrt(jnp.mean(values * values, axis=1, keepdims=True) + eps)
                out[at(full), :] = (values * size * gain[...]).astype(BF)
                out_scale[at(full), :] = jnp.broadcast_to(size, (rows, 128))

        return 0

    lax.fori_loop(0, chunks + last * (summing + gathering), tick, 0)

    def settle(c, _):
        for side in (0, 1):
            place = (me, last - me)[side]
            for slot in range(1, count) if summing else ():

                @pl.when(place + slot <= last)
                def _(side=side, slot=slot):
                    sum_copy(side, slot, c).wait_send()

            for far in range(0, last) if gathering else ():

                @pl.when(jnp.logical_and(place < last, place >= far))
                def _(side=side, far=far):
                    all_copy(side, far, c).wait_send()

        return 0

    if backward:
        for p in range(2, len(halving.stages) - 1):
            halving.stage(p)
        halving.stage(len(halving.stages) - 1, out_spread)
        halving.settle()

    if mode == "last":
        mixer_sum = jnp.sum(out_gain[...], axis=0, keepdims=True)
        feed_sum = jnp.sum(feed_sums[...], axis=0, keepdims=True)
        gain_own[...] = jnp.concatenate([mixer_sum, feed_sum, jnp.zeros((6, width), F32)], axis=0)
        for copy in gain_rows:
            copy.start()
        for p in range(min(2, len(small_moves) - 1), len(small_moves)):
            small_stage(p)
        for copy in gain_rows:
            copy.wait_recv()
        added = gain_own[...]
        for d in range(1, lax.axis_size("row")):
            added = added + gain_row[d]
        gain_row[0] = added
        for copy in gain_seqs:
            copy.start()
        for copy in gain_seqs:
            copy.wait_recv()
        added = gain_row[0]
        for d in range(1, lax.axis_size("seq")):
            added = added + gain_seq[d]
        gain_seq[0] = added
        for copy in gain_reps:
            copy.start()
        own_gains[...] = added
        for copy in gain_reps:
            copy.wait_recv()
        for copy in small_moves + gain_rows + gain_seqs + gain_reps:
            copy.wait_send()

    lax.fori_loop(0, chunks, settle, 0)


def exchange(mode, operands, width, chunks=16):
    count = lax.axis_size("rep")
    length = operands[0].shape[0]
    features = count * width
    backward, summing, gathering = mode in ("back", "last"), mode != "first", mode != "last"
    vmem = pl.BlockSpec(memory_space=pltpu.VMEM)
    in_specs = [vmem] * len(operands)
    sems = [pltpu.SemaphoreType.DMA((2, count, chunks)), pltpu.SemaphoreType.DMA((2, count, chunks))]
    full, own = jax.ShapeDtypeStruct((length, features), BF), jax.ShapeDtypeStruct((length, width), F32)
    scale, gain = jax.ShapeDtypeStruct((length, 128), F32), jax.ShapeDtypeStruct((8, width), F32)
    if mode == "first":
        out_shape = [full, scale]
    elif mode == "norm":
        hidden = operands[0].shape
        out_shape = [full, scale, own, jax.ShapeDtypeStruct(hidden, F32), jax.ShapeDtypeStruct(hidden, BF)]
    elif mode == "back":
        out_shape = [full, own, gain]
    else:
        small = operands[7].shape
        out_shape = [
            jax.ShapeDtypeStruct((length, width), BF),
            jax.ShapeDtypeStruct(small, F32),
            jax.ShapeDtypeStruct((8, features), F32),
        ]
    if backward:
        spread = operands[-1].shape
        devices = lax.axis_size("row") * lax.axis_size("seq")
        out_shape.append(jax.ShapeDtypeStruct((spread[0] // devices, spread[1]), F32))
    scratch = [] if backward else [pltpu.VMEM((length, features), BF)]
    if backward:
        in_specs[-1] = pl.BlockSpec(memory_space=pl.ANY)
        scratch += halving_scratch(operands[-1].shape)
    if mode == "last":
        row, seq, stages = lax.axis_size("row"), lax.axis_size("seq"), len(halving_stages())
        most = max(row, seq, count)
        scratch += [
            pltpu.VMEM((8, width), F32),
            pltpu.VMEM((8, width), F32),
            pltpu.VMEM((row, 8, width), F32),
            pltpu.VMEM((seq, 8, width), F32),
            pltpu.VMEM((stages,) + small, BF),
            pltpu.VMEM((stages,) + small, BF),
            pltpu.SemaphoreType.DMA((3, 2, most)),
            pltpu.SemaphoreType.DMA((2, stages)),
        ]
    if summing:
        in_specs[4 if mode == "norm" else 1] = pl.BlockSpec(memory_space=pl.ANY)
        scratch += [
            pltpu.VMEM((length, features), BF),
            pltpu.VMEM((features, operands[0].shape[1]), BF),
            pltpu.VMEM((count, length, width), BF),
            pltpu.VMEM((count, length, width), BF),
            pltpu.VMEM((length // chunks, width), F32),
            pltpu.SemaphoreType.DMA,
        ] + sems
    if gathering:
        scratch += sems
    return pl.pallas_call(
        partial_call(exchange_kernel, count, chunks, mode),
        in_specs=in_specs,
        out_specs=[vmem] * len(out_shape),
        out_shape=out_shape,
        scratch_shapes=scratch,
        compiler_params=pltpu.CompilerParams(
            collective_id=("first", "norm", "back", "last").index(mode),
            has_side_effects=True,
            vmem_limit_bytes=LIMIT + (8 * 1024 * 1024 if mode == "back" else 0),
        ),
        cost_estimate=pl.CostEstimate(
            flops=10 * length * features, bytes_accessed=160 * length * features, transcendentals=0
        ),
    )(*operands)


def feed_kernel(normed_mid, cot, weights, out_low, out_grads, out_part, out_dot, held, sems):
    half = out_low.shape[1]
    step = pl.program_id(0)
    loads = [
        pltpu.make_async_copy(weights.at[:, pl.ds(k * half, half)], held.at[k], sems.at[k]) for k in range(3)
    ]

    @pl.when(step == 0)
    def _():
        for load in loads:
            load.start()

    def weight(k):
        @pl.when(step == 0)
        def _():
            loads[k].wait()

        return held[k]

    gate_pre = jnp.dot(normed_mid[...], weight(0), preferred_element_type=F32)
    up_pre = jnp.dot(normed_mid[...], weight(1), preferred_element_type=F32)
    value, slope = gelu_both(gate_pre)
    low = (value * up_pre).astype(BF)
    out_low[...] = low
    upstream = jnp.dot(cot[...], weight(2), preferred_element_type=F32)
    out_part[...] = back_dot(low, held[2]).astype(BF)
    gate_grad, up_grad = upstream * up_pre * slope, upstream * value
    out_grads[:, :half] = gate_grad.astype(BF)
    out_grads[:, half:] = up_grad.astype(BF)
    dots = jnp.sum(gate_grad * gate_pre + up_grad * up_pre, axis=1, keepdims=True)
    out_dot[...] = jnp.broadcast_to(dots, out_dot.shape)


def feed_both(normed_mid, cot, weights, rows=256):
    length, features = cot.shape
    half = weights.shape[1] // 3
    block = lambda width: pl.BlockSpec((rows, width), lambda i: (i, 0))
    return pl.pallas_call(
        feed_kernel,
        grid=(length // rows,),
        in_specs=[block(features), block(features), pl.BlockSpec(memory_space=pl.ANY)],
        out_specs=[block(half), block(2 * half), block(features), block(128)],
        out_shape=[
            jax.ShapeDtypeStruct((length, half), BF),
            jax.ShapeDtypeStruct((length, 2 * half), BF),
            jax.ShapeDtypeStruct((length, features), BF),
            jax.ShapeDtypeStruct((length, 128), F32),
        ],
        scratch_shapes=[pltpu.VMEM((3, features, half), BF), pltpu.SemaphoreType.DMA((3,))],
        compiler_params=pltpu.CompilerParams(vmem_limit_bytes=LIMIT),
        cost_estimate=pl.CostEstimate(
            flops=8 * length * features * half, bytes_accessed=12 * features * half, transcendentals=length * half
        ),
    )(normed_mid, cot, weights)


def per_segment(small, length):
    return jnp.broadcast_to(small[None], (length // SEGS,) + small.shape).reshape(length, small.shape[1])


def rows_dot(left, right):
    return lax.dot_general(left, right, (((0,), (0,)), ((), ())), preferred_element_type=F32)


def back_dot(left, right):
    return lax.dot_general(left, right, (((1,), (1,)), ((), ())), preferred_element_type=F32)


def dot(left, right):
    return jnp.dot(left, right, preferred_element_type=F32)


def shards(
    block_input, cotangent, segment_ids, pad_mask, state_init, window_init,
    recur_input, recur_gate, recur_output, feed_gate, feed_up, feed_down,
    conv_kernel, conv_bias, decay_gate, input_gate, decay_bias, input_bias, decay_logit, mixer_gain, feed_gain,
):
    own_width = block_input.shape[2]
    features = mixer_gain.shape[0]
    length = segment_ids.shape[1]
    taps = conv_kernel.shape[0]
    edge = taps - 1
    heads, head_width = decay_gate.shape[0], decay_gate.shape[2]
    rep = lax.axis_index("rep")
    seq, seqs = lax.axis_index("seq"), lax.axis_size("seq")
    at_start = seq == 0
    to_next = [(i, i + 1) for i in range(seqs - 1)]
    to_last = [(i + 1, i) for i in range(seqs - 1)]

    def weights(shard):
        return lax.all_gather(shard, ("seq", "row"), axis=0, tiled=True)

    def spread(partial_grad):
        return lax.psum_scatter(partial_grad, ("seq", "row"), scatter_dimension=0, tiled=True)

    def own_part(vector):
        return lax.dynamic_slice_in_dim(vector, rep * own_width, own_width, 0)[None]

    channels = conv_bias.shape[0]
    spare = -channels % 128

    def wide(values, fill=0):
        return jnp.pad(values, ((0, 0),) * (values.ndim - 1) + ((0, spare),), constant_values=fill)

    width = channels + spare

    x_low = by_step(block_input[0])
    cot_own = by_step(cotangent[0] * pad_mask[0][:, None].astype(BF))
    mixer_own, feed_own = own_part(mixer_gain), own_part(feed_gain)
    recur_shard = jnp.concatenate([wide(recur_input), wide(recur_gate), wide(recur_output)], axis=1)
    recur_shard, cot_own, x_low = after((recur_shard, cot_own, x_low))
    w_recur = weights(recur_shard)
    normed, s1 = exchange("first", (x_low, mixer_gain[None]), own_width)
    cot = lax.all_gather(cot_own, "rep", axis=1, tiled=True)
    w_input = w_recur[:, : 2 * width]

    left_ids = lax.ppermute(segment_ids[:, -edge:].astype(F32), "seq", to_next).astype(jnp.int32)
    left_ids = jnp.where(at_start, jnp.broadcast_to(segment_ids[:, :1], left_ids.shape), left_ids)
    ids_ext = jnp.concatenate([left_ids, segment_ids], axis=1)[0]
    same = [(ids_ext[edge - k : edge - k + length] == segment_ids[0]).astype(F32) for k in range(taps)]
    same = by_step(jnp.stack(same + [same[0]] * (8 - taps), axis=1))

    rate = 8.0 * jax.nn.softplus(decay_logit)
    params = wide(jnp.concatenate([conv_kernel, jnp.stack([conv_bias, decay_bias, input_bias])], axis=0))
    params = jnp.concatenate([params, wide(rate[None], 1)], axis=0)
    decay_w, input_w = block_diagonal(decay_gate, width), block_diagonal(input_gate, width)
    state_init = wide(state_init)

    projected = dot(normed, w_input)
    feed_shard, projected = after((jnp.concatenate([feed_gate, feed_up, feed_down], axis=1), projected))
    w_feed = weights(feed_shard)
    ends = projected[-edge * SEGS :, :width].astype(BF).reshape(edge, SEGS, width)
    left = lax.ppermute(ends[:, -1], "seq", to_next)
    left = jnp.where(at_start, wide(window_init[0]), left)
    prefix = jnp.concatenate([left[:, None], ends[:, :-1]], axis=1).reshape(edge * SEGS, -1)
    block_windows = ends[:, -1, :channels]

    gates, conv_out, decay_sig, gate_sig, retain, products, states, pre_a, pre_b, total = recur_forward(
        projected, same, prefix, params, decay_w, input_w
    )
    state_in = state_init
    for k in range(1, seqs):
        arriving = lax.ppermute(total[0:1] * state_in + total[1:2], "seq", to_next)
        state_in = jnp.where(seq == k, arriving, state_in)
    block_states = total[0:1] * state_in + total[1:2]
    carry = pre_a * state_in + pre_b

    normed_mid, s2, middle, hidden, gated = exchange(
        "norm", (states, products, gates, carry, w_recur, x_low, feed_gain[None]), own_width
    )
    normed_mid, cot = after((normed_mid, cot))
    feed_low, feed_grads, feed_part, mid_mean = feed_both(normed_mid, cot, w_feed)
    mid_mean = small_sum(mid_mean[:, 0].reshape(8, -1), "rep").reshape(-1, 1) / features

    half = feed_down.shape[1]
    down_grad = rows_dot(cot, feed_low).astype(BF)
    feed_grads, down_grad, mid_mean = after((feed_grads, down_grad, mid_mean))
    feed_all = rows_dot(normed_mid, feed_grads).astype(BF)
    feed_grads, feed_all, feed_part = after((feed_grads, feed_all, feed_part))
    feed_out = lax.psum_scatter(feed_part, "rep", scatter_dimension=1, tiled=True)
    feed_all = spread(feed_all)
    middle_low, middle_grad, feed_gain_own, feed_down_grad = exchange(
        "back",
        (feed_grads, w_feed, cot_own, middle, s2, jnp.broadcast_to(mid_mean, (length, 128)), feed_own, down_grad),
        own_width,
    )

    local, after_prod, branch_grad, enter_a, enter_b, back_total, branch_dot = recur_adjoint(
        middle_low, w_recur, projected, hidden, retain
    )
    output_all = rows_dot(middle_low, gated).astype(BF)
    local, output_all = after((local, output_all))
    entering = jnp.zeros_like(state_init)
    for k in range(1, seqs):
        arriving = lax.ppermute(back_total[0:1] * entering + back_total[1:2], "seq", to_last)
        entering = jnp.where(seq == seqs - 1 - k, arriving, entering)
    enter = enter_a * entering + enter_b
    decay_grad, input_grad_low, low_grad, low_dot, first, sums = recur_backward(
        local, after_prod, enter, hidden, carry, conv_out, decay_sig, gate_sig, retain, same, params, projected,
        decay_w, input_w,
    )
    owed = [first[0:8], first[8:24], first[24:48]]
    owed = [o.reshape(k + 1, SEGS, -1) for k, o in enumerate(owed)]
    ahead = prefix.reshape(edge, SEGS, -1).astype(F32)
    back_share = jnp.zeros_like(ahead)
    tap_extra = [jnp.zeros((width,), F32)]
    for k in range(1, taps):
        term = jnp.pad(owed[k - 1], ((edge - k, 0), (0, 0), (0, 0)))
        tap_extra.append(jnp.sum(term * ahead, axis=(0, 1)))
        back_share = back_share + params[k] * term
    from_right = lax.ppermute(back_share[:, 0], "seq", to_last)
    share = jnp.concatenate([back_share[:, 1:], from_right[:, None]], axis=1)
    low_grad = low_grad.reshape(length // SEGS, SEGS, -1)
    low_grad = jnp.concatenate([low_grad[:-edge], low_grad[-edge:] + share], axis=0).reshape(length, -1)
    share_dot = jnp.sum(share * ends.astype(F32), axis=2).reshape(-1)
    in_mean = low_dot[:, 0] + branch_dot[:, 0] + jnp.pad(share_dot, (length - share_dot.shape[0], 0))
    in_mean = small_sum(in_mean.reshape(8, -1), "rep").reshape(-1, 1) / features

    both_grads = jnp.concatenate([low_grad.astype(BF), branch_grad], axis=1)
    both_grads, in_mean, feed_all = after((both_grads, in_mean, feed_all))
    feed_gate_grad, feed_up_grad = feed_all[:, :half].astype(F32), feed_all[:, half:].astype(F32)
    conv_low = conv_out.astype(BF)
    decay_gate_grad = diagonal_rows(rows_dot(conv_low, decay_grad), heads, head_width)
    input_gate_grad = diagonal_rows(rows_dot(conv_low, input_grad_low), heads, head_width)
    sums = jnp.sum(sums.reshape(8, 8, -1), axis=1)
    conv_kernel_grad = sums[:taps] + jnp.stack(tap_extra)
    logit_grad = sums[7:, :channels] * 8.0 * jax.nn.sigmoid(decay_logit)
    vectors = jnp.concatenate([conv_kernel_grad, sums[4:7]], axis=0)[:, :channels]
    vectors = jnp.concatenate([vectors, logit_grad], axis=0)
    parts = (decay_gate_grad, input_gate_grad, vectors)
    small, counts = join_small(parts)
    recur_raw = rows_dot(normed, both_grads).astype(BF)
    recur_all = spread(recur_raw)
    both_grads, recur_raw, small, feed_out, feed_gate_grad, feed_up_grad = after(
        (both_grads, recur_raw, small, feed_out, feed_gate_grad, feed_up_grad)
    )
    input_grad, summed, gains, output_all = exchange(
        "last",
        (
            both_grads, w_recur, middle_grad, x_low, s1, jnp.broadcast_to(in_mean, (length, 128)), mixer_own,
            small, feed_gain_own, output_all,
        ),
        own_width,
    )
    input_grad, feed_out, recur_all = after((input_grad, feed_out, recur_all))
    recur_output_grad = output_all[:, :channels]
    recur_input_grad = recur_all[:, :channels].astype(F32)
    recur_gate_grad = recur_all[:, width : width + channels].astype(F32)
    input_grad = by_segment(input_grad)[None]
    block_output = by_segment((middle + feed_out.astype(F32)).astype(BF))[None]
    decay_gate_grad, input_gate_grad, vectors = split_small(summed, counts, parts)
    decay_gate_grad, input_gate_grad = (
        g[:, :head_width].reshape(decay_gate.shape) for g in (decay_gate_grad, input_gate_grad)
    )
    return (
        block_output, block_states[:, None, :channels], block_windows[None, None], input_grad,
        recur_input_grad, recur_gate_grad, recur_output_grad, feed_gate_grad, feed_up_grad, feed_down_grad,
        vectors[:taps], vectors[4], decay_gate_grad, input_gate_grad, vectors[5], vectors[6], vectors[7],
        gains[0], gains[1],
    )


def solution(mesh):
    tokens = P("row", "seq", "rep")
    matrix = P(("seq", "row"), "rep")
    in_specs = (
        tokens, tokens, P("row", "seq"), P("row", "seq"), P("row", "rep"), P("row", None, "rep"),
        matrix, matrix, matrix, matrix, matrix, matrix,
        P(None, "rep"), P("rep"), P("rep", None, None), P("rep", None, None), P("rep"), P("rep"), P("rep"), P(), P(),
    )
    out_specs = (
        tokens, tokens, P("row", "seq", None, "rep"), tokens,
        matrix, matrix, matrix, matrix, matrix, matrix,
        P(None, "rep"), P("rep"), P("rep", None, None), P("rep", None, None), P("rep"), P("rep"), P("rep"), P(), P(),
    )
    return jax.shard_map(shards, mesh=mesh, in_specs=in_specs, out_specs=out_specs, check_vma=False)
```

```python
from functools import partial as partial_call

import jax
import jax.numpy as jnp
from jax import lax
from jax.experimental import pallas as pl
from jax.experimental.pallas import tpu as pltpu
from jax.sharding import PartitionSpec as P

eps = 1e-06
SEGS = 8
BF = jnp.bfloat16
F32 = jnp.float32
LIMIT = 48 * 1024 * 1024


def gelu(v):
    return 0.5 * v * (1.0 + jnp.tanh(0.7978845608 * (v + 0.044715 * v * v * v)))


def gelu_both(v):
    square = v * v
    t = jnp.tanh(0.7978845608 * v * (1.0 + 0.044715 * square))
    value = 0.5 * v * (1.0 + t)
    slope = 0.5 * (1.0 + t) + 0.5 * v * (1.0 - t * t) * 0.7978845608 * (1.0 + 3 * 0.044715 * square)
    return value, slope


def one_minus_exp(y):
    series = y * (1 - y / 2 * (1 - y / 3 * (1 - y / 4 * (1 - y / 5 * (1 - y / 6 * (1 - y / 7))))))
    return jnp.where(y < 0.4, series, 1.0 - jnp.exp(-y))


after = lax.optimization_barrier


def join_small(parts):
    width = 256
    padded = []
    for part in parts:
        columns = -part.shape[1] % width
        padded.append(jnp.pad(part, ((0, 0), (0, columns))).reshape(-1, width))
    counts = [p.shape[0] for p in padded]
    spare = jnp.zeros((-sum(counts) % 16, width), F32)
    return jnp.concatenate(padded + [spare], axis=0).astype(BF), counts


def split_small(joined, counts, parts):
    out, start = [], 0
    for part, rows in zip(parts, counts):
        out.append(joined[start : start + rows].reshape(part.shape[0], -1)[:, : part.shape[1]])
        start += rows
    return out


def by_step(values):
    length, width = values.shape
    return values.reshape(SEGS, length // SEGS, width).transpose(1, 0, 2).reshape(length, width)


def by_segment(values):
    length, width = values.shape
    return values.reshape(length // SEGS, SEGS, width).transpose(1, 0, 2).reshape(length, width)


def block_diagonal(blocks, width):
    heads, wide = blocks.shape[0], blocks.shape[1]
    rows = [jnp.pad(blocks[h], ((0, 0), (h * wide, width - (h + 1) * wide))) for h in range(heads)]
    rows.append(jnp.zeros((width - heads * wide, width), blocks.dtype))
    return jnp.concatenate(rows, axis=0)


def diagonal_rows(dense, heads, wide):
    blocks = [dense[h * wide : (h + 1) * wide, h * wide : (h + 1) * wide] for h in range(heads)]
    return jnp.concatenate(blocks, axis=0)


def forward_kernel(
    conv_in, gate_branch, same, prefix, params, decay_w, input_w,
    out_gelu, out_conv, out_decay, out_gate, out_retain, out_prod, out_state, out_pre_a, out_pre_b, out_total,
    last_rows, prod_now, state_now, inflow_s,
):
    step = pl.program_id(0)
    rows = conv_in.shape[0]

    @pl.when(step == 0)
    def _():
        last_rows[...] = prefix[...].astype(F32)
        prod_now[...] = jnp.ones_like(prod_now)
        state_now[...] = jnp.zeros_like(state_now)

    out_gelu[...] = gelu(gate_branch[...])
    now = conv_in[...].astype(BF).astype(F32)
    ext = jnp.concatenate([last_rows[...], now], axis=0)
    same_all = same[...]
    total = params[4:5, :] + params[0:1, :] * now
    for k in (1, 2, 3):
        start = 24 - 8 * k
        total = total + params[k : k + 1, :] * ext[start : start + rows] * same_all[:, k : k + 1]
    last_rows[...] = now[rows - 24 :]
    out_conv[...] = total
    low = total.astype(BF)
    decay_sig = jax.nn.sigmoid(jnp.dot(low, decay_w[...], preferred_element_type=F32) + params[5:6, :])
    gate_sig = jax.nn.sigmoid(jnp.dot(low, input_w[...], preferred_element_type=F32) + params[6:7, :])
    out_decay[...] = decay_sig
    out_gate[...] = gate_sig
    expo = params[7:8, :] * decay_sig
    out_retain[...] = same_all[:, 1:2] * jnp.exp(-expo)
    inflow_s[...] = jnp.sqrt(one_minus_exp(2.0 * expo)) * gate_sig * total
    prod, state = prod_now[...], state_now[...]
    for t in range(rows // SEGS):
        at = slice(t * SEGS, (t + 1) * SEGS)
        keep = out_retain[at, :]
        prod = prod * keep
        state = state * keep + inflow_s[at, :]
        out_prod[at, :] = prod
        out_state[at, :] = state
    prod_now[...] = prod
    state_now[...] = state

    @pl.when(step == pl.num_programs(0) - 1)
    def _():
        carry_a = jnp.ones_like(prod[0:1])
        carry_b = jnp.zeros_like(carry_a)
        for s in range(SEGS):
            out_pre_a[s : s + 1, :] = carry_a
            out_pre_b[s : s + 1, :] = carry_b
            carry_b = prod[s : s + 1] * carry_b + state[s : s + 1]
            carry_a = prod[s : s + 1] * carry_a
        out_total[0:1, :] = carry_a
        out_total[1:2, :] = carry_b
        out_total[2:8, :] = jnp.zeros((6, carry_a.shape[1]), F32)


def recur_forward(conv_in, same, prefix, params, decay_w, input_w, rows=256):
    length, width = conv_in.shape[0], params.shape[1]
    block = pl.BlockSpec((rows, width), lambda i: (i, 0))
    fixed = lambda shape: pl.BlockSpec(shape, lambda i: (0, 0))
    big = jax.ShapeDtypeStruct((length, width), F32)
    small = jax.ShapeDtypeStruct((SEGS, width), F32)
    return pl.pallas_call(
        forward_kernel,
        grid=(length // rows,),
        in_specs=[
            block,
            pl.BlockSpec((rows, width), lambda i: (i, 1)),
            pl.BlockSpec((rows, 8), lambda i: (i, 0)),
            fixed((24, width)),
            fixed((8, width)),
            fixed((width, width)),
            fixed((width, width)),
        ],
        out_specs=[block] * 7 + [fixed((SEGS, width))] * 3,
        out_shape=[big] * 7 + [small] * 3,
        scratch_shapes=[
            pltpu.VMEM((24, width), F32),
            pltpu.VMEM((SEGS, width), F32),
            pltpu.VMEM((SEGS, width), F32),
            pltpu.VMEM((rows, width), F32),
        ],
        compiler_params=pltpu.CompilerParams(vmem_limit_bytes=LIMIT),
        cost_estimate=pl.CostEstimate(flops=length * width, bytes_accessed=4 * length * width, transcendentals=0),
    )(conv_in, conv_in, same, prefix, params, decay_w, input_w)


def adjoint_kernel(
    middle_low, weight, gate_branch, hidden, retain,
    out_local, out_after, out_branch, out_pre_a, out_pre_b, out_total, out_dot,
    local_now, after_now, next_retain, grad_s,
):
    step = pl.program_id(0)
    rows = hidden.shape[0]

    @pl.when(step == 0)
    def _():
        local_now[...] = jnp.zeros_like(local_now)
        after_now[...] = jnp.ones_like(after_now)
        next_retain[...] = jnp.ones_like(next_retain)

    value, slope = gelu_both(gate_branch[...])
    upstream = jnp.dot(middle_low[...], weight[...], preferred_element_type=F32)
    grad_s[...] = upstream * value
    branch = upstream * hidden[...] * slope
    out_branch[...] = branch.astype(BF)
    out_dot[...] = jnp.broadcast_to(jnp.sum(branch * gate_branch[...], axis=1, keepdims=True), out_dot.shape)
    local, after, keep = local_now[...], after_now[...], next_retain[...]
    for t in reversed(range(rows // SEGS)):
        at = slice(t * SEGS, (t + 1) * SEGS)
        local = grad_s[at, :] + keep * local
        after = keep * after
        out_local[at, :] = local
        out_after[at, :] = after
        keep = retain[at, :]
    local_now[...] = local
    after_now[...] = after
    next_retain[...] = keep

    @pl.when(step == pl.num_programs(0) - 1)
    def _():
        carry_a = jnp.ones_like(local[0:1])
        carry_b = jnp.zeros_like(carry_a)
        for s in reversed(range(SEGS)):
            out_pre_a[s : s + 1, :] = carry_a
            out_pre_b[s : s + 1, :] = carry_b
            carry_b = keep[s : s + 1] * (local[s : s + 1] + after[s : s + 1] * carry_b)
            carry_a = keep[s : s + 1] * after[s : s + 1] * carry_a
        out_total[0:1, :] = carry_a
        out_total[1:2, :] = carry_b
        out_total[2:8, :] = jnp.zeros((6, carry_a.shape[1]), F32)


def recur_adjoint(middle_low, w_recur, gate_branch, hidden, retain, rows=256):
    length, width = hidden.shape
    features = middle_low.shape[1]
    last = length // rows - 1
    block = pl.BlockSpec((rows, width), lambda i: (last - i, 0))
    second = pl.BlockSpec((rows, width), lambda i: (last - i, 1))
    fixed = lambda shape: pl.BlockSpec(shape, lambda i: (0, 0))
    big = jax.ShapeDtypeStruct((length, width), F32)
    small = jax.ShapeDtypeStruct((SEGS, width), F32)
    return pl.pallas_call(
        adjoint_kernel,
        grid=(length // rows,),
        in_specs=[
            pl.BlockSpec((rows, features), lambda i: (last - i, 0)),
            pl.BlockSpec((features, width), lambda i: (0, 2), pipeline_mode=pl.Buffered(1)),
            second, block, block,
        ],
        out_specs=[block] * 3 + [fixed((SEGS, width))] * 3 + [pl.BlockSpec((rows, 128), lambda i: (last - i, 0))],
        out_shape=[big, big, jax.ShapeDtypeStruct((length, width), BF)]
        + [small] * 3
        + [jax.ShapeDtypeStruct((length, 128), F32)],
        scratch_shapes=[pltpu.VMEM((SEGS, width), F32)] * 3 + [pltpu.VMEM((rows, width), F32)],
        compiler_params=pltpu.CompilerParams(vmem_limit_bytes=LIMIT),
        cost_estimate=pl.CostEstimate(flops=length * width, bytes_accessed=4 * length * width, transcendentals=0),
    )(middle_low, w_recur, gate_branch, hidden, retain)


def backward_kernel(
    local, after, enter, hidden, hidden_before, carry, conv_out, decay_sig, gate_sig, retain, same, params, conv_in,
    decay_w, input_w,
    out_decay, out_input, out_low, out_dot, out_first, out_sums,
    next_one, next_two, next_three,
):
    step = pl.program_id(0)
    blocks = pl.num_programs(0)
    rows = local.shape[0]
    width = local.shape[1]

    @pl.when(step == 0)
    def _():
        for held in (next_one, next_two, next_three):
            held[...] = jnp.zeros_like(held)
        out_sums[...] = jnp.zeros_like(out_sums)

    def per_step(small):
        return jnp.broadcast_to(small[None], (rows // SEGS, SEGS, width)).reshape(rows, width)

    def sums(values):
        return jnp.sum(values.reshape(rows // SEGS, SEGS, width), axis=0)

    adjoint = local[...] + after[...] * per_step(enter[...])
    ahead = jnp.where(step == blocks - 1, carry[...], hidden_before[...])
    hidden_prev = jnp.concatenate([ahead, hidden[...][: rows - SEGS]], axis=0)
    conv, decay, gate = conv_out[...], decay_sig[...], gate_sig[...]
    rate = params[7:8, :]
    expo = rate * decay
    inner = one_minus_exp(2.0 * expo)
    root = jnp.sqrt(inner)
    expo_grad = adjoint * (gate * conv * (1.0 - inner) / root - retain[...] * hidden_prev)
    decay_grad = (expo_grad * rate * decay * (1.0 - decay)).astype(BF)
    input_grad = (adjoint * root * conv * gate * (1.0 - gate)).astype(BF)
    out_decay[...] = decay_grad
    out_input[...] = input_grad
    dims = (((1,), (1,)), ((), ()))
    conv_grad = (
        adjoint * root * gate
        + lax.dot_general(decay_grad, decay_w[...], dims, preferred_element_type=F32)
        + lax.dot_general(input_grad, input_w[...], dims, preferred_element_type=F32)
    )
    same_all = same[...]
    now = conv_in[...].astype(BF).astype(F32)
    low = params[0:1, :] * conv_grad
    out_sums[0:8, :] += sums(conv_grad * now)
    for k, held in ((1, next_one), (2, next_two), (3, next_three)):
        masked = conv_grad * same_all[:, k : k + 1]
        moved = jnp.concatenate([masked[8 * k :], held[...]], axis=0)
        held[...] = masked[: 8 * k]
        low = low + params[k : k + 1, :] * moved
        out_sums[8 * k : 8 * k + 8, :] += sums(moved * now)
    out_low[...] = low
    out_dot[...] = jnp.broadcast_to(jnp.sum(low * now, axis=1, keepdims=True), out_dot.shape)
    out_sums[32:40, :] += sums(conv_grad)
    out_sums[40:48, :] += sums(decay_grad.astype(F32))
    out_sums[48:56, :] += sums(input_grad.astype(F32))
    out_sums[56:64, :] += sums(expo_grad * decay)

    @pl.when(step == blocks - 1)
    def _():
        out_first[0:8, :] = next_one[...]
        out_first[8:24, :] = next_two[...]
        out_first[24:48, :] = next_three[...]


def recur_backward(
    local, after, enter, hidden, carry, conv_out, decay_sig, gate_sig, retain, same, params, conv_in, decay_w, input_w,
    rows=256,
):
    length, width = local.shape
    last = length // rows - 1
    block = pl.BlockSpec((rows, width), lambda i: (last - i, 0))
    fixed = lambda shape: pl.BlockSpec(shape, lambda i: (0, 0))
    steps = rows // SEGS
    before = pl.BlockSpec((SEGS, width), lambda i: (jnp.maximum((last - i) * steps - 1, 0), 0))
    return pl.pallas_call(
        backward_kernel,
        grid=(length // rows,),
        in_specs=[
            block, block, fixed((SEGS, width)), block, before, fixed((SEGS, width)), block, block, block, block,
            pl.BlockSpec((rows, 8), lambda i: (last - i, 0)),
            fixed((8, width)), block, fixed((width, width)), fixed((width, width)),
        ],
        out_specs=[
            block, block, block, pl.BlockSpec((rows, 128), lambda i: (last - i, 0)), fixed((48, width)),
            fixed((64, width)),
        ],
        out_shape=[
            jax.ShapeDtypeStruct((length, width), BF),
            jax.ShapeDtypeStruct((length, width), BF),
            jax.ShapeDtypeStruct((length, width), F32),
            jax.ShapeDtypeStruct((length, 128), F32),
            jax.ShapeDtypeStruct((48, width), F32),
            jax.ShapeDtypeStruct((64, width), F32),
        ],
        scratch_shapes=[
            pltpu.VMEM((8, width), F32),
            pltpu.VMEM((16, width), F32),
            pltpu.VMEM((24, width), F32),
        ],
        compiler_params=pltpu.CompilerParams(vmem_limit_bytes=LIMIT),
        cost_estimate=pl.CostEstimate(flops=length * width, bytes_accessed=4 * length * width, transcendentals=0),
    )(
        local, after, enter, hidden, hidden, carry, conv_out, decay_sig, gate_sig, retain, same, params, conv_in,
        decay_w, input_w,
    )


class Halving:
    def __init__(self, source, keep, arrivals, sends, receives, loads):
        self.source, self.keep, self.arrivals = source, keep, arrivals
        self.sends, self.receives, self.loads = sends, receives, loads
        rows, seqs = lax.axis_size("row"), lax.axis_size("seq")
        self.total = rows * seqs
        self.place = lax.axis_index("seq") * rows + lax.axis_index("row")
        self.stages = halving_stages()
        self.height = source.shape[0] // self.total

    def own_bit(self, p):
        axis, step = self.stages[p]
        return lax.rem(lax.axis_index(axis) // step, 2)

    def block(self, p, mine, j):
        bit = self.own_bit(p) if mine else 1 - self.own_bit(p)
        return lax.rem(self.place, 2**p) + bit * 2**p + j * 2 ** (p + 1)

    def many(self, p):
        return self.total // 2 ** (p + 1)

    def held(self, p, mine, j):
        return self.keep.at[self.block(p, mine, j) // 2]

    def rows_of(self, block):
        return self.source.at[pl.ds(pl.multiple_of(block * self.height, self.height), self.height)]

    def moves(self, p):
        axis, step = self.stages[p]
        partner = lax.axis_index(axis) + step - 2 * step * self.own_bit(p)
        start = self.total - self.total // 2**p
        copies = []
        for j in range(self.many(p)):
            copies.append(
                pltpu.make_async_remote_copy(
                    src_ref=self.held(p, False, j) if p else self.rows_of(self.block(0, False, j)),
                    dst_ref=self.arrivals.at[start + j],
                    send_sem=self.sends.at[start + j],
                    recv_sem=self.receives.at[start + j],
                    device_id={axis: partner},
                    device_id_type=pl.DeviceIdType.MESH,
                )
            )
        return copies

    def local(self):
        return [
            pltpu.make_async_copy(self.rows_of(self.block(0, True, j)), self.keep.at[j], self.loads.at[j])
            for j in range(self.many(0))
        ]

    def begin(self):
        for copy in self.moves(0) + self.local():
            copy.start()

    def stage(self, p, out=None):
        if p == 0:
            for copy in self.local():
                copy.wait()
        for copy in self.moves(p):
            copy.wait_recv()
        start = self.total - self.total // 2**p
        piece = 32
        for j in range(self.many(p)):
            slot = self.block(p, True, j) // 2

            def add(i, _, j=j, slot=slot):
                at = pl.ds(pl.multiple_of(i * piece, piece), piece)
                added = self.keep[slot, at, :].astype(F32) + self.arrivals[start + j, at, :].astype(F32)
                if out is None:
                    self.keep[slot, at, :] = added.astype(BF)
                else:
                    out[at, :] = added
                return 0

            lax.fori_loop(0, self.height // piece, add, 0)
        if out is None:
            for copy in self.moves(p + 1):
                copy.start()

    def settle(self):
        for p in range(len(self.stages)):
            for copy in self.moves(p):
                copy.wait_send()

    def partners(self):
        found = []
        for p, (axis, step) in enumerate(self.stages):
            found.append({axis: lax.axis_index(axis) + step - 2 * step * self.own_bit(p)})
        return found


def halving_stages():
    stages = []
    for axis in ("row", "seq"):
        step = 1
        while step < lax.axis_size(axis):
            stages.append((axis, step))
            step *= 2
    return stages


def halving_scratch(shape):
    total = lax.axis_size("row") * lax.axis_size("seq")
    height = shape[0] // total
    return [
        pltpu.VMEM((total // 2, height, shape[1]), BF),
        pltpu.VMEM((total - 1, height, shape[1]), BF),
        pltpu.SemaphoreType.DMA((total - 1,)),
        pltpu.SemaphoreType.DMA((total - 1,)),
        pltpu.SemaphoreType.DMA((total // 2,)),
    ]


def exchange_kernel(count, chunks, mode, *refs):
    backward, summing, gathering = mode in ("back", "last"), mode != "first", mode != "last"
    refs = list(refs)
    take = lambda number: [refs.pop(0) for _ in range(number)]
    if mode == "first":
        residual, gain, out, out_scale, gathered = take(5)
    elif mode == "norm":
        states, products, gates, carry, weight, residual, gain, out, out_scale, out_own, out_hidden, out_gated = take(12)
        (gathered,) = take(1)
    elif mode == "back":
        grads, weight, residual, middle, scale, mean, gain, spread_in, out, out_own, out_gain, out_spread = take(12)
        gathered = out
        halving = Halving(spread_in, *take(5))
    else:
        grads, weight, residual, middle, scale, mean, gain, small, feed_sums, spread_in = take(10)
        out_own, out_small, out_gains, out_spread = take(4)
        halving = Halving(spread_in, *take(5))
        out_gain, gain_own, gain_row, gain_seq, small_held, small_got, gain_sems, small_sems = take(8)
    if backward:
        mean_got, mean_sum, mean_sems = take(3)
    if summing:
        partial, held_weight, right, left, total, weight_sem, sum_send, sum_recv = take(8)
    if gathering:
        all_send, all_recv = take(2)
    me = lax.axis_index("rep")
    length, width = residual.shape
    rows = length // chunks
    last = count - 1

    if summing:
        start = weight.shape[1] - held_weight.shape[1] if mode == "norm" else 0
        load = pltpu.make_async_copy(weight.at[:, pl.ds(start, held_weight.shape[1])], held_weight, weight_sem)
        load.start()
    barrier = pltpu.get_barrier_semaphore()

    def greet(device):
        pl.semaphore_signal(barrier, inc=1, device_id=device, device_id_type=pl.DeviceIdType.MESH)

    if backward:
        axes = ("rep",) if mode == "back" else ("row", "seq", "rep")
        devices = halving.partners() if mode == "back" else []
        for axis in axes:
            for d in range(1, lax.axis_size(axis)):
                devices.append({axis: lax.rem(lax.axis_index(axis) + d, lax.axis_size(axis))})
        for device in devices:
            greet(device)
        pl.semaphore_wait(barrier, len(devices))
        halving.begin()
    else:

        @pl.when(me > 0)
        def _():
            greet({"rep": me - 1})

        @pl.when(me < last)
        def _():
            greet({"rep": me + 1})

        inner = jnp.logical_and(me > 0, me < last)

        @pl.when(inner)
        def _():
            pl.semaphore_wait(barrier, 2)

        @pl.when(jnp.logical_not(inner))
        def _():
            pl.semaphore_wait(barrier, 1)

    def to_peers(axis, source, target, sems):
        copies = []
        for d in range(1, lax.axis_size(axis)):
            peer = lax.rem(lax.axis_index(axis) + d, lax.axis_size(axis))
            copies.append(
                pltpu.make_async_remote_copy(
                    src_ref=source,
                    dst_ref=target(d),
                    send_sem=sems.at[0, d],
                    recv_sem=sems.at[1, d],
                    device_id={axis: peer},
                    device_id_type=pl.DeviceIdType.MESH,
                )
            )
        return copies

    if backward:
        mean_moves = to_peers("rep", mean, lambda d: mean_got.at[d], mean_sems)
        for copy in mean_moves:
            copy.start()

    def mean_column(c):
        per = 128 // rows
        line = jnp.broadcast_to(mean_sum[pl.ds(c // per, 1), :], (rows, 128))
        lane = lax.broadcasted_iota(jnp.int32, (rows, 128), 1)
        row = lax.broadcasted_iota(jnp.int32, (rows, 128), 0) + lax.rem(c, per) * rows
        return jnp.sum(jnp.where(lane == row, line, 0.0), axis=1, keepdims=True)

    if mode == "last":
        small_moves = [
            pltpu.make_async_remote_copy(
                src_ref=small_held.at[p],
                dst_ref=small_got.at[p],
                send_sem=small_sems.at[0, p],
                recv_sem=small_sems.at[1, p],
                device_id=partner,
                device_id_type=pl.DeviceIdType.MESH,
            )
            for p, partner in enumerate(halving.partners())
        ]
        gain_rows = to_peers("row", gain_own, lambda d: gain_row.at[d], gain_sems.at[0])
        gain_seqs = to_peers("seq", gain_row.at[0], lambda d: gain_seq.at[d], gain_sems.at[1])
        own_gains = out_gains.at[:, pl.ds(pl.multiple_of(me * width, width), width)]
        gain_reps = to_peers("rep", gain_seq.at[0], lambda d: own_gains, gain_sems.at[2])
        small_held[0] = small[...]
        small_moves[0].start()

    def small_stage(p):
        small_moves[p].wait_recv()
        added = small_held[p].astype(F32) + small_got[p].astype(F32)
        if p + 1 < len(small_moves):
            small_held[p + 1] = added.astype(BF)
            small_moves[p + 1].start()
        else:
            out_small[...] = added

    if backward:
        out_gain[...] = jnp.zeros_like(out_gain)
    if summing:
        load.wait()

    def at(c):
        return pl.ds(pl.multiple_of(c * rows, rows), rows)

    def columns(device):
        return pl.ds(pl.multiple_of(device * width, width), width)

    def sum_copy(side, slot, c):
        buffer, to = ((right, me + 1), (left, me - 1))[side]
        return pltpu.make_async_remote_copy(
            src_ref=buffer.at[slot, at(c)],
            dst_ref=buffer.at[slot - 1, at(c)],
            send_sem=sum_send.at[side, slot, c],
            recv_sem=sum_recv.at[side, slot - 1, c],
            device_id={"rep": to},
            device_id_type=pl.DeviceIdType.MESH,
        )

    def sum_arrived(side, slot, c):
        buffer, sender = ((right, me - 1), (left, me + 1))[side]
        pltpu.make_async_remote_copy(
            src_ref=buffer.at[slot, at(c)],
            dst_ref=buffer.at[slot, at(c)],
            send_sem=sum_send.at[side, slot, c],
            recv_sem=sum_recv.at[side, slot, c],
            device_id={"rep": sender},
            device_id_type=pl.DeviceIdType.MESH,
        ).wait_recv()

    def all_copy(side, far, c):
        source, to = ((me - far, me + 1), (me + far, me - 1))[side]
        piece = gathered.at[at(c), columns(source)]
        return pltpu.make_async_remote_copy(
            src_ref=piece,
            dst_ref=piece,
            send_sem=all_send.at[side, far, c],
            recv_sem=all_recv.at[side, far + 1, c],
            device_id={"rep": to},
            device_id_type=pl.DeviceIdType.MESH,
        )

    def all_arrived(side, far, c):
        source, sender = ((me - far, me - 1), (me + far, me + 1))[side]
        piece = gathered.at[at(c), columns(source)]
        pltpu.make_async_remote_copy(
            src_ref=piece,
            dst_ref=piece,
            send_sem=all_send.at[side, far, c],
            recv_sem=all_recv.at[side, far, c],
            device_id={"rep": sender},
            device_id_type=pl.DeviceIdType.MESH,
        ).wait_recv()

    def inside(c):
        return jnp.logical_and(c >= 0, c < chunks)

    stride = 1

    def produce(c):
        some = pl.ds(pl.multiple_of(c * rows, stride * rows), stride * rows)
        if mode == "norm":
            wide = (stride * rows // SEGS, SEGS, carry.shape[1])
            enter = jnp.broadcast_to(carry[...][None], wide).reshape(stride * rows, carry.shape[1])
            hidden = states[some, :] + products[some, :] * enter
            low = (hidden * gates[some, :]).astype(BF)
            out_hidden[some, :] = hidden
            out_gated[some, :] = low
        else:
            low = grads[some, :]
        partial[some, :] = back_dot(low, held_weight[...]).astype(BF)

    def tick(now, _):
        if backward:

            @pl.when(now == last)
            def _():
                for copy in mean_moves:
                    copy.wait_recv()
                added = mean[...]
                for d in range(1, count):
                    added = added + mean_got[d]
                mean_sum[...] = added * (1.0 / (count * width))

            for p, when in ((0, 2), (1, 15 if mode == "back" else 13)):
                if p < len(halving.stages) - 1:

                    @pl.when(now == when)
                    def _(p=p):
                        halving.stage(p)

        if mode == "last":
            for p, when in ((0, 1), (1, 8)):
                if p < len(small_moves) - 1:

                    @pl.when(now == when)
                    def _(p=p):
                        small_stage(p)

        if summing:

            @pl.when(jnp.logical_and(now < chunks, lax.rem(now, stride) == 0))
            def _():
                produce(now)

        for side in (0, 1) if summing else ():
            place = (me, last - me)[side]
            c = now - place
            for slot in range(last, 0, -1):

                @pl.when(jnp.logical_and(inside(c), place + slot <= last))
                def _(side=side, place=place, c=c, slot=slot):
                    buffer = (right, left)[side]
                    target = (me + slot, me - slot)[side]

                    @pl.when(place > 0)
                    def _():
                        sum_arrived(side, slot, c)
                        added = buffer[slot, at(c), :].astype(F32) + partial[at(c), columns(target)].astype(F32)
                        buffer[slot, at(c), :] = added.astype(BF)

                    @pl.when(place == 0)
                    def _():
                        buffer[slot, at(c), :] = partial[at(c), columns(target)]

                    sum_copy(side, slot, c).start()

        def finish(done):
            total[...] = partial[at(done), columns(me)].astype(F32)

            @pl.when(me > 0)
            def _():
                sum_arrived(0, 0, done)
                total[...] += right[0, at(done), :].astype(F32)

            @pl.when(me < last)
            def _():
                sum_arrived(1, 0, done)
                total[...] += left[0, at(done), :].astype(F32)

            if backward:
                size = scale[at(done), 0:1]
                normal = middle[at(done), :].astype(F32) * size
                summed = total[...]
                own = residual[at(done), :].astype(F32) + size * (
                    summed * gain[...] - normal * mean_column(done)
                )
                out_gain[...] += jnp.sum((summed * normal).reshape(rows // 8, 8, width), axis=0)
            else:
                own = residual[at(done), :].astype(F32) + total[...]
            out_own[at(done), :] = own.astype(out_own.dtype)
            if gathering:
                gathered[at(done), columns(me)] = own.astype(BF)

        done = now - last if summing else now

        @pl.when(inside(done))
        def _():
            if summing:
                finish(done)
            else:
                gathered[at(done), columns(me)] = residual[at(done), :]
            if gathering:

                @pl.when(me < last)
                def _():
                    all_copy(0, 0, done).start()

                @pl.when(me > 0)
                def _():
                    all_copy(1, 0, done).start()

        for far in range(1, count) if gathering else ():
            c = done - far
            for side in (0, 1):
                place = (me, last - me)[side]

                @pl.when(jnp.logical_and(inside(c), place >= far))
                def _(side=side, place=place, c=c, far=far):
                    all_arrived(side, far, c)

                    @pl.when(place < last)
                    def _():
                        all_copy(side, far, c).start()

        if not backward:
            full = done - last

            @pl.when(inside(full))
            def _():
                values = gathered[at(full), :].astype(F32)
                size = lax.rsqrt(jnp.mean(values * values, axis=1, keepdims=True) + eps)
                out[at(full), :] = (values * size * gain[...]).astype(BF)
                out_scale[at(full), :] = jnp.broadcast_to(size, (rows, 128))

        return 0

    lax.fori_loop(0, chunks + last * (summing + gathering), tick, 0)

    def settle(c, _):
        for side in (0, 1):
            place = (me, last - me)[side]
            for slot in range(1, count) if summing else ():

                @pl.when(place + slot <= last)
                def _(side=side, slot=slot):
                    sum_copy(side, slot, c).wait_send()

            for far in range(0, last) if gathering else ():

                @pl.when(jnp.logical_and(place < last, place >= far))
                def _(side=side, far=far):
                    all_copy(side, far, c).wait_send()

        return 0

    if backward:
        for p in range(2, len(halving.stages) - 1):
            halving.stage(p)
        halving.stage(len(halving.stages) - 1, out_spread)
        halving.settle()
        for copy in mean_moves:
            copy.wait_send()

    if mode == "last":
        mixer_sum = jnp.sum(out_gain[...], axis=0, keepdims=True)
        feed_sum = jnp.sum(feed_sums[...], axis=0, keepdims=True)
        gain_own[...] = jnp.concatenate([mixer_sum, feed_sum, jnp.zeros((6, width), F32)], axis=0)
        for copy in gain_rows:
            copy.start()
        for p in range(min(2, len(small_moves) - 1), len(small_moves)):
            small_stage(p)
        for copy in gain_rows:
            copy.wait_recv()
        added = gain_own[...]
        for d in range(1, lax.axis_size("row")):
            added = added + gain_row[d]
        gain_row[0] = added
        for copy in gain_seqs:
            copy.start()
        for copy in gain_seqs:
            copy.wait_recv()
        added = gain_row[0]
        for d in range(1, lax.axis_size("seq")):
            added = added + gain_seq[d]
        gain_seq[0] = added
        for copy in gain_reps:
            copy.start()
        own_gains[...] = added
        for copy in gain_reps:
            copy.wait_recv()
        for copy in small_moves + gain_rows + gain_seqs + gain_reps:
            copy.wait_send()

    lax.fori_loop(0, chunks, settle, 0)


def exchange(mode, operands, width, chunks=16):
    count = lax.axis_size("rep")
    length = operands[0].shape[0]
    features = count * width
    backward, summing, gathering = mode in ("back", "last"), mode != "first", mode != "last"
    vmem = pl.BlockSpec(memory_space=pltpu.VMEM)
    in_specs = [vmem] * len(operands)
    sems = [pltpu.SemaphoreType.DMA((2, count, chunks)), pltpu.SemaphoreType.DMA((2, count, chunks))]
    full, own = jax.ShapeDtypeStruct((length, features), BF), jax.ShapeDtypeStruct((length, width), F32)
    scale, gain = jax.ShapeDtypeStruct((length, 128), F32), jax.ShapeDtypeStruct((8, width), F32)
    if mode == "first":
        out_shape = [full, scale]
    elif mode == "norm":
        hidden = operands[0].shape
        out_shape = [full, scale, own, jax.ShapeDtypeStruct(hidden, F32), jax.ShapeDtypeStruct(hidden, BF)]
    elif mode == "back":
        out_shape = [full, own, gain]
    else:
        small = operands[7].shape
        out_shape = [
            jax.ShapeDtypeStruct((length, width), BF),
            jax.ShapeDtypeStruct(small, F32),
            jax.ShapeDtypeStruct((8, features), F32),
        ]
    if backward:
        spread = operands[-1].shape
        devices = lax.axis_size("row") * lax.axis_size("seq")
        out_shape.append(jax.ShapeDtypeStruct((spread[0] // devices, spread[1]), F32))
    scratch = [] if backward else [pltpu.VMEM((length, features), BF)]
    if backward:
        in_specs[-1] = pl.BlockSpec(memory_space=pl.ANY)
        scratch += halving_scratch(operands[-1].shape)
    if mode == "last":
        row, seq, stages = lax.axis_size("row"), lax.axis_size("seq"), len(halving_stages())
        most = max(row, seq, count)
        scratch += [
            pltpu.VMEM((8, width), F32),
            pltpu.VMEM((8, width), F32),
            pltpu.VMEM((row, 8, width), F32),
            pltpu.VMEM((seq, 8, width), F32),
            pltpu.VMEM((stages,) + small, BF),
            pltpu.VMEM((stages,) + small, BF),
            pltpu.SemaphoreType.DMA((3, 2, most)),
            pltpu.SemaphoreType.DMA((2, stages)),
        ]
    if backward:
        packed = (length // 128, 128)
        scratch += [
            pltpu.VMEM((count,) + packed, F32), pltpu.VMEM(packed, F32), pltpu.SemaphoreType.DMA((2, count)),
        ]
    if summing:
        in_specs[4 if mode == "norm" else 1] = pl.BlockSpec(memory_space=pl.ANY)
        scratch += [
            pltpu.VMEM((length, features), BF),
            pltpu.VMEM((features, operands[0].shape[1]), BF),
            pltpu.VMEM((count, length, width), BF),
            pltpu.VMEM((count, length, width), BF),
            pltpu.VMEM((length // chunks, width), F32),
            pltpu.SemaphoreType.DMA,
        ] + sems
    if gathering:
        scratch += sems
    return pl.pallas_call(
        partial_call(exchange_kernel, count, chunks, mode),
        in_specs=in_specs,
        out_specs=[vmem] * len(out_shape),
        out_shape=out_shape,
        scratch_shapes=scratch,
        compiler_params=pltpu.CompilerParams(
            collective_id=("first", "norm", "back", "last").index(mode),
            has_side_effects=True,
            vmem_limit_bytes=LIMIT + (8 * 1024 * 1024 if mode == "back" else 0),
        ),
        cost_estimate=pl.CostEstimate(
            flops=10 * length * features, bytes_accessed=160 * length * features, transcendentals=0
        ),
    )(*operands)


def feed_kernel(normed_mid, cot, weights, out_low, out_grads, out_part, out_dot, held, sems):
    half = out_low.shape[1]
    step = pl.program_id(0)
    loads = [
        pltpu.make_async_copy(weights.at[:, pl.ds(k * half, half)], held.at[k], sems.at[k]) for k in range(3)
    ]

    @pl.when(step == 0)
    def _():
        for load in loads:
            load.start()

    def weight(k):
        @pl.when(step == 0)
        def _():
            loads[k].wait()

        return held[k]

    gate_pre = jnp.dot(normed_mid[...], weight(0), preferred_element_type=F32)
    up_pre = jnp.dot(normed_mid[...], weight(1), preferred_element_type=F32)
    value, slope = gelu_both(gate_pre)
    low = (value * up_pre).astype(BF)
    out_low[...] = low
    upstream = jnp.dot(cot[...], weight(2), preferred_element_type=F32)
    out_part[...] = back_dot(low, held[2]).astype(BF)
    gate_grad, up_grad = upstream * up_pre * slope, upstream * value
    out_grads[:, :half] = gate_grad.astype(BF)
    out_grads[:, half:] = up_grad.astype(BF)
    dots = jnp.sum(gate_grad * gate_pre + up_grad * up_pre, axis=1, keepdims=True)
    out_dot[...] = jnp.broadcast_to(dots, out_dot.shape)


def feed_both(normed_mid, cot, weights, rows=256):
    length, features = cot.shape
    half = weights.shape[1] // 3
    block = lambda width: pl.BlockSpec((rows, width), lambda i: (i, 0))
    return pl.pallas_call(
        feed_kernel,
        grid=(length // rows,),
        in_specs=[block(features), block(features), pl.BlockSpec(memory_space=pl.ANY)],
        out_specs=[block(half), block(2 * half), block(features), block(128)],
        out_shape=[
            jax.ShapeDtypeStruct((length, half), BF),
            jax.ShapeDtypeStruct((length, 2 * half), BF),
            jax.ShapeDtypeStruct((length, features), BF),
            jax.ShapeDtypeStruct((length, 128), F32),
        ],
        scratch_shapes=[pltpu.VMEM((3, features, half), BF), pltpu.SemaphoreType.DMA((3,))],
        compiler_params=pltpu.CompilerParams(vmem_limit_bytes=LIMIT),
        cost_estimate=pl.CostEstimate(
            flops=8 * length * features * half, bytes_accessed=12 * features * half, transcendentals=length * half
        ),
    )(normed_mid, cot, weights)


def per_segment(small, length):
    return jnp.broadcast_to(small[None], (length // SEGS,) + small.shape).reshape(length, small.shape[1])


def rows_dot(left, right):
    return lax.dot_general(left, right, (((0,), (0,)), ((), ())), preferred_element_type=F32)


def back_dot(left, right):
    return lax.dot_general(left, right, (((1,), (1,)), ((), ())), preferred_element_type=F32)


def dot(left, right):
    return jnp.dot(left, right, preferred_element_type=F32)


def shards(
    block_input, cotangent, segment_ids, pad_mask, state_init, window_init,
    recur_input, recur_gate, recur_output, feed_gate, feed_up, feed_down,
    conv_kernel, conv_bias, decay_gate, input_gate, decay_bias, input_bias, decay_logit, mixer_gain, feed_gain,
):
    own_width = block_input.shape[2]
    features = mixer_gain.shape[0]
    length = segment_ids.shape[1]
    taps = conv_kernel.shape[0]
    edge = taps - 1
    heads, head_width = decay_gate.shape[0], decay_gate.shape[2]
    rep = lax.axis_index("rep")
    seq, seqs = lax.axis_index("seq"), lax.axis_size("seq")
    at_start = seq == 0
    to_next = [(i, i + 1) for i in range(seqs - 1)]
    to_last = [(i + 1, i) for i in range(seqs - 1)]

    def weights(shard):
        return lax.all_gather(shard, ("seq", "row"), axis=0, tiled=True)

    def spread(partial_grad):
        return lax.psum_scatter(partial_grad, ("seq", "row"), scatter_dimension=0, tiled=True)

    def own_part(vector):
        return lax.dynamic_slice_in_dim(vector, rep * own_width, own_width, 0)[None]

    channels = conv_bias.shape[0]
    spare = -channels % 128

    def wide(values, fill=0):
        return jnp.pad(values, ((0, 0),) * (values.ndim - 1) + ((0, spare),), constant_values=fill)

    width = channels + spare

    x_low = by_step(block_input[0])
    cot_own = by_step(cotangent[0] * pad_mask[0][:, None].astype(BF))
    mixer_own, feed_own = own_part(mixer_gain), own_part(feed_gain)
    recur_shard = jnp.concatenate([wide(recur_input), wide(recur_gate), wide(recur_output)], axis=1)
    recur_shard, cot_own, x_low = after((recur_shard, cot_own, x_low))
    w_recur = weights(recur_shard)
    normed, s1 = exchange("first", (x_low, mixer_gain[None]), own_width)
    cot = lax.all_gather(cot_own, "rep", axis=1, tiled=True)
    w_input = w_recur[:, : 2 * width]

    left_ids = lax.ppermute(segment_ids[:, -edge:].astype(F32), "seq", to_next).astype(jnp.int32)
    left_ids = jnp.where(at_start, jnp.broadcast_to(segment_ids[:, :1], left_ids.shape), left_ids)
    ids_ext = jnp.concatenate([left_ids, segment_ids], axis=1)[0]
    same = [(ids_ext[edge - k : edge - k + length] == segment_ids[0]).astype(F32) for k in range(taps)]
    same = by_step(jnp.stack(same + [same[0]] * (8 - taps), axis=1))

    rate = 8.0 * jax.nn.softplus(decay_logit)
    params = wide(jnp.concatenate([conv_kernel, jnp.stack([conv_bias, decay_bias, input_bias])], axis=0))
    params = jnp.concatenate([params, wide(rate[None], 1)], axis=0)
    decay_w, input_w = block_diagonal(decay_gate, width), block_diagonal(input_gate, width)
    state_init = wide(state_init)

    projected = dot(normed, w_input)
    feed_shard, projected = after((jnp.concatenate([feed_gate, feed_up, feed_down], axis=1), projected))
    w_feed = weights(feed_shard)
    ends = projected[-edge * SEGS :, :width].astype(BF).reshape(edge, SEGS, width)
    left = lax.ppermute(ends[:, -1], "seq", to_next)
    left = jnp.where(at_start, wide(window_init[0]), left)
    prefix = jnp.concatenate([left[:, None], ends[:, :-1]], axis=1).reshape(edge * SEGS, -1)
    block_windows = ends[:, -1, :channels]

    gates, conv_out, decay_sig, gate_sig, retain, products, states, pre_a, pre_b, total = recur_forward(
        projected, same, prefix, params, decay_w, input_w
    )
    state_in = state_init
    for k in range(1, seqs):
        arriving = lax.ppermute(total[0:1] * state_in + total[1:2], "seq", to_next)
        state_in = jnp.where(seq == k, arriving, state_in)
    block_states = total[0:1] * state_in + total[1:2]
    carry = pre_a * state_in + pre_b

    normed_mid, s2, middle, hidden, gated = exchange(
        "norm", (states, products, gates, carry, w_recur, x_low, feed_gain[None]), own_width
    )
    normed_mid, cot = after((normed_mid, cot))
    feed_low, feed_grads, feed_part, mid_mean = feed_both(normed_mid, cot, w_feed)
    mid_mean = mid_mean[:, 0].reshape(-1, 128)

    half = feed_down.shape[1]
    down_grad = rows_dot(cot, feed_low).astype(BF)
    feed_grads, down_grad, mid_mean = after((feed_grads, down_grad, mid_mean))
    feed_all = rows_dot(normed_mid, feed_grads).astype(BF)
    feed_grads, feed_all, feed_part = after((feed_grads, feed_all, feed_part))
    feed_out = lax.psum_scatter(feed_part, "rep", scatter_dimension=1, tiled=True)
    feed_all = spread(feed_all)
    middle_low, middle_grad, feed_gain_own, feed_down_grad = exchange(
        "back",
        (feed_grads, w_feed, cot_own, middle, s2, mid_mean, feed_own, down_grad),
        own_width,
    )

    local, after_prod, branch_grad, enter_a, enter_b, back_total, branch_dot = recur_adjoint(
        middle_low, w_recur, projected, hidden, retain
    )
    output_all = rows_dot(middle_low, gated).astype(BF)
    local, output_all = after((local, output_all))
    entering = jnp.zeros_like(state_init)
    for k in range(1, seqs):
        arriving = lax.ppermute(back_total[0:1] * entering + back_total[1:2], "seq", to_last)
        entering = jnp.where(seq == seqs - 1 - k, arriving, entering)
    enter = enter_a * entering + enter_b
    decay_grad, input_grad_low, low_grad, low_dot, first, sums = recur_backward(
        local, after_prod, enter, hidden, carry, conv_out, decay_sig, gate_sig, retain, same, params, projected,
        decay_w, input_w,
    )
    owed = [first[0:8], first[8:24], first[24:48]]
    owed = [o.reshape(k + 1, SEGS, -1) for k, o in enumerate(owed)]
    ahead = prefix.reshape(edge, SEGS, -1).astype(F32)
    back_share = jnp.zeros_like(ahead)
    tap_extra = [jnp.zeros((width,), F32)]
    for k in range(1, taps):
        term = jnp.pad(owed[k - 1], ((edge - k, 0), (0, 0), (0, 0)))
        tap_extra.append(jnp.sum(term * ahead, axis=(0, 1)))
        back_share = back_share + params[k] * term
    from_right = lax.ppermute(back_share[:, 0], "seq", to_last)
    share = jnp.concatenate([back_share[:, 1:], from_right[:, None]], axis=1)
    low_grad = low_grad.reshape(length // SEGS, SEGS, -1)
    low_grad = jnp.concatenate([low_grad[:-edge], low_grad[-edge:] + share], axis=0).reshape(length, -1)
    share_dot = jnp.sum(share * ends.astype(F32), axis=2).reshape(-1)
    in_mean = low_dot[:, 0] + branch_dot[:, 0] + jnp.pad(share_dot, (length - share_dot.shape[0], 0))
    in_mean = in_mean.reshape(-1, 128)

    both_grads = jnp.concatenate([low_grad.astype(BF), branch_grad], axis=1)
    both_grads, in_mean, feed_all = after((both_grads, in_mean, feed_all))
    feed_gate_grad, feed_up_grad = feed_all[:, :half].astype(F32), feed_all[:, half:].astype(F32)
    conv_low = conv_out.astype(BF)
    decay_gate_grad = diagonal_rows(rows_dot(conv_low, decay_grad), heads, head_width)
    input_gate_grad = diagonal_rows(rows_dot(conv_low, input_grad_low), heads, head_width)
    sums = jnp.sum(sums.reshape(8, 8, -1), axis=1)
    conv_kernel_grad = sums[:taps] + jnp.stack(tap_extra)
    logit_grad = sums[7:, :channels] * 8.0 * jax.nn.sigmoid(decay_logit)
    vectors = jnp.concatenate([conv_kernel_grad, sums[4:7]], axis=0)[:, :channels]
    vectors = jnp.concatenate([vectors, logit_grad], axis=0)
    parts = (decay_gate_grad, input_gate_grad, vectors)
    small, counts = join_small(parts)
    recur_raw = rows_dot(normed, both_grads).astype(BF)
    recur_all = spread(recur_raw)
    both_grads, recur_raw, small, feed_out, feed_gate_grad, feed_up_grad = after(
        (both_grads, recur_raw, small, feed_out, feed_gate_grad, feed_up_grad)
    )
    input_grad, summed, gains, output_all = exchange(
        "last",
        (
            both_grads, w_recur, middle_grad, x_low, s1, in_mean, mixer_own,
            small, feed_gain_own, output_all,
        ),
        own_width,
    )
    input_grad, feed_out, recur_all = after((input_grad, feed_out, recur_all))
    recur_output_grad = output_all[:, :channels]
    recur_input_grad = recur_all[:, :channels].astype(F32)
    recur_gate_grad = recur_all[:, width : width + channels].astype(F32)
    input_grad = by_segment(input_grad)[None]
    block_output = by_segment((middle + feed_out.astype(F32)).astype(BF))[None]
    decay_gate_grad, input_gate_grad, vectors = split_small(summed, counts, parts)
    decay_gate_grad, input_gate_grad = (
        g[:, :head_width].reshape(decay_gate.shape) for g in (decay_gate_grad, input_gate_grad)
    )
    return (
        block_output, block_states[:, None, :channels], block_windows[None, None], input_grad,
        recur_input_grad, recur_gate_grad, recur_output_grad, feed_gate_grad, feed_up_grad, feed_down_grad,
        vectors[:taps], vectors[4], decay_gate_grad, input_gate_grad, vectors[5], vectors[6], vectors[7],
        gains[0], gains[1],
    )


def solution(mesh):
    tokens = P("row", "seq", "rep")
    matrix = P(("seq", "row"), "rep")
    in_specs = (
        tokens, tokens, P("row", "seq"), P("row", "seq"), P("row", "rep"), P("row", None, "rep"),
        matrix, matrix, matrix, matrix, matrix, matrix,
        P(None, "rep"), P("rep"), P("rep", None, None), P("rep", None, None), P("rep"), P("rep"), P("rep"), P(), P(),
    )
    out_specs = (
        tokens, tokens, P("row", "seq", None, "rep"), tokens,
        matrix, matrix, matrix, matrix, matrix, matrix,
        P(None, "rep"), P("rep"), P("rep", None, None), P("rep", None, None), P("rep"), P("rep"), P("rep"), P(), P(),
    )
    return jax.shard_map(shards, mesh=mesh, in_specs=in_specs, out_specs=out_specs, check_vma=False)
```

```python
from functools import partial as partial_call

import jax
import jax.numpy as jnp
from jax import lax
from jax.experimental import pallas as pl
from jax.experimental.pallas import tpu as pltpu
from jax.sharding import PartitionSpec as P

eps = 1e-06
SEGS = 8
BF = jnp.bfloat16
F32 = jnp.float32
LIMIT = 48 * 1024 * 1024


def gelu(v):
    return 0.5 * v * (1.0 + jnp.tanh(0.7978845608 * (v + 0.044715 * v * v * v)))


def gelu_both(v):
    square = v * v
    t = jnp.tanh(0.7978845608 * v * (1.0 + 0.044715 * square))
    value = 0.5 * v * (1.0 + t)
    slope = 0.5 * (1.0 + t) + 0.5 * v * (1.0 - t * t) * 0.7978845608 * (1.0 + 3 * 0.044715 * square)
    return value, slope


def one_minus_exp(y):
    series = y * (1 - y / 2 * (1 - y / 3 * (1 - y / 4 * (1 - y / 5 * (1 - y / 6 * (1 - y / 7))))))
    return jnp.where(y < 0.4, series, 1.0 - jnp.exp(-y))


after = lax.optimization_barrier


def join_small(parts):
    width = 256
    padded = []
    for part in parts:
        columns = -part.shape[1] % width
        padded.append(jnp.pad(part, ((0, 0), (0, columns))).reshape(-1, width))
    counts = [p.shape[0] for p in padded]
    spare = jnp.zeros((-sum(counts) % 16, width), F32)
    return jnp.concatenate(padded + [spare], axis=0).astype(BF), counts


def split_small(joined, counts, parts):
    out, start = [], 0
    for part, rows in zip(parts, counts):
        out.append(joined[start : start + rows].reshape(part.shape[0], -1)[:, : part.shape[1]])
        start += rows
    return out


def by_step(values):
    length, width = values.shape
    return values.reshape(SEGS, length // SEGS, width).transpose(1, 0, 2).reshape(length, width)


def by_segment(values):
    length, width = values.shape
    return values.reshape(length // SEGS, SEGS, width).transpose(1, 0, 2).reshape(length, width)


def block_diagonal(blocks, width):
    heads, wide = blocks.shape[0], blocks.shape[1]
    rows = [jnp.pad(blocks[h], ((0, 0), (h * wide, width - (h + 1) * wide))) for h in range(heads)]
    rows.append(jnp.zeros((width - heads * wide, width), blocks.dtype))
    return jnp.concatenate(rows, axis=0)


def diagonal_rows(dense, heads, wide):
    blocks = [dense[h * wide : (h + 1) * wide, h * wide : (h + 1) * wide] for h in range(heads)]
    return jnp.concatenate(blocks, axis=0)


def forward_kernel(
    conv_in, gate_branch, same, prefix, params, decay_w, input_w,
    out_gelu, out_conv, out_decay, out_gate, out_retain, out_prod, out_state, out_pre_a, out_pre_b, out_total,
    last_rows, prod_now, state_now, inflow_s,
):
    step = pl.program_id(0)
    rows = conv_in.shape[0]

    @pl.when(step == 0)
    def _():
        last_rows[...] = prefix[...].astype(F32)
        prod_now[...] = jnp.ones_like(prod_now)
        state_now[...] = jnp.zeros_like(state_now)

    out_gelu[...] = gelu(gate_branch[...])
    now = conv_in[...].astype(BF).astype(F32)
    ext = jnp.concatenate([last_rows[...], now], axis=0)
    same_all = same[...]
    total = params[4:5, :] + params[0:1, :] * now
    for k in (1, 2, 3):
        start = 24 - 8 * k
        total = total + params[k : k + 1, :] * ext[start : start + rows] * same_all[:, k : k + 1]
    last_rows[...] = now[rows - 24 :]
    out_conv[...] = total
    low = total.astype(BF)
    decay_sig = jax.nn.sigmoid(jnp.dot(low, decay_w[...], preferred_element_type=F32) + params[5:6, :])
    gate_sig = jax.nn.sigmoid(jnp.dot(low, input_w[...], preferred_element_type=F32) + params[6:7, :])
    out_decay[...] = decay_sig
    out_gate[...] = gate_sig
    expo = params[7:8, :] * decay_sig
    out_retain[...] = same_all[:, 1:2] * jnp.exp(-expo)
    inflow_s[...] = jnp.sqrt(one_minus_exp(2.0 * expo)) * gate_sig * total
    prod, state = prod_now[...], state_now[...]
    for t in range(rows // SEGS):
        at = slice(t * SEGS, (t + 1) * SEGS)
        keep = out_retain[at, :]
        prod = prod * keep
        state = state * keep + inflow_s[at, :]
        out_prod[at, :] = prod
        out_state[at, :] = state
    prod_now[...] = prod
    state_now[...] = state

    @pl.when(step == pl.num_programs(0) - 1)
    def _():
        carry_a = jnp.ones_like(prod[0:1])
        carry_b = jnp.zeros_like(carry_a)
        for s in range(SEGS):
            out_pre_a[s : s + 1, :] = carry_a
            out_pre_b[s : s + 1, :] = carry_b
            carry_b = prod[s : s + 1] * carry_b + state[s : s + 1]
            carry_a = prod[s : s + 1] * carry_a
        out_total[0:1, :] = carry_a
        out_total[1:2, :] = carry_b
        out_total[2:8, :] = jnp.zeros((6, carry_a.shape[1]), F32)


def recur_forward(conv_in, same, prefix, params, decay_w, input_w, rows=512):
    length, width = conv_in.shape[0], params.shape[1]
    block = pl.BlockSpec((rows, width), lambda i: (i, 0))
    fixed = lambda shape: pl.BlockSpec(shape, lambda i: (0, 0))
    big = jax.ShapeDtypeStruct((length, width), F32)
    small = jax.ShapeDtypeStruct((SEGS, width), F32)
    return pl.pallas_call(
        forward_kernel,
        grid=(length // rows,),
        in_specs=[
            block,
            pl.BlockSpec((rows, width), lambda i: (i, 1)),
            pl.BlockSpec((rows, 8), lambda i: (i, 0)),
            fixed((24, width)),
            fixed((8, width)),
            fixed((width, width)),
            fixed((width, width)),
        ],
        out_specs=[block] * 7 + [fixed((SEGS, width))] * 3,
        out_shape=[big] * 7 + [small] * 3,
        scratch_shapes=[
            pltpu.VMEM((24, width), F32),
            pltpu.VMEM((SEGS, width), F32),
            pltpu.VMEM((SEGS, width), F32),
            pltpu.VMEM((rows, width), F32),
        ],
        compiler_params=pltpu.CompilerParams(vmem_limit_bytes=LIMIT),
        cost_estimate=pl.CostEstimate(flops=length * width, bytes_accessed=4 * length * width, transcendentals=0),
    )(conv_in, conv_in, same, prefix, params, decay_w, input_w)


def adjoint_kernel(
    middle_low, weight, gate_branch, hidden, retain,
    out_local, out_after, out_branch, out_pre_a, out_pre_b, out_total, out_dot,
    local_now, after_now, next_retain, grad_s,
):
    step = pl.program_id(0)
    rows = hidden.shape[0]

    @pl.when(step == 0)
    def _():
        local_now[...] = jnp.zeros_like(local_now)
        after_now[...] = jnp.ones_like(after_now)
        next_retain[...] = jnp.ones_like(next_retain)

    value, slope = gelu_both(gate_branch[...])
    upstream = jnp.dot(middle_low[...], weight[...], preferred_element_type=F32)
    grad_s[...] = upstream * value
    branch = upstream * hidden[...] * slope
    out_branch[...] = branch.astype(BF)
    out_dot[...] = jnp.broadcast_to(jnp.sum(branch * gate_branch[...], axis=1, keepdims=True), out_dot.shape)
    local, after, keep = local_now[...], after_now[...], next_retain[...]
    for t in reversed(range(rows // SEGS)):
        at = slice(t * SEGS, (t + 1) * SEGS)
        local = grad_s[at, :] + keep * local
        after = keep * after
        out_local[at, :] = local
        out_after[at, :] = after
        keep = retain[at, :]
    local_now[...] = local
    after_now[...] = after
    next_retain[...] = keep

    @pl.when(step == pl.num_programs(0) - 1)
    def _():
        carry_a = jnp.ones_like(local[0:1])
        carry_b = jnp.zeros_like(carry_a)
        for s in reversed(range(SEGS)):
            out_pre_a[s : s + 1, :] = carry_a
            out_pre_b[s : s + 1, :] = carry_b
            carry_b = keep[s : s + 1] * (local[s : s + 1] + after[s : s + 1] * carry_b)
            carry_a = keep[s : s + 1] * after[s : s + 1] * carry_a
        out_total[0:1, :] = carry_a
        out_total[1:2, :] = carry_b
        out_total[2:8, :] = jnp.zeros((6, carry_a.shape[1]), F32)


def recur_adjoint(middle_low, w_recur, gate_branch, hidden, retain, rows=512):
    length, width = hidden.shape
    features = middle_low.shape[1]
    last = length // rows - 1
    block = pl.BlockSpec((rows, width), lambda i: (last - i, 0))
    second = pl.BlockSpec((rows, width), lambda i: (last - i, 1))
    fixed = lambda shape: pl.BlockSpec(shape, lambda i: (0, 0))
    big = jax.ShapeDtypeStruct((length, width), F32)
    small = jax.ShapeDtypeStruct((SEGS, width), F32)
    return pl.pallas_call(
        adjoint_kernel,
        grid=(length // rows,),
        in_specs=[
            pl.BlockSpec((rows, features), lambda i: (last - i, 0)),
            pl.BlockSpec((features, width), lambda i: (0, 2), pipeline_mode=pl.Buffered(1)),
            second, block, block,
        ],
        out_specs=[block] * 3 + [fixed((SEGS, width))] * 3 + [pl.BlockSpec((rows, 128), lambda i: (last - i, 0))],
        out_shape=[big, big, jax.ShapeDtypeStruct((length, width), BF)]
        + [small] * 3
        + [jax.ShapeDtypeStruct((length, 128), F32)],
        scratch_shapes=[pltpu.VMEM((SEGS, width), F32)] * 3 + [pltpu.VMEM((rows, width), F32)],
        compiler_params=pltpu.CompilerParams(vmem_limit_bytes=LIMIT),
        cost_estimate=pl.CostEstimate(flops=length * width, bytes_accessed=4 * length * width, transcendentals=0),
    )(middle_low, w_recur, gate_branch, hidden, retain)


def backward_kernel(
    local, after, enter, hidden, hidden_before, carry, conv_out, decay_sig, gate_sig, retain, same, params, conv_in,
    decay_w, input_w,
    out_decay, out_input, out_low, out_dot, out_first, out_sums,
    next_one, next_two, next_three,
):
    step = pl.program_id(0)
    blocks = pl.num_programs(0)
    rows = local.shape[0]
    width = local.shape[1]

    @pl.when(step == 0)
    def _():
        for held in (next_one, next_two, next_three):
            held[...] = jnp.zeros_like(held)
        out_sums[...] = jnp.zeros_like(out_sums)

    def per_step(small):
        return jnp.broadcast_to(small[None], (rows // SEGS, SEGS, width)).reshape(rows, width)

    def sums(values):
        return jnp.sum(values.reshape(rows // SEGS, SEGS, width), axis=0)

    adjoint = local[...] + after[...] * per_step(enter[...])
    ahead = jnp.where(step == blocks - 1, carry[...], hidden_before[...])
    hidden_prev = jnp.concatenate([ahead, hidden[...][: rows - SEGS]], axis=0)
    conv, decay, gate = conv_out[...], decay_sig[...], gate_sig[...]
    rate = params[7:8, :]
    expo = rate * decay
    inner = one_minus_exp(2.0 * expo)
    root = jnp.sqrt(inner)
    expo_grad = adjoint * (gate * conv * (1.0 - inner) / root - retain[...] * hidden_prev)
    decay_grad = (expo_grad * rate * decay * (1.0 - decay)).astype(BF)
    input_grad = (adjoint * root * conv * gate * (1.0 - gate)).astype(BF)
    out_decay[...] = decay_grad
    out_input[...] = input_grad
    dims = (((1,), (1,)), ((), ()))
    conv_grad = (
        adjoint * root * gate
        + lax.dot_general(decay_grad, decay_w[...], dims, preferred_element_type=F32)
        + lax.dot_general(input_grad, input_w[...], dims, preferred_element_type=F32)
    )
    same_all = same[...]
    now = conv_in[...].astype(BF).astype(F32)
    low = params[0:1, :] * conv_grad
    out_sums[0:8, :] += sums(conv_grad * now)
    for k, held in ((1, next_one), (2, next_two), (3, next_three)):
        masked = conv_grad * same_all[:, k : k + 1]
        moved = jnp.concatenate([masked[8 * k :], held[...]], axis=0)
        held[...] = masked[: 8 * k]
        low = low + params[k : k + 1, :] * moved
        out_sums[8 * k : 8 * k + 8, :] += sums(moved * now)
    out_low[...] = low
    out_dot[...] = jnp.broadcast_to(jnp.sum(low * now, axis=1, keepdims=True), out_dot.shape)
    out_sums[32:40, :] += sums(conv_grad)
    out_sums[40:48, :] += sums(decay_grad.astype(F32))
    out_sums[48:56, :] += sums(input_grad.astype(F32))
    out_sums[56:64, :] += sums(expo_grad * decay)

    @pl.when(step == blocks - 1)
    def _():
        out_first[0:8, :] = next_one[...]
        out_first[8:24, :] = next_two[...]
        out_first[24:48, :] = next_three[...]


def recur_backward(
    local, after, enter, hidden, carry, conv_out, decay_sig, gate_sig, retain, same, params, conv_in, decay_w, input_w,
    rows=512,
):
    length, width = local.shape
    last = length // rows - 1
    block = pl.BlockSpec((rows, width), lambda i: (last - i, 0))
    fixed = lambda shape: pl.BlockSpec(shape, lambda i: (0, 0))
    steps = rows // SEGS
    before = pl.BlockSpec((SEGS, width), lambda i: (jnp.maximum((last - i) * steps - 1, 0), 0))
    return pl.pallas_call(
        backward_kernel,
        grid=(length // rows,),
        in_specs=[
            block, block, fixed((SEGS, width)), block, before, fixed((SEGS, width)), block, block, block, block,
            pl.BlockSpec((rows, 8), lambda i: (last - i, 0)),
            fixed((8, width)), block, fixed((width, width)), fixed((width, width)),
        ],
        out_specs=[
            block, block, block, pl.BlockSpec((rows, 128), lambda i: (last - i, 0)), fixed((48, width)),
            fixed((64, width)),
        ],
        out_shape=[
            jax.ShapeDtypeStruct((length, width), BF),
            jax.ShapeDtypeStruct((length, width), BF),
            jax.ShapeDtypeStruct((length, width), F32),
            jax.ShapeDtypeStruct((length, 128), F32),
            jax.ShapeDtypeStruct((48, width), F32),
            jax.ShapeDtypeStruct((64, width), F32),
        ],
        scratch_shapes=[
            pltpu.VMEM((8, width), F32),
            pltpu.VMEM((16, width), F32),
            pltpu.VMEM((24, width), F32),
        ],
        compiler_params=pltpu.CompilerParams(vmem_limit_bytes=LIMIT),
        cost_estimate=pl.CostEstimate(flops=length * width, bytes_accessed=4 * length * width, transcendentals=0),
    )(
        local, after, enter, hidden, hidden, carry, conv_out, decay_sig, gate_sig, retain, same, params, conv_in,
        decay_w, input_w,
    )


class Halving:
    def __init__(self, source, keep, arrivals, sends, receives, loads):
        self.source, self.keep, self.arrivals = source, keep, arrivals
        self.sends, self.receives, self.loads = sends, receives, loads
        rows, seqs = lax.axis_size("row"), lax.axis_size("seq")
        self.total = rows * seqs
        self.place = lax.axis_index("seq") * rows + lax.axis_index("row")
        self.stages = halving_stages()
        self.height = source.shape[0] // self.total

    def own_bit(self, p):
        axis, step = self.stages[p]
        return lax.rem(lax.axis_index(axis) // step, 2)

    def block(self, p, mine, j):
        bit = self.own_bit(p) if mine else 1 - self.own_bit(p)
        return lax.rem(self.place, 2**p) + bit * 2**p + j * 2 ** (p + 1)

    def many(self, p):
        return self.total // 2 ** (p + 1)

    def held(self, p, mine, j):
        return self.keep.at[self.block(p, mine, j) // 2]

    def rows_of(self, block):
        return self.source.at[pl.ds(pl.multiple_of(block * self.height, self.height), self.height)]

    def moves(self, p):
        axis, step = self.stages[p]
        partner = lax.axis_index(axis) + step - 2 * step * self.own_bit(p)
        start = self.total - self.total // 2**p
        copies = []
        for j in range(self.many(p)):
            copies.append(
                pltpu.make_async_remote_copy(
                    src_ref=self.held(p, False, j) if p else self.rows_of(self.block(0, False, j)),
                    dst_ref=self.arrivals.at[start + j],
                    send_sem=self.sends.at[start + j],
                    recv_sem=self.receives.at[start + j],
                    device_id={axis: partner},
                    device_id_type=pl.DeviceIdType.MESH,
                )
            )
        return copies

    def local(self):
        return [
            pltpu.make_async_copy(self.rows_of(self.block(0, True, j)), self.keep.at[j], self.loads.at[j])
            for j in range(self.many(0))
        ]

    def begin(self):
        for copy in self.moves(0) + self.local():
            copy.start()

    def stage(self, p, out=None):
        if p == 0:
            for copy in self.local():
                copy.wait()
        for copy in self.moves(p):
            copy.wait_recv()
        start = self.total - self.total // 2**p
        piece = 32
        for j in range(self.many(p)):
            slot = self.block(p, True, j) // 2

            def add(i, _, j=j, slot=slot):
                at = pl.ds(pl.multiple_of(i * piece, piece), piece)
                added = self.keep[slot, at, :].astype(F32) + self.arrivals[start + j, at, :].astype(F32)
                if out is None:
                    self.keep[slot, at, :] = added.astype(BF)
                else:
                    out[at, :] = added
                return 0

            lax.fori_loop(0, self.height // piece, add, 0)
        if out is None:
            for copy in self.moves(p + 1):
                copy.start()

    def settle(self):
        for p in range(len(self.stages)):
            for copy in self.moves(p):
                copy.wait_send()

    def partners(self):
        found = []
        for p, (axis, step) in enumerate(self.stages):
            found.append({axis: lax.axis_index(axis) + step - 2 * step * self.own_bit(p)})
        return found


def halving_stages():
    stages = []
    for axis in ("row", "seq"):
        step = 1
        while step < lax.axis_size(axis):
            stages.append((axis, step))
            step *= 2
    return stages


def halving_scratch(shape):
    total = lax.axis_size("row") * lax.axis_size("seq")
    height = shape[0] // total
    return [
        pltpu.VMEM((total // 2, height, shape[1]), BF),
        pltpu.VMEM((total - 1, height, shape[1]), BF),
        pltpu.SemaphoreType.DMA((total - 1,)),
        pltpu.SemaphoreType.DMA((total - 1,)),
        pltpu.SemaphoreType.DMA((total // 2,)),
    ]


def exchange_kernel(count, chunks, mode, *refs):
    backward, summing, gathering = mode in ("back", "last"), mode != "first", mode != "last"
    refs = list(refs)
    take = lambda number: [refs.pop(0) for _ in range(number)]
    if mode == "first":
        residual, gain, out, out_scale, gathered = take(5)
    elif mode == "norm":
        states, products, gates, carry, weight, residual, gain, out, out_scale, out_own, out_hidden, out_gated = take(12)
        (gathered,) = take(1)
    elif mode == "back":
        grads, weight, residual, middle, scale, mean, gain, spread_in, out, out_own, out_gain, out_spread = take(12)
        gathered = out
        halving = Halving(spread_in, *take(5))
    else:
        grads, weight, residual, middle, scale, mean, gain, small, feed_sums, spread_in = take(10)
        out_own, out_small, out_gains, out_spread = take(4)
        halving = Halving(spread_in, *take(5))
        out_gain, gain_own, gain_row, gain_seq, small_held, small_got, gain_sems, small_sems = take(8)
    if backward:
        mean_got, mean_sum, mean_sems = take(3)
    if summing:
        partial, held_weight, right, left, total, weight_sem, sum_send, sum_recv = take(8)
    if gathering:
        all_send, all_recv = take(2)
    me = lax.axis_index("rep")
    length, width = residual.shape
    rows = length // chunks
    last = count - 1

    if summing:
        start = weight.shape[1] - held_weight.shape[1] if mode == "norm" else 0
        load = pltpu.make_async_copy(weight.at[:, pl.ds(start, held_weight.shape[1])], held_weight, weight_sem)
        load.start()
    barrier = pltpu.get_barrier_semaphore()

    def greet(device):
        pl.semaphore_signal(barrier, inc=1, device_id=device, device_id_type=pl.DeviceIdType.MESH)

    if backward:
        axes = ("rep",) if mode == "back" else ("row", "seq", "rep")
        devices = halving.partners() if mode == "back" else []
        for axis in axes:
            for d in range(1, lax.axis_size(axis)):
                devices.append({axis: lax.rem(lax.axis_index(axis) + d, lax.axis_size(axis))})
        for device in devices:
            greet(device)
        pl.semaphore_wait(barrier, len(devices))
        halving.begin()
    else:

        @pl.when(me > 0)
        def _():
            greet({"rep": me - 1})

        @pl.when(me < last)
        def _():
            greet({"rep": me + 1})

        inner = jnp.logical_and(me > 0, me < last)

        @pl.when(inner)
        def _():
            pl.semaphore_wait(barrier, 2)

        @pl.when(jnp.logical_not(inner))
        def _():
            pl.semaphore_wait(barrier, 1)

    def to_peers(axis, source, target, sems):
        copies = []
        for d in range(1, lax.axis_size(axis)):
            peer = lax.rem(lax.axis_index(axis) + d, lax.axis_size(axis))
            copies.append(
                pltpu.make_async_remote_copy(
                    src_ref=source,
                    dst_ref=target(d),
                    send_sem=sems.at[0, d],
                    recv_sem=sems.at[1, d],
                    device_id={axis: peer},
                    device_id_type=pl.DeviceIdType.MESH,
                )
            )
        return copies

    if backward:
        mean_moves = to_peers("rep", mean, lambda d: mean_got.at[d], mean_sems)
        for copy in mean_moves:
            copy.start()

    def mean_column(c):
        per = 128 // rows
        line = jnp.broadcast_to(mean_sum[pl.ds(c // per, 1), :], (rows, 128))
        lane = lax.broadcasted_iota(jnp.int32, (rows, 128), 1)
        row = lax.broadcasted_iota(jnp.int32, (rows, 128), 0) + lax.rem(c, per) * rows
        return jnp.sum(jnp.where(lane == row, line, 0.0), axis=1, keepdims=True)

    if mode == "last":
        small_moves = [
            pltpu.make_async_remote_copy(
                src_ref=small_held.at[p],
                dst_ref=small_got.at[p],
                send_sem=small_sems.at[0, p],
                recv_sem=small_sems.at[1, p],
                device_id=partner,
                device_id_type=pl.DeviceIdType.MESH,
            )
            for p, partner in enumerate(halving.partners())
        ]
        gain_rows = to_peers("row", gain_own, lambda d: gain_row.at[d], gain_sems.at[0])
        gain_seqs = to_peers("seq", gain_row.at[0], lambda d: gain_seq.at[d], gain_sems.at[1])
        own_gains = out_gains.at[:, pl.ds(pl.multiple_of(me * width, width), width)]
        gain_reps = to_peers("rep", gain_seq.at[0], lambda d: own_gains, gain_sems.at[2])
        small_held[0] = small[...]
        small_moves[0].start()

    def small_stage(p):
        small_moves[p].wait_recv()
        added = small_held[p].astype(F32) + small_got[p].astype(F32)
        if p + 1 < len(small_moves):
            small_held[p + 1] = added.astype(BF)
            small_moves[p + 1].start()
        else:
            out_small[...] = added

    if backward:
        out_gain[...] = jnp.zeros_like(out_gain)
    if summing:
        load.wait()

    def at(c):
        return pl.ds(pl.multiple_of(c * rows, rows), rows)

    def columns(device):
        return pl.ds(pl.multiple_of(device * width, width), width)

    def sum_copy(side, slot, c):
        buffer, to = ((right, me + 1), (left, me - 1))[side]
        return pltpu.make_async_remote_copy(
            src_ref=buffer.at[slot, at(c)],
            dst_ref=buffer.at[slot - 1, at(c)],
            send_sem=sum_send.at[side, slot, c],
            recv_sem=sum_recv.at[side, slot - 1, c],
            device_id={"rep": to},
            device_id_type=pl.DeviceIdType.MESH,
        )

    def sum_arrived(side, slot, c):
        buffer, sender = ((right, me - 1), (left, me + 1))[side]
        pltpu.make_async_remote_copy(
            src_ref=buffer.at[slot, at(c)],
            dst_ref=buffer.at[slot, at(c)],
            send_sem=sum_send.at[side, slot, c],
            recv_sem=sum_recv.at[side, slot, c],
            device_id={"rep": sender},
            device_id_type=pl.DeviceIdType.MESH,
        ).wait_recv()

    def all_copy(side, far, c):
        source, to = ((me - far, me + 1), (me + far, me - 1))[side]
        piece = gathered.at[at(c), columns(source)]
        return pltpu.make_async_remote_copy(
            src_ref=piece,
            dst_ref=piece,
            send_sem=all_send.at[side, far, c],
            recv_sem=all_recv.at[side, far + 1, c],
            device_id={"rep": to},
            device_id_type=pl.DeviceIdType.MESH,
        )

    def all_arrived(side, far, c):
        source, sender = ((me - far, me - 1), (me + far, me + 1))[side]
        piece = gathered.at[at(c), columns(source)]
        pltpu.make_async_remote_copy(
            src_ref=piece,
            dst_ref=piece,
            send_sem=all_send.at[side, far, c],
            recv_sem=all_recv.at[side, far, c],
            device_id={"rep": sender},
            device_id_type=pl.DeviceIdType.MESH,
        ).wait_recv()

    def inside(c):
        return jnp.logical_and(c >= 0, c < chunks)

    stride = 1

    def produce(c):
        some = pl.ds(pl.multiple_of(c * rows, stride * rows), stride * rows)
        if mode == "norm":
            wide = (stride * rows // SEGS, SEGS, carry.shape[1])
            enter = jnp.broadcast_to(carry[...][None], wide).reshape(stride * rows, carry.shape[1])
            hidden = states[some, :] + products[some, :] * enter
            low = (hidden * gates[some, :]).astype(BF)
            out_hidden[some, :] = hidden
            out_gated[some, :] = low
        else:
            low = grads[some, :]
        partial[some, :] = back_dot(low, held_weight[...]).astype(BF)

    def tick(now, _):
        if backward:

            @pl.when(now == last)
            def _():
                for copy in mean_moves:
                    copy.wait_recv()
                added = mean[...]
                for d in range(1, count):
                    added = added + mean_got[d]
                mean_sum[...] = added * (1.0 / (count * width))

            for p, when in ((0, 2), (1, 15 if mode == "back" else 13)):
                if p < len(halving.stages) - 1:

                    @pl.when(now == when)
                    def _(p=p):
                        halving.stage(p)

        if mode == "last":
            for p, when in ((0, 1), (1, 8)):
                if p < len(small_moves) - 1:

                    @pl.when(now == when)
                    def _(p=p):
                        small_stage(p)

        if summing:

            @pl.when(jnp.logical_and(now < chunks, lax.rem(now, stride) == 0))
            def _():
                produce(now)

        for side in (0, 1) if summing else ():
            place = (me, last - me)[side]
            c = now - place
            for slot in range(last, 0, -1):

                @pl.when(jnp.logical_and(inside(c), place + slot <= last))
                def _(side=side, place=place, c=c, slot=slot):
                    buffer = (right, left)[side]
                    target = (me + slot, me - slot)[side]

                    @pl.when(place > 0)
                    def _():
                        sum_arrived(side, slot, c)
                        added = buffer[slot, at(c), :].astype(F32) + partial[at(c), columns(target)].astype(F32)
                        buffer[slot, at(c), :] = added.astype(BF)

                    @pl.when(place == 0)
                    def _():
                        buffer[slot, at(c), :] = partial[at(c), columns(target)]

                    sum_copy(side, slot, c).start()

        def finish(done):
            total[...] = partial[at(done), columns(me)].astype(F32)

            @pl.when(me > 0)
            def _():
                sum_arrived(0, 0, done)
                total[...] += right[0, at(done), :].astype(F32)

            @pl.when(me < last)
            def _():
                sum_arrived(1, 0, done)
                total[...] += left[0, at(done), :].astype(F32)

            if backward:
                size = scale[at(done), 0:1]
                normal = middle[at(done), :].astype(F32) * size
                summed = total[...]
                own = residual[at(done), :].astype(F32) + size * (
                    summed * gain[...] - normal * mean_column(done)
                )
                out_gain[...] += jnp.sum((summed * normal).reshape(rows // 8, 8, width), axis=0)
            else:
                own = residual[at(done), :].astype(F32) + total[...]
            out_own[at(done), :] = own.astype(out_own.dtype)
            if gathering:
                gathered[at(done), columns(me)] = own.astype(BF)

        done = now - last if summing else now

        @pl.when(inside(done))
        def _():
            if summing:
                finish(done)
            else:
                gathered[at(done), columns(me)] = residual[at(done), :]
            if gathering:

                @pl.when(me < last)
                def _():
                    all_copy(0, 0, done).start()

                @pl.when(me > 0)
                def _():
                    all_copy(1, 0, done).start()

        for far in range(1, count) if gathering else ():
            c = done - far
            for side in (0, 1):
                place = (me, last - me)[side]

                @pl.when(jnp.logical_and(inside(c), place >= far))
                def _(side=side, place=place, c=c, far=far):
                    all_arrived(side, far, c)

                    @pl.when(place < last)
                    def _():
                        all_copy(side, far, c).start()

        if not backward:
            full = done - last

            @pl.when(inside(full))
            def _():
                values = gathered[at(full), :].astype(F32)
                size = lax.rsqrt(jnp.mean(values * values, axis=1, keepdims=True) + eps)
                out[at(full), :] = (values * size * gain[...]).astype(BF)
                out_scale[at(full), :] = jnp.broadcast_to(size, (rows, 128))

        return 0

    lax.fori_loop(0, chunks + last * (summing + gathering), tick, 0)

    def settle(c, _):
        for side in (0, 1):
            place = (me, last - me)[side]
            for slot in range(1, count) if summing else ():

                @pl.when(place + slot <= last)
                def _(side=side, slot=slot):
                    sum_copy(side, slot, c).wait_send()

            for far in range(0, last) if gathering else ():

                @pl.when(jnp.logical_and(place < last, place >= far))
                def _(side=side, far=far):
                    all_copy(side, far, c).wait_send()

        return 0

    if backward:
        for p in range(2, len(halving.stages) - 1):
            halving.stage(p)
        halving.stage(len(halving.stages) - 1, out_spread)
        halving.settle()
        for copy in mean_moves:
            copy.wait_send()

    if mode == "last":
        mixer_sum = jnp.sum(out_gain[...], axis=0, keepdims=True)
        feed_sum = jnp.sum(feed_sums[...], axis=0, keepdims=True)
        gain_own[...] = jnp.concatenate([mixer_sum, feed_sum, jnp.zeros((6, width), F32)], axis=0)
        for copy in gain_rows:
            copy.start()
        for p in range(min(2, len(small_moves) - 1), len(small_moves)):
            small_stage(p)
        for copy in gain_rows:
            copy.wait_recv()
        added = gain_own[...]
        for d in range(1, lax.axis_size("row")):
            added = added + gain_row[d]
        gain_row[0] = added
        for copy in gain_seqs:
            copy.start()
        for copy in gain_seqs:
            copy.wait_recv()
        added = gain_row[0]
        for d in range(1, lax.axis_size("seq")):
            added = added + gain_seq[d]
        gain_seq[0] = added
        for copy in gain_reps:
            copy.start()
        own_gains[...] = added
        for copy in gain_reps:
            copy.wait_recv()
        for copy in small_moves + gain_rows + gain_seqs + gain_reps:
            copy.wait_send()

    lax.fori_loop(0, chunks, settle, 0)


def exchange(mode, operands, width, chunks=16):
    count = lax.axis_size("rep")
    length = operands[0].shape[0]
    features = count * width
    backward, summing, gathering = mode in ("back", "last"), mode != "first", mode != "last"
    vmem = pl.BlockSpec(memory_space=pltpu.VMEM)
    in_specs = [vmem] * len(operands)
    sems = [pltpu.SemaphoreType.DMA((2, count, chunks)), pltpu.SemaphoreType.DMA((2, count, chunks))]
    full, own = jax.ShapeDtypeStruct((length, features), BF), jax.ShapeDtypeStruct((length, width), F32)
    scale, gain = jax.ShapeDtypeStruct((length, 128), F32), jax.ShapeDtypeStruct((8, width), F32)
    if mode == "first":
        out_shape = [full, scale]
    elif mode == "norm":
        hidden = operands[0].shape
        out_shape = [full, scale, own, jax.ShapeDtypeStruct(hidden, F32), jax.ShapeDtypeStruct(hidden, BF)]
    elif mode == "back":
        out_shape = [full, own, gain]
    else:
        small = operands[7].shape
        out_shape = [
            jax.ShapeDtypeStruct((length, width), BF),
            jax.ShapeDtypeStruct(small, F32),
            jax.ShapeDtypeStruct((8, features), F32),
        ]
    if backward:
        spread = operands[-1].shape
        devices = lax.axis_size("row") * lax.axis_size("seq")
        out_shape.append(jax.ShapeDtypeStruct((spread[0] // devices, spread[1]), F32))
    scratch = [] if backward else [pltpu.VMEM((length, features), BF)]
    if backward:
        in_specs[-1] = pl.BlockSpec(memory_space=pl.ANY)
        scratch += halving_scratch(operands[-1].shape)
    if mode == "last":
        row, seq, stages = lax.axis_size("row"), lax.axis_size("seq"), len(halving_stages())
        most = max(row, seq, count)
        scratch += [
            pltpu.VMEM((8, width), F32),
            pltpu.VMEM((8, width), F32),
            pltpu.VMEM((row, 8, width), F32),
            pltpu.VMEM((seq, 8, width), F32),
            pltpu.VMEM((stages,) + small, BF),
            pltpu.VMEM((stages,) + small, BF),
            pltpu.SemaphoreType.DMA((3, 2, most)),
            pltpu.SemaphoreType.DMA((2, stages)),
        ]
    if backward:
        packed = (length // 128, 128)
        scratch += [
            pltpu.VMEM((count,) + packed, F32), pltpu.VMEM(packed, F32), pltpu.SemaphoreType.DMA((2, count)),
        ]
    if summing:
        in_specs[4 if mode == "norm" else 1] = pl.BlockSpec(memory_space=pl.ANY)
        scratch += [
            pltpu.VMEM((length, features), BF),
            pltpu.VMEM((features, operands[0].shape[1]), BF),
            pltpu.VMEM((count, length, width), BF),
            pltpu.VMEM((count, length, width), BF),
            pltpu.VMEM((length // chunks, width), F32),
            pltpu.SemaphoreType.DMA,
        ] + sems
    if gathering:
        scratch += sems
    return pl.pallas_call(
        partial_call(exchange_kernel, count, chunks, mode),
        in_specs=in_specs,
        out_specs=[vmem] * len(out_shape),
        out_shape=out_shape,
        scratch_shapes=scratch,
        compiler_params=pltpu.CompilerParams(
            collective_id=("first", "norm", "back", "last").index(mode),
            has_side_effects=True,
            vmem_limit_bytes=LIMIT + (8 * 1024 * 1024 if mode == "back" else 0),
        ),
        cost_estimate=pl.CostEstimate(
            flops=10 * length * features, bytes_accessed=160 * length * features, transcendentals=0
        ),
    )(*operands)


def feed_kernel(normed_mid, cot, weights, out_low, out_grads, out_part, out_dot, held, sems):
    half = out_low.shape[1]
    step = pl.program_id(0)
    loads = [
        pltpu.make_async_copy(weights.at[:, pl.ds(k * half, half)], held.at[k], sems.at[k]) for k in range(3)
    ]

    @pl.when(step == 0)
    def _():
        for load in loads:
            load.start()

    def weight(k):
        @pl.when(step == 0)
        def _():
            loads[k].wait()

        return held[k]

    gate_pre = jnp.dot(normed_mid[...], weight(0), preferred_element_type=F32)
    up_pre = jnp.dot(normed_mid[...], weight(1), preferred_element_type=F32)
    value, slope = gelu_both(gate_pre)
    low = (value * up_pre).astype(BF)
    out_low[...] = low
    upstream = jnp.dot(cot[...], weight(2), preferred_element_type=F32)
    out_part[...] = back_dot(low, held[2]).astype(BF)
    gate_grad, up_grad = upstream * up_pre * slope, upstream * value
    out_grads[:, :half] = gate_grad.astype(BF)
    out_grads[:, half:] = up_grad.astype(BF)
    dots = jnp.sum(gate_grad * gate_pre + up_grad * up_pre, axis=1, keepdims=True)
    out_dot[...] = jnp.broadcast_to(dots, out_dot.shape)


def feed_both(normed_mid, cot, weights, rows=256):
    length, features = cot.shape
    half = weights.shape[1] // 3
    block = lambda width: pl.BlockSpec((rows, width), lambda i: (i, 0))
    return pl.pallas_call(
        feed_kernel,
        grid=(length // rows,),
        in_specs=[block(features), block(features), pl.BlockSpec(memory_space=pl.ANY)],
        out_specs=[block(half), block(2 * half), block(features), block(128)],
        out_shape=[
            jax.ShapeDtypeStruct((length, half), BF),
            jax.ShapeDtypeStruct((length, 2 * half), BF),
            jax.ShapeDtypeStruct((length, features), BF),
            jax.ShapeDtypeStruct((length, 128), F32),
        ],
        scratch_shapes=[pltpu.VMEM((3, features, half), BF), pltpu.SemaphoreType.DMA((3,))],
        compiler_params=pltpu.CompilerParams(vmem_limit_bytes=LIMIT),
        cost_estimate=pl.CostEstimate(
            flops=8 * length * features * half, bytes_accessed=12 * features * half, transcendentals=length * half
        ),
    )(normed_mid, cot, weights)


def per_segment(small, length):
    return jnp.broadcast_to(small[None], (length // SEGS,) + small.shape).reshape(length, small.shape[1])


def rows_dot(left, right):
    return lax.dot_general(left, right, (((0,), (0,)), ((), ())), preferred_element_type=F32)


def back_dot(left, right):
    return lax.dot_general(left, right, (((1,), (1,)), ((), ())), preferred_element_type=F32)


def dot(left, right):
    return jnp.dot(left, right, preferred_element_type=F32)


def shards(
    block_input, cotangent, segment_ids, pad_mask, state_init, window_init,
    recur_input, recur_gate, recur_output, feed_gate, feed_up, feed_down,
    conv_kernel, conv_bias, decay_gate, input_gate, decay_bias, input_bias, decay_logit, mixer_gain, feed_gain,
):
    own_width = block_input.shape[2]
    features = mixer_gain.shape[0]
    length = segment_ids.shape[1]
    taps = conv_kernel.shape[0]
    edge = taps - 1
    heads, head_width = decay_gate.shape[0], decay_gate.shape[2]
    rep = lax.axis_index("rep")
    seq, seqs = lax.axis_index("seq"), lax.axis_size("seq")
    at_start = seq == 0
    to_next = [(i, i + 1) for i in range(seqs - 1)]
    to_last = [(i + 1, i) for i in range(seqs - 1)]

    def weights(shard):
        return lax.all_gather(shard, ("seq", "row"), axis=0, tiled=True)

    def spread(partial_grad):
        return lax.psum_scatter(partial_grad, ("seq", "row"), scatter_dimension=0, tiled=True)

    def own_part(vector):
        return lax.dynamic_slice_in_dim(vector, rep * own_width, own_width, 0)[None]

    channels = conv_bias.shape[0]
    spare = -channels % 128

    def wide(values, fill=0):
        return jnp.pad(values, ((0, 0),) * (values.ndim - 1) + ((0, spare),), constant_values=fill)

    width = channels + spare

    x_low = by_step(block_input[0])
    cot_own = by_step(cotangent[0] * pad_mask[0][:, None].astype(BF))
    mixer_own, feed_own = own_part(mixer_gain), own_part(feed_gain)
    recur_shard = jnp.concatenate([wide(recur_input), wide(recur_gate), wide(recur_output)], axis=1)
    recur_shard, cot_own, x_low = after((recur_shard, cot_own, x_low))
    w_recur = weights(recur_shard)
    normed, s1 = exchange("first", (x_low, mixer_gain[None]), own_width)
    cot = lax.all_gather(cot_own, "rep", axis=1, tiled=True)
    w_input = w_recur[:, : 2 * width]

    left_ids = lax.ppermute(segment_ids[:, -edge:].astype(F32), "seq", to_next).astype(jnp.int32)
    left_ids = jnp.where(at_start, jnp.broadcast_to(segment_ids[:, :1], left_ids.shape), left_ids)
    ids_ext = jnp.concatenate([left_ids, segment_ids], axis=1)[0]
    same = [(ids_ext[edge - k : edge - k + length] == segment_ids[0]).astype(F32) for k in range(taps)]
    same = by_step(jnp.stack(same + [same[0]] * (8 - taps), axis=1))

    rate = 8.0 * jax.nn.softplus(decay_logit)
    params = wide(jnp.concatenate([conv_kernel, jnp.stack([conv_bias, decay_bias, input_bias])], axis=0))
    params = jnp.concatenate([params, wide(rate[None], 1)], axis=0)
    decay_w, input_w = block_diagonal(decay_gate, width), block_diagonal(input_gate, width)
    state_init = wide(state_init)

    projected = dot(normed, w_input)
    feed_shard, projected = after((jnp.concatenate([feed_gate, feed_up, feed_down], axis=1), projected))
    w_feed = weights(feed_shard)
    ends = projected[-edge * SEGS :, :width].astype(BF).reshape(edge, SEGS, width)
    left = lax.ppermute(ends[:, -1], "seq", to_next)
    left = jnp.where(at_start, wide(window_init[0]), left)
    prefix = jnp.concatenate([left[:, None], ends[:, :-1]], axis=1).reshape(edge * SEGS, -1)
    block_windows = ends[:, -1, :channels]

    gates, conv_out, decay_sig, gate_sig, retain, products, states, pre_a, pre_b, total = recur_forward(
        projected, same, prefix, params, decay_w, input_w
    )
    state_in = state_init
    for k in range(1, seqs):
        arriving = lax.ppermute(total[0:1] * state_in + total[1:2], "seq", to_next)
        state_in = jnp.where(seq == k, arriving, state_in)
    block_states = total[0:1] * state_in + total[1:2]
    carry = pre_a * state_in + pre_b

    normed_mid, s2, middle, hidden, gated = exchange(
        "norm", (states, products, gates, carry, w_recur, x_low, feed_gain[None]), own_width
    )
    normed_mid, cot = after((normed_mid, cot))
    feed_low, feed_grads, feed_part, mid_mean = feed_both(normed_mid, cot, w_feed)
    mid_mean = mid_mean[:, 0].reshape(-1, 128)

    half = feed_down.shape[1]
    down_grad = rows_dot(cot, feed_low).astype(BF)
    feed_grads, down_grad, mid_mean = after((feed_grads, down_grad, mid_mean))
    feed_all = rows_dot(normed_mid, feed_grads).astype(BF)
    feed_grads, feed_all, feed_part = after((feed_grads, feed_all, feed_part))
    feed_out = lax.psum_scatter(feed_part, "rep", scatter_dimension=1, tiled=True)
    feed_all = spread(feed_all)
    middle_low, middle_grad, feed_gain_own, feed_down_grad = exchange(
        "back",
        (feed_grads, w_feed, cot_own, middle, s2, mid_mean, feed_own, down_grad),
        own_width,
    )

    local, after_prod, branch_grad, enter_a, enter_b, back_total, branch_dot = recur_adjoint(
        middle_low, w_recur, projected, hidden, retain
    )
    output_all = rows_dot(middle_low, gated).astype(BF)
    local, output_all = after((local, output_all))
    entering = jnp.zeros_like(state_init)
    for k in range(1, seqs):
        arriving = lax.ppermute(back_total[0:1] * entering + back_total[1:2], "seq", to_last)
        entering = jnp.where(seq == seqs - 1 - k, arriving, entering)
    enter = enter_a * entering + enter_b
    decay_grad, input_grad_low, low_grad, low_dot, first, sums = recur_backward(
        local, after_prod, enter, hidden, carry, conv_out, decay_sig, gate_sig, retain, same, params, projected,
        decay_w, input_w,
    )
    owed = [first[0:8], first[8:24], first[24:48]]
    owed = [o.reshape(k + 1, SEGS, -1) for k, o in enumerate(owed)]
    ahead = prefix.reshape(edge, SEGS, -1).astype(F32)
    back_share = jnp.zeros_like(ahead)
    tap_extra = [jnp.zeros((width,), F32)]
    for k in range(1, taps):
        term = jnp.pad(owed[k - 1], ((edge - k, 0), (0, 0), (0, 0)))
        tap_extra.append(jnp.sum(term * ahead, axis=(0, 1)))
        back_share = back_share + params[k] * term
    from_right = lax.ppermute(back_share[:, 0], "seq", to_last)
    share = jnp.concatenate([back_share[:, 1:], from_right[:, None]], axis=1)
    low_grad = low_grad.reshape(length // SEGS, SEGS, -1)
    low_grad = jnp.concatenate([low_grad[:-edge], low_grad[-edge:] + share], axis=0).reshape(length, -1)
    share_dot = jnp.sum(share * ends.astype(F32), axis=2).reshape(-1)
    in_mean = low_dot[:, 0] + branch_dot[:, 0] + jnp.pad(share_dot, (length - share_dot.shape[0], 0))
    in_mean = in_mean.reshape(-1, 128)

    both_grads = jnp.concatenate([low_grad.astype(BF), branch_grad], axis=1)
    both_grads, in_mean, feed_all = after((both_grads, in_mean, feed_all))
    feed_gate_grad, feed_up_grad = feed_all[:, :half].astype(F32), feed_all[:, half:].astype(F32)
    conv_low = conv_out.astype(BF)
    decay_gate_grad = diagonal_rows(rows_dot(conv_low, decay_grad), heads, head_width)
    input_gate_grad = diagonal_rows(rows_dot(conv_low, input_grad_low), heads, head_width)
    sums = jnp.sum(sums.reshape(8, 8, -1), axis=1)
    conv_kernel_grad = sums[:taps] + jnp.stack(tap_extra)
    logit_grad = sums[7:, :channels] * 8.0 * jax.nn.sigmoid(decay_logit)
    vectors = jnp.concatenate([conv_kernel_grad, sums[4:7]], axis=0)[:, :channels]
    vectors = jnp.concatenate([vectors, logit_grad], axis=0)
    parts = (decay_gate_grad, input_gate_grad, vectors)
    small, counts = join_small(parts)
    recur_raw = rows_dot(normed, both_grads).astype(BF)
    recur_all = spread(recur_raw)
    both_grads, recur_raw, small, feed_out, feed_gate_grad, feed_up_grad = after(
        (both_grads, recur_raw, small, feed_out, feed_gate_grad, feed_up_grad)
    )
    input_grad, summed, gains, output_all = exchange(
        "last",
        (
            both_grads, w_recur, middle_grad, x_low, s1, in_mean, mixer_own,
            small, feed_gain_own, output_all,
        ),
        own_width,
    )
    input_grad, feed_out, recur_all = after((input_grad, feed_out, recur_all))
    recur_output_grad = output_all[:, :channels]
    recur_input_grad = recur_all[:, :channels].astype(F32)
    recur_gate_grad = recur_all[:, width : width + channels].astype(F32)
    input_grad = by_segment(input_grad)[None]
    block_output = by_segment((middle + feed_out.astype(F32)).astype(BF))[None]
    decay_gate_grad, input_gate_grad, vectors = split_small(summed, counts, parts)
    decay_gate_grad, input_gate_grad = (
        g[:, :head_width].reshape(decay_gate.shape) for g in (decay_gate_grad, input_gate_grad)
    )
    return (
        block_output, block_states[:, None, :channels], block_windows[None, None], input_grad,
        recur_input_grad, recur_gate_grad, recur_output_grad, feed_gate_grad, feed_up_grad, feed_down_grad,
        vectors[:taps], vectors[4], decay_gate_grad, input_gate_grad, vectors[5], vectors[6], vectors[7],
        gains[0], gains[1],
    )


def solution(mesh):
    tokens = P("row", "seq", "rep")
    matrix = P(("seq", "row"), "rep")
    in_specs = (
        tokens, tokens, P("row", "seq"), P("row", "seq"), P("row", "rep"), P("row", None, "rep"),
        matrix, matrix, matrix, matrix, matrix, matrix,
        P(None, "rep"), P("rep"), P("rep", None, None), P("rep", None, None), P("rep"), P("rep"), P("rep"), P(), P(),
    )
    out_specs = (
        tokens, tokens, P("row", "seq", None, "rep"), tokens,
        matrix, matrix, matrix, matrix, matrix, matrix,
        P(None, "rep"), P("rep"), P("rep", None, None), P("rep", None, None), P("rep"), P("rep"), P("rep"), P(), P(),
    )
    return jax.shard_map(shards, mesh=mesh, in_specs=in_specs, out_specs=out_specs, check_vma=False)
```
